512 devices in a mesh: tm: 64 (over z, x, core), pairs: 8 (over y).
Axes of the slice: x: 4, y: 8, z: 8, core: 2. Of those that a mesh axis runs over, the one named last changes fastest.
Arguments:
- records: bfloat16 [2048, 65536], P('pairs', 'tm'), may hold values from -400 to 400
- station_order: int32 [2048], replicated, may hold values from 0 to 2047, each once
- block_list: int32 [80, 2], P('pairs'), may hold values from -1 to 31, as said below
Outputs:
- correlations: bfloat16 [80, 384, 2, 4096], P('pairs', 'tm')
The draws below stay inside these ranges and needn't reach their ends.
Inputs may be any that keep to these rules, and one draw needn't show every extreme that they name: `station_order`: each station once. `block_list`: rows k * 10 to (k + 1) * 10 - 1 belong to owner k of the pairs axis; an owner's live blocks come first and its other rows hold -1 in both columns; some owner has all 10 rows live; in a live row the second group is the first plus 0 to 3, modulo 32.
All inputs are finite; a program needn't handle non-finite values.
Results may differ from the reference program's by a relative error of at most 0.0076.
Values may be sent and summed in bfloat16 or wider, within the bound.
No kernel may reach another device: no remote copies, remote signals or barrier semaphores. Data moves between devices by JAX's collectives and lax.ppermute only.
A program may use at most 64 MiB of HBM per device.

```python
import math
import jax
import jax.numpy as jnp
from jax import lax

RECEIVER_TOTAL = 2048
GSIZE = 64
GROUPS = 32
SUBWIN = 16
SAMPLES = 4096
TIME = 65536
BINS = 384
FIRST_BIN = 8
BAND = 64
HALF = 64
SLOTS = 10
N_PAIRS = 8


def draw_records(key, part):
    first, second, tertiary_item = jax.random.split(jax.random.fold_in(key, 11), 3)
    seismogram_pieces = TIME // 128
    base = jnp.clip(jax.random.normal(first, (RECEIVER_TOTAL, TIME), jnp.float32), -6.0, 6.0)
    gains = jnp.exp(jax.random.uniform(second, (RECEIVER_TOTAL, 1), jnp.float32, -1.2, 1.2))
    random_recordings = jnp.exp(jax.random.uniform(tertiary_item, (RECEIVER_TOTAL, seismogram_pieces), jnp.float32, -1.0, 1.0))
    averaged_amplitude_curve = jnp.repeat(random_recordings, 128, axis=1)
    return (base * gains * averaged_amplitude_curve).astype(jnp.bfloat16)


def draw_block_list(key, part):
    keys = jax.random.split(jax.random.fold_in(key, 23), 4)
    first = jax.random.randint(keys[0], (N_PAIRS, SLOTS), 0, GROUPS)
    offset = jax.random.randint(keys[1], (N_PAIRS, SLOTS), 0, 4)
    second = (first + offset) % GROUPS
    counts = jax.random.randint(keys[2], (N_PAIRS, 1), max(SLOTS // 8, 1), SLOTS // 2 + 1)
    largest_modulus = jax.random.randint(keys[3], (), 0, N_PAIRS)
    counts = jnp.where(jnp.arange(N_PAIRS)[:, None] == largest_modulus, SLOTS, counts)
    live = jnp.arange(SLOTS)[None, :] < counts
    first = jnp.where(live, first, -1)
    second = jnp.where(live, second, -1)
    return jnp.stack([first, second], axis=-1).reshape(N_PAIRS * SLOTS, 2).astype(jnp.int32)


def setup_inputs(seed: int = 0) -> dict:
    splits = jax.random.split(jax.random.key(seed), 4)
    records = draw_records(jax.random.fold_in(splits[3], 71), 0)
    station_order = jax.random.permutation(splits[1], RECEIVER_TOTAL).astype(jnp.int32)
    block_list = draw_block_list(jax.random.fold_in(splits[3], 71), 0)
    return {"records": records, "station_order": station_order, "block_list": block_list}


EPS = 1e-06

def dft_table(dtype):
    rows = jnp.arange(SAMPLES, dtype=jnp.int32)[:, None]
    cols = jnp.arange(BINS, dtype=jnp.int32)[None, :] + FIRST_BIN
    phase = (rows * cols % SAMPLES).astype(dtype) * (2.0 * math.pi / SAMPLES)
    return jnp.concatenate([jnp.cos(phase), -jnp.sin(phase)], axis=1).astype(jnp.bfloat16)

def window_sum(values, width):
    length = values.shape[1]
    out_len = length - width + 1
    total = jnp.zeros((values.shape[0], out_len), values.dtype)
    power = values
    size = 1
    offset = 0
    need = width
    while need > 0:
        if need % 2 == 1:
            total = total + power[:, offset:offset + out_len]
            offset = offset + size
        need = need // 2
        if need > 0:
            power = power[:, :-size] + power[:, size:]
            size = size * 2
    return total

def moving_norm(values, abs_padded, position):
    sums = window_sum(abs_padded, 2 * HALF + 1)
    upper = jnp.minimum(position + HALF, TIME - 1)
    lower = jnp.maximum(position - HALF, 0)
    counts = (upper - lower + 1).astype(abs_padded.dtype)
    return (values.astype(abs_padded.dtype) / (sums / counts + EPS)).astype(jnp.bfloat16)

def whiten(raw_rows):
    count = raw_rows.shape[0]
    parts = raw_rows.reshape(count, SUBWIN, 2, BINS // BAND, BAND)
    power = lax.optimization_barrier(jnp.mean(parts[:, :, 0] ** 2 + parts[:, :, 1] ** 2, axis=-1))
    level = jnp.sqrt(power + EPS)
    return (parts / level[:, :, None, :, None]).reshape(count, SUBWIN, 2, BINS).astype(jnp.bfloat16)

def reference(records, station_order, block_list):
    table = dft_table(jnp.float32)
    position = jnp.arange(TIME, dtype=jnp.int32)

    def per_group(block):
        magnitude = jnp.pad(jnp.abs(block.astype(jnp.float32)), ((0, 0), (HALF, HALF)))
        normed = moving_norm(block, magnitude, position)
        frames = normed.reshape(GSIZE * SUBWIN, SAMPLES)
        raw_rows = jnp.dot(frames, table, preferred_element_type=jnp.float32)
        return whiten(raw_rows.reshape(GSIZE, SUBWIN, 2 * BINS))
    fourier_coefficients = lax.map(per_group, records.reshape(RECEIVER_TOTAL // GSIZE, GSIZE, TIME))
    fourier_coefficients = jnp.transpose(fourier_coefficients.reshape(RECEIVER_TOTAL, SUBWIN, 2, BINS), (3, 1, 2, 0))
    group_members = station_order.reshape(GROUPS, GSIZE)

    def one_block(row):
        first = row[0]
        second = row[1]
        valid = (first >= 0).astype(jnp.float32)
        left = jnp.take(fourier_coefficients, group_members[jnp.maximum(first, 0)], axis=3).astype(jnp.float32)
        right = jnp.take(fourier_coefficients, group_members[jnp.maximum(second, 0)], axis=3).astype(jnp.float32)
        left_rows = left.reshape(BINS, SUBWIN * 2, GSIZE)
        right_rows = right.reshape(BINS, SUBWIN * 2, GSIZE)
        turned = jnp.stack([right[:, :, 1], -right[:, :, 0]], axis=2).reshape(BINS, SUBWIN * 2, GSIZE)
        cosine_component = jnp.einsum('fqi,fqj->fij', left_rows, right_rows)
        imag_part = jnp.einsum('fqi,fqj->fij', left_rows, turned)
        stacked = jnp.stack([cosine_component, imag_part], axis=1).reshape(BINS, 2, GSIZE * GSIZE)
        return (stacked * (valid / SUBWIN)).astype(jnp.bfloat16)
    return lax.map(one_block, block_list)
```

```python
import math

import jax
import jax.numpy as jnp
import ml_dtypes
import numpy as np
from jax import lax
from jax.experimental import pallas as pl
from jax.experimental.pallas import tpu as pltpu
from jax.sharding import PartitionSpec as P

RECEIVER_TOTAL = 2048
GSIZE = 64
GROUPS = 32
SUBWIN = 16
SAMPLES = 4096
TIME = 65536
BINS = 384
FIRST_BIN = 8
BAND = 64
HALF = 64
SLOTS = 10
EPS = 1e-06

N_TIME = 64
N_OWNER = 8
QUAD = 4
SLICE = TIME // N_TIME
ROWS = RECEIVER_TOTAL // N_OWNER
PART = ROWS // QUAD
LOCAL_BINS = BINS // N_TIME
LINES = LOCAL_BINS * 2 * SUBWIN
EDGE = 128

f32 = jnp.float32
bf16 = jnp.bfloat16
NT = (((1,), (1,)), ((), ()))


def quarter_table():
    bins = np.arange(BINS)[:, None] + FIRST_BIN
    phase = (bins * np.arange(SLICE)[None, :] % SAMPLES) * (2.0 * math.pi / SAMPLES)
    return np.concatenate([np.cos(phase), -np.sin(phase)]).astype(ml_dtypes.bfloat16)


def normalize_kernel(tm_ref, x_ref, left_ref, right_ref, out_ref):
    mag = jnp.concatenate(
        [jnp.abs(left_ref[...]), jnp.abs(x_ref[...]), jnp.abs(right_ref[...])], axis=1
    )
    step = 256
    span = step + 2 * EDGE
    k = lax.broadcasted_iota(jnp.int32, (span, step), 0)
    n = lax.broadcasted_iota(jnp.int32, (span, step), 1)
    near = jnp.abs(k - EDGE - n) <= HALF
    band = jnp.where(near, 1.0, 0.0).astype(bf16)
    for j in range(SLICE // step):
        sums = jnp.dot(
            mag[:, j * step : j * step + span], band, preferred_element_type=f32
        )
        position = (
            tm_ref[0] * SLICE + j * step + lax.broadcasted_iota(jnp.int32, (1, step), 1)
        )
        upper = jnp.minimum(position + HALF, TIME - 1)
        lower = jnp.maximum(position - HALF, 0)
        counts = (upper - lower + 1).astype(f32)
        values = x_ref[:, j * step : (j + 1) * step].astype(f32)
        out_ref[:, j * step : (j + 1) * step] = (values / (sums / counts + EPS)).astype(bf16)


def spectra_kernel(table_ref, y_ref, out_ref):
    p = lax.dot_general(table_ref[...], y_ref[...], NT, preferred_element_type=f32)
    re, im = p[:BINS], p[BINS:]
    f = lax.broadcasted_iota(jnp.int32, (BINS, 128), 0)
    lane = lax.broadcasted_iota(jnp.int32, (BINS, 128), 1)
    odd = (f & 1) == 1
    low = lane < PART
    u_re = jnp.where(odd, re[:, :128] - re[:, 128:], re[:, :128] + re[:, 128:])
    u_im = jnp.where(odd, im[:, :128] - im[:, 128:], im[:, :128] + im[:, 128:])
    sign = jnp.where((f & 3) < 2, 1.0, -1.0)
    v_re = sign * jnp.where(odd, u_im, u_re)
    v_im = sign * jnp.where(odd, -u_re, u_im)
    raw = jnp.where(low, u_re, v_im) + pltpu.roll(jnp.where(low, u_im, v_re), PART, 1)
    for m in range(BINS // BAND):
        block = raw[m * BAND : (m + 1) * BAND]
        power = jnp.sum(block * block, axis=0, keepdims=True)
        power = jnp.broadcast_to(power, (8, 128))
        power = power + pltpu.roll(power, PART, 1)
        level = jnp.sqrt(power / BAND + EPS)
        out_ref[m * BAND : (m + 1) * BAND] = (block / level[:1]).astype(bf16)


def arrange_kernel(x_ref, out_ref):
    o = lax.broadcasted_iota(jnp.int32, (BINS, BINS), 0)
    i = lax.broadcasted_iota(jnp.int32, (BINS, BINS), 1)
    per = LOCAL_BINS * SUBWIN
    source = (o % SUBWIN) * (QUAD * LOCAL_BINS) + (o // per) * LOCAL_BINS + (o % per) // SUBWIN
    pick = jnp.where(i == source, 1.0, 0.0).astype(bf16)
    z = jnp.dot(pick, x_ref[...], preferred_element_type=f32)
    low = lax.broadcasted_iota(jnp.int32, (per, 128), 1) < PART
    for h in range(QUAD // 2):
        first = z[2 * h * per : (2 * h + 1) * per]
        second = z[(2 * h + 1) * per : (2 * h + 2) * per]
        parts = (
            jnp.where(low, first, pltpu.roll(second, PART, 1)).astype(bf16),
            jnp.where(low, pltpu.roll(first, PART, 1), second).astype(bf16),
        )
        for b in range(LOCAL_BINS):
            for c in range(2):
                rows = parts[c][b * SUBWIN : (b + 1) * SUBWIN]
                for n in range(N_OWNER):
                    out_ref[
                        n,
                        (2 * b + c) * SUBWIN : (2 * b + c + 1) * SUBWIN,
                        h * 128 : (h + 1) * 128,
                    ] = rows


PER_STEP = 2


def correlate_kernel(list_ref, order_ref, s_ref, out_ref, all_ref):
    step = pl.program_id(0)

    @pl.when(step == 0)
    def _():
        for n in range(N_OWNER):
            all_ref[:, n * ROWS : (n + 1) * ROWS] = s_ref[n]

    rho = lax.broadcasted_iota(jnp.int32, (GSIZE, GSIZE), 0)
    col = lax.broadcasted_iota(jnp.int32, (GSIZE, GSIZE), 1)
    even = col == (rho // 2) * 2
    uneven = col == (rho // 2) * 2 + 1
    same = col == rho
    station = lax.broadcasted_iota(jnp.int32, (3 * GSIZE, RECEIVER_TOTAL), 1)
    k = lax.broadcasted_iota(jnp.int32, (LINES, LINES), 0)
    n = lax.broadcasted_iota(jnp.int32, (LINES, LINES), 1)
    turn = jnp.where(k == (n ^ SUBWIN), jnp.where((n & SUBWIN) == 0, -1.0, 1.0), 0.0).astype(bf16)
    imag_row = (lax.broadcasted_iota(jnp.int32, (2 * GSIZE, LINES), 0) & 1) == 1
    bin_of = lax.broadcasted_iota(jnp.int32, (GSIZE, 128), 1) // (2 * SUBWIN)

    for b in range(PER_STEP):
        slot = step * PER_STEP + b
        first, second = list_ref[slot, 0], list_ref[slot, 1]
        scale = jnp.where(first >= 0, 1.0 / SUBWIN, 0.0)
        members_a = order_ref[pl.ds(jnp.maximum(first, 0), 1), :]
        members_b = order_ref[pl.ds(jnp.maximum(second, 0), 1), :]
        wanted = jnp.concatenate(
            [
                jnp.sum(jnp.where(even, members_a, 0), axis=1, keepdims=True),
                jnp.sum(jnp.where(uneven, members_a, 0), axis=1, keepdims=True),
                jnp.sum(jnp.where(same, members_b, 0), axis=1, keepdims=True),
            ],
            axis=0,
        )
        pick = jnp.where(station == wanted, 1.0, 0.0).astype(bf16)
        g = lax.dot_general(pick, all_ref[...], NT, preferred_element_type=f32).astype(bf16)
        a = g[: 2 * GSIZE]
        turned = jnp.dot(a, turn, preferred_element_type=f32)
        a = jnp.where(imag_row, turned, a.astype(f32)).astype(bf16)
        right = g[2 * GSIZE :]
        pad = jnp.zeros((GSIZE, 64), bf16)
        zero = jnp.zeros((GSIZE, 128), bf16)
        sides = (
            (a[:GSIZE, :128], a[GSIZE:, :128], right[:, :128], 0, 4),
            (
                jnp.concatenate([a[:GSIZE, 128:], pad], axis=1),
                jnp.concatenate([a[GSIZE:, 128:], pad], axis=1),
                jnp.concatenate([right[:, 128:], pad], axis=1),
                4,
                2,
            ),
        )
        for a_even, a_odd, r, bin0, count in sides:
            lhs = jnp.concatenate([a_even, a_odd], axis=1)
            blocks = []
            for e in range(count):
                kept = jnp.where(bin_of == e, r.astype(f32), 0.0).astype(bf16)
                blocks.append(jnp.concatenate([kept, zero], axis=1))
                blocks.append(jnp.concatenate([zero, kept], axis=1))
            rhs = jnp.concatenate(blocks, axis=0)
            c = lax.dot_general(lhs, rhs, NT, preferred_element_type=f32) * scale
            for e in range(count):
                out_ref[b, bin0 + e] = c[:, e * 128 : (e + 1) * 128].astype(bf16)


def vmem():
    return pl.BlockSpec(memory_space=pltpu.VMEM)


def smem():
    return pl.BlockSpec(memory_space=pltpu.SMEM)


PARAMS = pltpu.CompilerParams(vmem_limit_bytes=40 * 1024 * 1024)


def local(records, station_order, block_list):
    me = lax.axis_index("tm").astype(jnp.int32).reshape(1)
    left = lax.ppermute(records[:, SLICE - EDGE :], "tm", [(i, i + 1) for i in range(N_TIME - 1)])
    right = lax.ppermute(records[:, :EDGE], "tm", [(i + 1, i) for i in range(N_TIME - 1)])
    normalized = pl.pallas_call(
        normalize_kernel,
        out_shape=jax.ShapeDtypeStruct((ROWS, SLICE), bf16),
        in_specs=[smem(), vmem(), vmem(), vmem()],
        out_specs=vmem(),
        compiler_params=PARAMS,
        name="normalize",
    )(me, records, left, right)
    quads = [[QUAD * g + i for i in range(QUAD)] for g in range(N_TIME // QUAD)]
    windows = lax.all_to_all(
        normalized.reshape(QUAD, PART, SLICE), "tm", 0, 0, axis_index_groups=quads, tiled=True
    ).reshape(ROWS, SLICE)
    spectra = pl.pallas_call(
        spectra_kernel,
        out_shape=jax.ShapeDtypeStruct((BINS, 2 * PART), bf16),
        in_specs=[vmem(), vmem()],
        out_specs=vmem(),
        compiler_params=PARAMS,
        name="spectra",
    )(jnp.asarray(quarter_table()), windows)
    by_bin = lax.all_to_all(
        spectra.reshape(N_TIME, LOCAL_BINS // 2, 2, 2 * PART), "tm", 0, 0, tiled=True
    ).reshape(BINS, 2 * PART)
    copies = pl.pallas_call(
        arrange_kernel,
        out_shape=jax.ShapeDtypeStruct((N_OWNER, LINES, ROWS), bf16),
        in_specs=[vmem()],
        out_specs=vmem(),
        compiler_params=PARAMS,
        name="arrange",
    )(by_bin)
    stations = lax.all_to_all(copies, "pairs", 0, 0, tiled=True)
    out = pl.pallas_call(
        correlate_kernel,
        out_shape=jax.ShapeDtypeStruct((SLOTS, LOCAL_BINS, GSIZE, 128), bf16),
        grid=(SLOTS // PER_STEP,),
        in_specs=[smem(), vmem(), vmem()],
        out_specs=pl.BlockSpec((PER_STEP, LOCAL_BINS, GSIZE, 128), lambda i: (i, 0, 0, 0)),
        scratch_shapes=[pltpu.VMEM((LINES, RECEIVER_TOTAL), bf16)],
        compiler_params=PARAMS,
        name="correlate",
    )(block_list, station_order.reshape(GROUPS, GSIZE), stations)
    out = out.reshape(SLOTS, LOCAL_BINS, GSIZE // 2, 2, 128)
    return jnp.transpose(out, (0, 1, 3, 2, 4)).reshape(SLOTS, LOCAL_BINS, 2, GSIZE * GSIZE)


def solution(mesh):
    placed = (P("pairs", "tm"), P(), P("pairs", None))
    return jax.shard_map(
        local, mesh=mesh, in_specs=placed, out_specs=P("pairs", "tm", None, None), check_vma=False
    )
```

```python
import math

import jax
import jax.numpy as jnp
import ml_dtypes
import numpy as np
from jax import lax
from jax.experimental import pallas as pl
from jax.experimental.pallas import tpu as pltpu
from jax.sharding import PartitionSpec as P

RECEIVER_TOTAL = 2048
GSIZE = 64
GROUPS = 32
SUBWIN = 16
SAMPLES = 4096
TIME = 65536
BINS = 384
FIRST_BIN = 8
BAND = 64
HALF = 64
SLOTS = 10
EPS = 1e-06

N_TIME = 64
N_OWNER = 8
QUAD = 4
SLICE = TIME // N_TIME
ROWS = RECEIVER_TOTAL // N_OWNER
PART = ROWS // QUAD
LOCAL_BINS = BINS // N_TIME
LINES = LOCAL_BINS * 2 * SUBWIN
EDGE = 128

f32 = jnp.float32
bf16 = jnp.bfloat16
NT = (((1,), (1,)), ((), ()))


def quarter_table():
    bins = np.arange(BINS)[:, None] + FIRST_BIN
    phase = (bins * np.arange(SLICE)[None, :] % SAMPLES) * (2.0 * math.pi / SAMPLES)
    return np.concatenate([np.cos(phase), -np.sin(phase)]).astype(ml_dtypes.bfloat16)


def band_matrix(span, step):
    k = lax.broadcasted_iota(jnp.int32, (span, step), 0)
    n = lax.broadcasted_iota(jnp.int32, (span, step), 1)
    return jnp.where(jnp.abs(k - EDGE - n) <= HALF, 1.0, 0.0).astype(bf16)


def normalize_inner_kernel(x_ref, out_ref):
    step = 256
    band = band_matrix(step + 2 * EDGE, step)
    for j in range((SLICE - 2 * EDGE) // step):
        mag = jnp.abs(x_ref[:, j * step : (j + 1) * step + 2 * EDGE])
        sums = jnp.dot(mag, band, preferred_element_type=f32)
        values = x_ref[:, j * step + EDGE : (j + 1) * step + EDGE].astype(f32)
        level = sums / (2 * HALF + 1)
        out_ref[:, j * step : (j + 1) * step] = (values / (level + EPS)).astype(bf16)


def normalize_edges_kernel(tm_ref, x_ref, left_ref, right_ref, inner_ref, out_ref):
    band = band_matrix(3 * EDGE, EDGE)
    me = tm_ref[0]
    out_ref[:, EDGE : SLICE - EDGE] = inner_ref[...]
    left = jnp.abs(left_ref[...].astype(f32)) * jnp.where(me > 0, 1.0, 0.0)
    right = jnp.abs(right_ref[...].astype(f32)) * jnp.where(me < N_TIME - 1, 1.0, 0.0)
    for start, mag in (
        (0, jnp.concatenate([left.astype(bf16), jnp.abs(x_ref[:, : 2 * EDGE])], axis=1)),
        (
            SLICE - EDGE,
            jnp.concatenate([jnp.abs(x_ref[:, SLICE - 2 * EDGE :]), right.astype(bf16)], axis=1),
        ),
    ):
        sums = jnp.dot(mag, band, preferred_element_type=f32)
        position = me * SLICE + start + lax.broadcasted_iota(jnp.int32, (1, EDGE), 1)
        upper = jnp.minimum(position + HALF, TIME - 1)
        lower = jnp.maximum(position - HALF, 0)
        counts = (upper - lower + 1).astype(f32)
        values = x_ref[:, start : start + EDGE].astype(f32)
        out_ref[:, start : start + EDGE] = (values / (sums / counts + EPS)).astype(bf16)


def spectra_kernel(table_ref, y_ref, out_ref):
    p = lax.dot_general(table_ref[...], y_ref[...], NT, preferred_element_type=f32)
    re, im = p[:BINS], p[BINS:]
    f = lax.broadcasted_iota(jnp.int32, (BINS, 128), 0)
    lane = lax.broadcasted_iota(jnp.int32, (BINS, 128), 1)
    odd = (f & 1) == 1
    low = lane < PART
    u_re = jnp.where(odd, re[:, :128] - re[:, 128:], re[:, :128] + re[:, 128:])
    u_im = jnp.where(odd, im[:, :128] - im[:, 128:], im[:, :128] + im[:, 128:])
    sign = jnp.where((f & 3) < 2, 1.0, -1.0)
    v_re = sign * jnp.where(odd, u_im, u_re)
    v_im = sign * jnp.where(odd, -u_re, u_im)
    raw = jnp.where(low, u_re, v_im) + pltpu.roll(jnp.where(low, u_im, v_re), PART, 1)
    for m in range(BINS // BAND):
        block = raw[m * BAND : (m + 1) * BAND]
        power = jnp.sum(block * block, axis=0, keepdims=True)
        power = jnp.broadcast_to(power, (8, 128))
        power = power + pltpu.roll(power, PART, 1)
        level = jnp.sqrt(power / BAND + EPS)
        out_ref[m * BAND : (m + 1) * BAND] = (block / level[:1]).astype(bf16)


def arrange_kernel(x_ref, out_ref):
    o = lax.broadcasted_iota(jnp.int32, (BINS, BINS), 0)
    i = lax.broadcasted_iota(jnp.int32, (BINS, BINS), 1)
    per = LOCAL_BINS * SUBWIN
    source = (o % SUBWIN) * (QUAD * LOCAL_BINS) + (o // per) * LOCAL_BINS + (o % per) // SUBWIN
    pick = jnp.where(i == source, 1.0, 0.0).astype(bf16)
    z = jnp.dot(pick, x_ref[...], preferred_element_type=f32)
    low = lax.broadcasted_iota(jnp.int32, (per, 128), 1) < PART
    for h in range(QUAD // 2):
        first = z[2 * h * per : (2 * h + 1) * per]
        second = z[(2 * h + 1) * per : (2 * h + 2) * per]
        real = jnp.where(low, first, pltpu.roll(second, PART, 1))
        imag = jnp.where(low, pltpu.roll(first, PART, 1), second)
        lines = []
        for e in range(LOCAL_BINS):
            lines += [part[e * SUBWIN : (e + 1) * SUBWIN] for part in (real, imag)]
        stations = jnp.concatenate(lines, axis=0).T.astype(bf16)
        out_ref[h * 128 : (h + 1) * 128] = stations[:, :128]
        out_ref[ROWS:, h * 64 : (h + 1) * 64] = stations[:, 128:]


def correlate_kernel(list_ref, order_ref, s_ref, out_ref, main_ref, tail_ref, gm_ref, gt_ref):
    for n in range(N_OWNER):
        block = s_ref[n * BINS : (n + 1) * BINS].astype(f32)
        main_ref[n * ROWS : (n + 1) * ROWS] = block[:ROWS]
        tail_ref[n * ROWS : n * ROWS + 128] = block[ROWS:]
        tail_ref[n * ROWS + 128 : (n + 1) * ROWS] = pltpu.roll(block[ROWS:], 64, 1)

    rights = SLOTS * 2 * GSIZE
    for b in range(SLOTS):
        base = jnp.maximum(list_ref[b, 0], 0) * GSIZE
        base_right = jnp.maximum(list_ref[b, 1], 0) * GSIZE
        for i in range(0, GSIZE, 8):
            ids = [order_ref[base + i + u] for u in range(8)]
            ids_right = [order_ref[base_right + i + u] for u in range(8)]
            for source, g_ref in ((main_ref, gm_ref), (tail_ref, gt_ref)):
                rows = [source[pl.ds(station, 1), :] for station in ids]
                for parity in range(2):
                    at = b * 2 * GSIZE + parity * GSIZE + i
                    twice = [rows[u - u % 2 + parity] for u in range(8)]
                    g_ref[at : at + 8, :] = jnp.concatenate(twice, axis=0)
                at = rights + b * GSIZE + i
                g_ref[at : at + 8, :] = jnp.concatenate(
                    [source[pl.ds(station, 1), :] for station in ids_right], axis=0
                )

    k = lax.broadcasted_iota(jnp.int32, (128, 128), 0)
    n = lax.broadcasted_iota(jnp.int32, (128, 128), 1)
    turn = jnp.where(k == (n ^ SUBWIN), jnp.where((n & SUBWIN) == 0, -1.0, 1.0), 0.0).astype(bf16)
    imag_row = (lax.broadcasted_iota(jnp.int32, (rights, 128), 0) & 1) == 1
    lefts = []
    for g_ref in (gm_ref, gt_ref):
        plain = g_ref[:rights]
        turned = jnp.dot(plain.astype(bf16), turn, preferred_element_type=f32)
        lefts.append(jnp.where(imag_row, turned, plain).astype(bf16))
    bin_of = lax.broadcasted_iota(jnp.int32, (GSIZE, 128), 1) // (2 * SUBWIN)
    zero = jnp.zeros((GSIZE, 128), bf16)
    for b in range(SLOTS):
        scale = jnp.where(list_ref[b, 0] >= 0, 1.0 / SUBWIN, 0.0)
        for a, g_ref, bin0, count in ((lefts[0], gm_ref, 0, 4), (lefts[1], gt_ref, 4, 2)):
            at = b * 2 * GSIZE
            lhs = jnp.concatenate(
                [a[at : at + GSIZE], a[at + GSIZE : at + 2 * GSIZE]], axis=1
            )
            r = g_ref[rights + b * GSIZE : rights + (b + 1) * GSIZE]
            blocks = []
            for e in range(count):
                kept = jnp.where(bin_of == e, r, 0.0).astype(bf16)
                blocks.append(jnp.concatenate([kept, zero], axis=1))
                blocks.append(jnp.concatenate([zero, kept], axis=1))
            rhs = jnp.concatenate(blocks, axis=0)
            c = lax.dot_general(lhs, rhs, NT, preferred_element_type=f32) * scale
            for e in range(count):
                out_ref[b, bin0 + e] = c[:, e * 128 : (e + 1) * 128].astype(bf16)


def vmem():
    return pl.BlockSpec(memory_space=pltpu.VMEM)


def smem():
    return pl.BlockSpec(memory_space=pltpu.SMEM)


PARAMS = pltpu.CompilerParams(vmem_limit_bytes=40 * 1024 * 1024)


def correlate(block_list, station_order, stations):
    return pl.pallas_call(
        correlate_kernel,
        out_shape=jax.ShapeDtypeStruct((SLOTS, LOCAL_BINS, GSIZE, 128), bf16),
        in_specs=[smem(), smem(), vmem()],
        out_specs=vmem(),
        scratch_shapes=[
            pltpu.VMEM((RECEIVER_TOTAL, 128), f32),
            pltpu.VMEM((RECEIVER_TOTAL, 128), f32),
            pltpu.VMEM((SLOTS * 3 * GSIZE, 128), f32),
            pltpu.VMEM((SLOTS * 3 * GSIZE, 128), f32),
        ],
        compiler_params=PARAMS,
        name="correlate",
    )(block_list, station_order, stations)


def local(records, station_order, block_list):
    me = lax.axis_index("tm").astype(jnp.int32).reshape(1)
    up = [(i, (i + 1) % N_TIME) for i in range(N_TIME)]
    left = lax.ppermute(records[:, SLICE - EDGE :], "tm", up)
    right = lax.ppermute(records[:, :EDGE], "tm", [(j, i) for i, j in up])
    inner = pl.pallas_call(
        normalize_inner_kernel,
        out_shape=jax.ShapeDtypeStruct((ROWS, SLICE - 2 * EDGE), bf16),
        in_specs=[vmem()],
        out_specs=vmem(),
        compiler_params=PARAMS,
        cost_estimate=pl.CostEstimate(
            flops=2 * ROWS * (SLICE - 2 * EDGE) * 512,
            bytes_accessed=4 * ROWS * SLICE,
            transcendentals=0,
        ),
        name="normalize_inner",
    )(records)
    normalized = pl.pallas_call(
        normalize_edges_kernel,
        out_shape=jax.ShapeDtypeStruct((ROWS, SLICE), bf16),
        in_specs=[smem(), vmem(), vmem(), vmem(), vmem()],
        out_specs=vmem(),
        compiler_params=PARAMS,
        name="normalize_edges",
    )(me, records, left, right, inner)
    quads = [[QUAD * g + i for i in range(QUAD)] for g in range(N_TIME // QUAD)]
    windows = lax.all_to_all(
        normalized.reshape(QUAD, PART, SLICE), "tm", 0, 0, axis_index_groups=quads, tiled=True
    ).reshape(ROWS, SLICE)
    spectra = pl.pallas_call(
        spectra_kernel,
        out_shape=jax.ShapeDtypeStruct((BINS, 2 * PART), bf16),
        in_specs=[vmem(), vmem()],
        out_specs=vmem(),
        compiler_params=PARAMS,
        name="spectra",
    )(jnp.asarray(quarter_table()), windows)
    by_bin = lax.all_to_all(
        spectra.reshape(N_TIME, LOCAL_BINS // 2, 2, 2 * PART), "tm", 0, 0, tiled=True
    ).reshape(BINS, 2 * PART)
    mine = pl.pallas_call(
        arrange_kernel,
        out_shape=jax.ShapeDtypeStruct((BINS, 128), bf16),
        in_specs=[vmem()],
        out_specs=vmem(),
        compiler_params=PARAMS,
        name="arrange",
    )(by_bin)
    stations = lax.all_gather(mine, "pairs", axis=0, tiled=True)
    out = correlate(block_list, station_order, stations)
    out = out.reshape(SLOTS, LOCAL_BINS, GSIZE // 2, 2, 128)
    return jnp.transpose(out, (0, 1, 3, 2, 4)).reshape(SLOTS, LOCAL_BINS, 2, GSIZE * GSIZE)


def solution(mesh):
    placed = (P("pairs", "tm"), P(), P("pairs", None))
    return jax.shard_map(
        local, mesh=mesh, in_specs=placed, out_specs=P("pairs", "tm", None, None), check_vma=False
    )
```

```python
import math

import jax
import jax.numpy as jnp
import ml_dtypes
import numpy as np
from jax import lax
from jax.experimental import pallas as pl
from jax.experimental.pallas import tpu as pltpu
from jax.sharding import PartitionSpec as P

RECEIVER_TOTAL = 2048
GSIZE = 64
GROUPS = 32
SUBWIN = 16
SAMPLES = 4096
TIME = 65536
BINS = 384
FIRST_BIN = 8
BAND = 64
HALF = 64
SLOTS = 10
EPS = 1e-06

N_TIME = 64
N_OWNER = 8
QUAD = 4
SLICE = TIME // N_TIME
ROWS = RECEIVER_TOTAL // N_OWNER
PART = ROWS // QUAD
LOCAL_BINS = BINS // N_TIME
LINES = LOCAL_BINS * 2 * SUBWIN
EDGE = 128

f32 = jnp.float32
bf16 = jnp.bfloat16
NT = (((1,), (1,)), ((), ()))


def quarter_table():
    bins = np.arange(BINS)[:, None] + FIRST_BIN
    phase = (bins * np.arange(SLICE)[None, :] % SAMPLES) * (2.0 * math.pi / SAMPLES)
    return np.concatenate([np.cos(phase), -np.sin(phase)]).astype(ml_dtypes.bfloat16)


def band_matrix(span, step):
    k = lax.broadcasted_iota(jnp.int32, (span, step), 0)
    n = lax.broadcasted_iota(jnp.int32, (span, step), 1)
    return jnp.where(jnp.abs(k - EDGE - n) <= HALF, 1.0, 0.0).astype(bf16)


def normalize_inner_kernel(x_ref, up_ref, down_ref, ends_ref, out_ref):
    up_ref[...] = x_ref[:, SLICE - EDGE :]
    down_ref[...] = x_ref[:, :EDGE]
    ends_ref[:, : 2 * EDGE] = x_ref[:, : 2 * EDGE]
    ends_ref[:, 2 * EDGE :] = x_ref[:, SLICE - 2 * EDGE :]
    step = 256
    band = band_matrix(step + 2 * EDGE, step)
    for j in range((SLICE - 2 * EDGE) // step):
        mag = jnp.abs(x_ref[:, j * step : (j + 1) * step + 2 * EDGE])
        sums = jnp.dot(mag, band, preferred_element_type=f32)
        values = x_ref[:, j * step + EDGE : (j + 1) * step + EDGE].astype(f32)
        level = sums / (2 * HALF + 1)
        out_ref[:, j * step : (j + 1) * step] = (values / (level + EPS)).astype(bf16)


def normalize_edges_kernel(tm_ref, ends_ref, left_ref, right_ref, inner_ref, out_ref):
    band = band_matrix(3 * EDGE, EDGE)
    me = tm_ref[0]
    out_ref[:, EDGE : SLICE - EDGE] = inner_ref[...]
    left = jnp.abs(left_ref[...].astype(f32)) * jnp.where(me > 0, 1.0, 0.0)
    right = jnp.abs(right_ref[...].astype(f32)) * jnp.where(me < N_TIME - 1, 1.0, 0.0)
    head, tail = ends_ref[:, : 2 * EDGE], ends_ref[:, 2 * EDGE :]
    for start, values, mag in (
        (0, head[:, :EDGE], jnp.concatenate([left.astype(bf16), jnp.abs(head)], axis=1)),
        (SLICE - EDGE, tail[:, EDGE:], jnp.concatenate([jnp.abs(tail), right.astype(bf16)], axis=1)),
    ):
        sums = jnp.dot(mag, band, preferred_element_type=f32)
        position = me * SLICE + start + lax.broadcasted_iota(jnp.int32, (1, EDGE), 1)
        upper = jnp.minimum(position + HALF, TIME - 1)
        lower = jnp.maximum(position - HALF, 0)
        counts = (upper - lower + 1).astype(f32)
        out_ref[:, start : start + EDGE] = (
            values.astype(f32) / (sums / counts + EPS)
        ).astype(bf16)


def spectra_kernel(table_ref, y_ref, out_ref):
    p = lax.dot_general(table_ref[...], y_ref[...], NT, preferred_element_type=f32)
    re, im = p[:BINS], p[BINS:]
    f = lax.broadcasted_iota(jnp.int32, (BINS, 128), 0)
    lane = lax.broadcasted_iota(jnp.int32, (BINS, 128), 1)
    odd = (f & 1) == 1
    low = lane < PART
    u_re = jnp.where(odd, re[:, :128] - re[:, 128:], re[:, :128] + re[:, 128:])
    u_im = jnp.where(odd, im[:, :128] - im[:, 128:], im[:, :128] + im[:, 128:])
    sign = jnp.where((f & 3) < 2, 1.0, -1.0)
    v_re = sign * jnp.where(odd, u_im, u_re)
    v_im = sign * jnp.where(odd, -u_re, u_im)
    raw = jnp.where(low, u_re, v_im) + pltpu.roll(jnp.where(low, u_im, v_re), PART, 1)
    for m in range(BINS // BAND):
        block = raw[m * BAND : (m + 1) * BAND]
        power = jnp.sum(block * block, axis=0, keepdims=True)
        power = jnp.broadcast_to(power, (8, 128))
        power = power + pltpu.roll(power, PART, 1)
        level = jnp.sqrt(power / BAND + EPS)
        out_ref[m * BAND : (m + 1) * BAND] = (block / level[:1]).astype(bf16)


def arrange_kernel(x_ref, out_ref):
    o = lax.broadcasted_iota(jnp.int32, (BINS, BINS), 0)
    i = lax.broadcasted_iota(jnp.int32, (BINS, BINS), 1)
    per = LOCAL_BINS * SUBWIN
    source = (o % SUBWIN) * (QUAD * LOCAL_BINS) + (o // per) * LOCAL_BINS + (o % per) // SUBWIN
    pick = jnp.where(i == source, 1.0, 0.0).astype(bf16)
    z = jnp.dot(pick, x_ref[...], preferred_element_type=f32)
    low = lax.broadcasted_iota(jnp.int32, (per, 128), 1) < PART
    for h in range(QUAD // 2):
        first = z[2 * h * per : (2 * h + 1) * per]
        second = z[(2 * h + 1) * per : (2 * h + 2) * per]
        real = jnp.where(low, first, pltpu.roll(second, PART, 1))
        imag = jnp.where(low, pltpu.roll(first, PART, 1), second)
        lines = []
        for e in range(LOCAL_BINS):
            lines += [part[e * SUBWIN : (e + 1) * SUBWIN] for part in (real, imag)]
        stations = jnp.concatenate(lines, axis=0).T.astype(bf16)
        out_ref[h * 128 : (h + 1) * 128] = stations[:, :128]
        out_ref[ROWS:, h * 64 : (h + 1) * 64] = stations[:, 128:]


def correlate_kernel(
    list_ref, order_ref, s_ref, out_hbm, main_ref, tail_ref, gm_ref, gt_ref, out_ref, sems
):
    for n in range(N_OWNER):
        block = s_ref[n * BINS : (n + 1) * BINS].astype(f32)
        main_ref[n * ROWS : (n + 1) * ROWS] = block[:ROWS]
        tail_ref[n * ROWS : n * ROWS + 128] = block[ROWS:]
        tail_ref[n * ROWS + 128 : (n + 1) * ROWS] = pltpu.roll(block[ROWS:], 64, 1)

    rights = SLOTS * 2 * GSIZE
    for b in range(SLOTS):
        base = jnp.maximum(list_ref[0, b], 0) * GSIZE
        base_right = jnp.maximum(list_ref[1, b], 0) * GSIZE
        for i in range(0, GSIZE, 8):
            ids = [order_ref[base + i + u] for u in range(8)]
            ids_right = [order_ref[base_right + i + u] for u in range(8)]
            for source, g_ref in ((main_ref, gm_ref), (tail_ref, gt_ref)):
                rows = [source[pl.ds(station, 1), :] for station in ids]
                for parity in range(2):
                    at = b * 2 * GSIZE + parity * GSIZE + i
                    twice = [rows[u - u % 2 + parity] for u in range(8)]
                    g_ref[at : at + 8, :] = jnp.concatenate(twice, axis=0)
                at = rights + b * GSIZE + i
                g_ref[at : at + 8, :] = jnp.concatenate(
                    [source[pl.ds(station, 1), :] for station in ids_right], axis=0
                )

    k = lax.broadcasted_iota(jnp.int32, (128, 128), 0)
    n = lax.broadcasted_iota(jnp.int32, (128, 128), 1)
    turn = jnp.where(k == (n ^ SUBWIN), jnp.where((n & SUBWIN) == 0, -1.0, 1.0), 0.0).astype(bf16)
    imag_row = (lax.broadcasted_iota(jnp.int32, (rights, 128), 0) & 1) == 1
    lefts = []
    for g_ref in (gm_ref, gt_ref):
        plain = g_ref[:rights]
        turned = jnp.dot(plain.astype(bf16), turn, preferred_element_type=f32)
        lefts.append(jnp.where(imag_row, turned, plain).astype(bf16))
    bin_of = lax.broadcasted_iota(jnp.int32, (GSIZE, 128), 1) // (2 * SUBWIN)
    zero = jnp.zeros((GSIZE, 128), bf16)
    copies = []
    for b in range(SLOTS):
        scale = jnp.where(list_ref[0, b] >= 0, 1.0 / SUBWIN, 0.0)
        for a, g_ref, bin0, count in ((lefts[0], gm_ref, 0, 4), (lefts[1], gt_ref, 4, 2)):
            at = b * 2 * GSIZE
            lhs = jnp.concatenate(
                [a[at : at + GSIZE], a[at + GSIZE : at + 2 * GSIZE]], axis=1
            )
            r = g_ref[rights + b * GSIZE : rights + (b + 1) * GSIZE]
            blocks = []
            for e in range(count):
                kept = jnp.where(bin_of == e, r, 0.0).astype(bf16)
                blocks.append(jnp.concatenate([kept, zero], axis=1))
                blocks.append(jnp.concatenate([zero, kept], axis=1))
            rhs = jnp.concatenate(blocks, axis=0)
            c = lax.dot_general(lhs, rhs, NT, preferred_element_type=f32) * scale
            for e in range(count):
                out_ref[b, bin0 + e] = c[:, e * 128 : (e + 1) * 128].astype(bf16)
        copies.append(pltpu.make_async_copy(out_ref.at[b], out_hbm.at[b], sems.at[b]))
        copies[-1].start()
    for copy in copies:
        copy.wait()


def vmem():
    return pl.BlockSpec(memory_space=pltpu.VMEM)


def smem():
    return pl.BlockSpec(memory_space=pltpu.SMEM)


PARAMS = pltpu.CompilerParams(vmem_limit_bytes=40 * 1024 * 1024)


def correlate(block_list, station_order, stations):
    return pl.pallas_call(
        correlate_kernel,
        out_shape=jax.ShapeDtypeStruct((SLOTS, LOCAL_BINS, GSIZE, 128), bf16),
        in_specs=[smem(), smem(), vmem()],
        out_specs=pl.BlockSpec(memory_space=pltpu.HBM),
        scratch_shapes=[
            pltpu.VMEM((RECEIVER_TOTAL, 128), f32),
            pltpu.VMEM((RECEIVER_TOTAL, 128), f32),
            pltpu.VMEM((SLOTS * 3 * GSIZE, 128), f32),
            pltpu.VMEM((SLOTS * 3 * GSIZE, 128), f32),
            pltpu.VMEM((SLOTS, LOCAL_BINS, GSIZE, 128), bf16),
            pltpu.SemaphoreType.DMA((SLOTS,)),
        ],
        compiler_params=PARAMS,
        name="correlate",
    )(block_list.T, station_order, stations)


def local(records, station_order, block_list):
    me = lax.axis_index("tm").astype(jnp.int32).reshape(1)
    up = [(i, (i + 1) % N_TIME) for i in range(N_TIME)]
    last, first, ends, inner = pl.pallas_call(
        normalize_inner_kernel,
        out_shape=[
            jax.ShapeDtypeStruct((ROWS, EDGE), bf16),
            jax.ShapeDtypeStruct((ROWS, EDGE), bf16),
            jax.ShapeDtypeStruct((ROWS, 4 * EDGE), bf16),
            jax.ShapeDtypeStruct((ROWS, SLICE - 2 * EDGE), bf16),
        ],
        in_specs=[vmem()],
        out_specs=[vmem()] * 4,
        compiler_params=PARAMS,
        name="normalize_inner",
    )(records)
    left = lax.ppermute(last, "tm", up)
    right = lax.ppermute(first, "tm", [(j, i) for i, j in up])
    normalized = pl.pallas_call(
        normalize_edges_kernel,
        out_shape=jax.ShapeDtypeStruct((ROWS, SLICE), bf16),
        in_specs=[smem(), vmem(), vmem(), vmem(), vmem()],
        out_specs=vmem(),
        compiler_params=PARAMS,
        name="normalize_edges",
    )(me, ends, left, right, inner)
    quads = [[QUAD * g + i for i in range(QUAD)] for g in range(N_TIME // QUAD)]
    windows = lax.all_to_all(
        normalized.reshape(QUAD, PART, SLICE), "tm", 0, 0, axis_index_groups=quads, tiled=True
    ).reshape(ROWS, SLICE)
    spectra = pl.pallas_call(
        spectra_kernel,
        out_shape=jax.ShapeDtypeStruct((BINS, 2 * PART), bf16),
        in_specs=[vmem(), vmem()],
        out_specs=vmem(),
        compiler_params=PARAMS,
        name="spectra",
    )(jnp.asarray(quarter_table()), windows)
    by_bin = lax.all_to_all(
        spectra.reshape(N_TIME, LOCAL_BINS // 2, 2, 2 * PART), "tm", 0, 0, tiled=True
    ).reshape(BINS, 2 * PART)
    mine = pl.pallas_call(
        arrange_kernel,
        out_shape=jax.ShapeDtypeStruct((BINS, 128), bf16),
        in_specs=[vmem()],
        out_specs=vmem(),
        compiler_params=PARAMS,
        name="arrange",
    )(by_bin)
    stations = lax.all_gather(mine, "pairs", axis=0, tiled=True)
    out = correlate(block_list, station_order, stations)
    out = out.reshape(SLOTS, LOCAL_BINS, GSIZE // 2, 2, 128)
    return jnp.transpose(out, (0, 1, 3, 2, 4)).reshape(SLOTS, LOCAL_BINS, 2, GSIZE * GSIZE)


def solution(mesh):
    placed = (P("pairs", "tm"), P(), P("pairs", None))
    return jax.shard_map(
        local, mesh=mesh, in_specs=placed, out_specs=P("pairs", "tm", None, None), check_vma=False
    )
```

```python
import math

import jax
import jax.numpy as jnp
import ml_dtypes
import numpy as np
from jax import lax
from jax.experimental import pallas as pl
from jax.experimental.pallas import tpu as pltpu
from jax.sharding import PartitionSpec as P

RECEIVER_TOTAL = 2048
GSIZE = 64
GROUPS = 32
SUBWIN = 16
SAMPLES = 4096
TIME = 65536
BINS = 384
FIRST_BIN = 8
BAND = 64
HALF = 64
SLOTS = 10
EPS = 1e-06

N_TIME = 64
N_OWNER = 8
QUAD = 4
SLICE = TIME // N_TIME
ROWS = RECEIVER_TOTAL // N_OWNER
PART = ROWS // QUAD
LOCAL_BINS = BINS // N_TIME
LINES = LOCAL_BINS * 2 * SUBWIN
EDGE = 128

f32 = jnp.float32
bf16 = jnp.bfloat16
NT = (((1,), (1,)), ((), ()))


def quarter_table():
    bins = np.arange(BINS)[:, None] + FIRST_BIN
    phase = (bins * np.arange(SLICE)[None, :] % SAMPLES) * (2.0 * math.pi / SAMPLES)
    return np.concatenate([np.cos(phase), -np.sin(phase)]).astype(ml_dtypes.bfloat16)


def band_matrix(span, step):
    k = lax.broadcasted_iota(jnp.int32, (span, step), 0)
    n = lax.broadcasted_iota(jnp.int32, (span, step), 1)
    return jnp.where(jnp.abs(k - EDGE - n) <= HALF, 1.0, 0.0).astype(bf16)


def normalize_inner_kernel(x_ref, up_ref, down_ref, ends_ref, out_ref):
    up_ref[...] = x_ref[:, SLICE - EDGE :]
    down_ref[...] = x_ref[:, :EDGE]
    ends_ref[:, : 2 * EDGE] = x_ref[:, : 2 * EDGE]
    ends_ref[:, 2 * EDGE :] = x_ref[:, SLICE - 2 * EDGE :]
    step = 256
    band = band_matrix(step + 2 * EDGE, step)
    for j in range((SLICE - 2 * EDGE) // step):
        mag = jnp.abs(x_ref[:, j * step : (j + 1) * step + 2 * EDGE])
        sums = jnp.dot(mag, band, preferred_element_type=f32)
        values = x_ref[:, j * step + EDGE : (j + 1) * step + EDGE].astype(f32)
        level = sums / (2 * HALF + 1)
        out_ref[:, j * step : (j + 1) * step] = (values / (level + EPS)).astype(bf16)


def normalize_edges_kernel(tm_ref, ends_ref, left_ref, right_ref, inner_ref, out_ref):
    band = band_matrix(3 * EDGE, EDGE)
    me = tm_ref[0]
    out_ref[:, EDGE : SLICE - EDGE] = inner_ref[...]
    left = jnp.abs(left_ref[...].astype(f32)) * jnp.where(me > 0, 1.0, 0.0)
    right = jnp.abs(right_ref[...].astype(f32)) * jnp.where(me < N_TIME - 1, 1.0, 0.0)
    head, tail = ends_ref[:, : 2 * EDGE], ends_ref[:, 2 * EDGE :]
    for start, values, mag in (
        (0, head[:, :EDGE], jnp.concatenate([left.astype(bf16), jnp.abs(head)], axis=1)),
        (SLICE - EDGE, tail[:, EDGE:], jnp.concatenate([jnp.abs(tail), right.astype(bf16)], axis=1)),
    ):
        sums = jnp.dot(mag, band, preferred_element_type=f32)
        position = me * SLICE + start + lax.broadcasted_iota(jnp.int32, (1, EDGE), 1)
        upper = jnp.minimum(position + HALF, TIME - 1)
        lower = jnp.maximum(position - HALF, 0)
        counts = (upper - lower + 1).astype(f32)
        out_ref[:, start : start + EDGE] = (
            values.astype(f32) / (sums / counts + EPS)
        ).astype(bf16)


def spectra_kernel(table_ref, y_ref, out_ref):
    p = lax.dot_general(table_ref[...], y_ref[...], NT, preferred_element_type=f32)
    re, im = p[:BINS], p[BINS:]
    f = lax.broadcasted_iota(jnp.int32, (BINS, 128), 0)
    lane = lax.broadcasted_iota(jnp.int32, (BINS, 128), 1)
    odd = (f & 1) == 1
    low = lane < PART
    u_re = jnp.where(odd, re[:, :128] - re[:, 128:], re[:, :128] + re[:, 128:])
    u_im = jnp.where(odd, im[:, :128] - im[:, 128:], im[:, :128] + im[:, 128:])
    sign = jnp.where((f & 3) < 2, 1.0, -1.0)
    v_re = sign * jnp.where(odd, u_im, u_re)
    v_im = sign * jnp.where(odd, -u_re, u_im)
    raw = jnp.where(low, u_re, v_im) + pltpu.roll(jnp.where(low, u_im, v_re), PART, 1)
    for m in range(BINS // BAND):
        block = raw[m * BAND : (m + 1) * BAND]
        power = jnp.sum(block * block, axis=0, keepdims=True)
        power = jnp.broadcast_to(power, (8, 128))
        power = power + pltpu.roll(power, PART, 1)
        level = jnp.sqrt(power / BAND + EPS)
        out_ref[m * BAND : (m + 1) * BAND] = (block / level[:1]).astype(bf16)


def arrange_kernel(x_ref, out_ref):
    out_ref[ROWS:] = jnp.zeros((ROWS, 128), bf16)
    o = lax.broadcasted_iota(jnp.int32, (BINS, BINS), 0)
    i = lax.broadcasted_iota(jnp.int32, (BINS, BINS), 1)
    per = LOCAL_BINS * SUBWIN
    source = (o % SUBWIN) * (QUAD * LOCAL_BINS) + (o // per) * LOCAL_BINS + (o % per) // SUBWIN
    pick = jnp.where(i == source, 1.0, 0.0).astype(bf16)
    z = jnp.dot(pick, x_ref[...], preferred_element_type=f32)
    low = lax.broadcasted_iota(jnp.int32, (per, 128), 1) < PART
    for h in range(QUAD // 2):
        first = z[2 * h * per : (2 * h + 1) * per]
        second = z[(2 * h + 1) * per : (2 * h + 2) * per]
        real = jnp.where(low, first, pltpu.roll(second, PART, 1))
        imag = jnp.where(low, pltpu.roll(first, PART, 1), second)
        lines = []
        for e in range(LOCAL_BINS):
            lines += [part[e * SUBWIN : (e + 1) * SUBWIN] for part in (real, imag)]
        stations = jnp.concatenate(lines, axis=0).T.astype(bf16)
        out_ref[h * 128 : (h + 1) * 128] = stations[:, :128]
        out_ref[ROWS + h * 128 : ROWS + (h + 1) * 128, :64] = stations[:, 128:]


def correlate_kernel(
    list_ref,
    order_ref,
    s_hbm,
    out_hbm,
    s_ref,
    main_ref,
    tail_ref,
    gm_ref,
    gt_ref,
    out_ref,
    in_sems,
    sems,
):
    loads = [
        pltpu.make_async_copy(s_hbm.at[n], s_ref.at[n], in_sems.at[n]) for n in range(N_OWNER)
    ]
    for load in loads:
        load.start()
    for n, load in enumerate(loads):
        load.wait()
        main_ref[n * ROWS : (n + 1) * ROWS] = s_ref[n, :ROWS].astype(f32)
        tail_ref[n * ROWS : (n + 1) * ROWS] = s_ref[n, ROWS:].astype(f32)

    rights = SLOTS * 2 * GSIZE
    for b in range(SLOTS):
        base = jnp.maximum(list_ref[0, b], 0) * GSIZE
        base_right = jnp.maximum(list_ref[1, b], 0) * GSIZE
        for i in range(0, GSIZE, 8):
            ids = [order_ref[base + i + u] for u in range(8)]
            ids_right = [order_ref[base_right + i + u] for u in range(8)]
            for source, g_ref in ((main_ref, gm_ref), (tail_ref, gt_ref)):
                rows = [source[pl.ds(station, 1), :] for station in ids]
                for parity in range(2):
                    at = b * 2 * GSIZE + parity * GSIZE + i
                    twice = [rows[u - u % 2 + parity] for u in range(8)]
                    g_ref[at : at + 8, :] = jnp.concatenate(twice, axis=0)
                at = rights + b * GSIZE + i
                g_ref[at : at + 8, :] = jnp.concatenate(
                    [source[pl.ds(station, 1), :] for station in ids_right], axis=0
                )

    k = lax.broadcasted_iota(jnp.int32, (128, 128), 0)
    n = lax.broadcasted_iota(jnp.int32, (128, 128), 1)
    turn = jnp.where(k == (n ^ SUBWIN), jnp.where((n & SUBWIN) == 0, -1.0, 1.0), 0.0).astype(bf16)
    imag_row = (lax.broadcasted_iota(jnp.int32, (rights, 128), 0) & 1) == 1
    lefts = []
    for g_ref in (gm_ref, gt_ref):
        plain = g_ref[:rights]
        turned = jnp.dot(plain.astype(bf16), turn, preferred_element_type=f32)
        lefts.append(jnp.where(imag_row, turned, plain).astype(bf16))
    bin_of = lax.broadcasted_iota(jnp.int32, (GSIZE, 128), 1) // (2 * SUBWIN)
    zero = jnp.zeros((GSIZE, 128), bf16)
    copies = []
    for b in range(SLOTS):
        scale = jnp.where(list_ref[0, b] >= 0, 1.0 / SUBWIN, 0.0)
        for a, g_ref, bin0, count in ((lefts[0], gm_ref, 0, 4), (lefts[1], gt_ref, 4, 2)):
            at = b * 2 * GSIZE
            lhs = jnp.concatenate(
                [a[at : at + GSIZE], a[at + GSIZE : at + 2 * GSIZE]], axis=1
            )
            r = g_ref[rights + b * GSIZE : rights + (b + 1) * GSIZE]
            blocks = []
            for e in range(count):
                kept = jnp.where(bin_of == e, r, 0.0).astype(bf16)
                blocks.append(jnp.concatenate([kept, zero], axis=1))
                blocks.append(jnp.concatenate([zero, kept], axis=1))
            rhs = jnp.concatenate(blocks, axis=0)
            c = lax.dot_general(lhs, rhs, NT, preferred_element_type=f32) * scale
            for e in range(count):
                out_ref[b, bin0 + e] = c[:, e * 128 : (e + 1) * 128].astype(bf16)
        copies.append(pltpu.make_async_copy(out_ref.at[b], out_hbm.at[b], sems.at[b]))
        copies[-1].start()
    for copy in copies:
        copy.wait()


def vmem():
    return pl.BlockSpec(memory_space=pltpu.VMEM)


def smem():
    return pl.BlockSpec(memory_space=pltpu.SMEM)


PARAMS = pltpu.CompilerParams(vmem_limit_bytes=40 * 1024 * 1024)


def correlate(block_list, station_order, stations):
    return pl.pallas_call(
        correlate_kernel,
        out_shape=jax.ShapeDtypeStruct((SLOTS, LOCAL_BINS, GSIZE, 128), bf16),
        in_specs=[smem(), smem(), pl.BlockSpec(memory_space=pltpu.HBM)],
        out_specs=pl.BlockSpec(memory_space=pltpu.HBM),
        scratch_shapes=[
            pltpu.VMEM((N_OWNER, 2 * ROWS, 128), bf16),
            pltpu.VMEM((RECEIVER_TOTAL, 128), f32),
            pltpu.VMEM((RECEIVER_TOTAL, 128), f32),
            pltpu.VMEM((SLOTS * 3 * GSIZE, 128), f32),
            pltpu.VMEM((SLOTS * 3 * GSIZE, 128), f32),
            pltpu.VMEM((SLOTS, LOCAL_BINS, GSIZE, 128), bf16),
            pltpu.SemaphoreType.DMA((N_OWNER,)),
            pltpu.SemaphoreType.DMA((SLOTS,)),
        ],
        compiler_params=pltpu.CompilerParams(vmem_limit_bytes=60 * 1024 * 1024),
        name="correlate",
    )(block_list.T, station_order, stations.reshape(N_OWNER, 2 * ROWS, 128))


def local(records, station_order, block_list):
    me = lax.axis_index("tm").astype(jnp.int32).reshape(1)
    up = [(i, (i + 1) % N_TIME) for i in range(N_TIME)]
    last, first, ends, inner = pl.pallas_call(
        normalize_inner_kernel,
        out_shape=[
            jax.ShapeDtypeStruct((ROWS, EDGE), bf16),
            jax.ShapeDtypeStruct((ROWS, EDGE), bf16),
            jax.ShapeDtypeStruct((ROWS, 4 * EDGE), bf16),
            jax.ShapeDtypeStruct((ROWS, SLICE - 2 * EDGE), bf16),
        ],
        in_specs=[vmem()],
        out_specs=[vmem()] * 4,
        compiler_params=PARAMS,
        name="normalize_inner",
    )(records)
    left = lax.ppermute(last, "tm", up)
    right = lax.ppermute(first, "tm", [(j, i) for i, j in up])
    normalized = pl.pallas_call(
        normalize_edges_kernel,
        out_shape=jax.ShapeDtypeStruct((ROWS, SLICE), bf16),
        in_specs=[smem(), vmem(), vmem(), vmem(), vmem()],
        out_specs=vmem(),
        compiler_params=PARAMS,
        name="normalize_edges",
    )(me, ends, left, right, inner)
    quads = [[QUAD * g + i for i in range(QUAD)] for g in range(N_TIME // QUAD)]
    windows = lax.all_to_all(
        normalized.reshape(QUAD, PART, SLICE), "tm", 0, 0, axis_index_groups=quads, tiled=True
    ).reshape(ROWS, SLICE)
    spectra = pl.pallas_call(
        spectra_kernel,
        out_shape=jax.ShapeDtypeStruct((BINS, 2 * PART), bf16),
        in_specs=[vmem(), vmem()],
        out_specs=vmem(),
        compiler_params=PARAMS,
        name="spectra",
    )(jnp.asarray(quarter_table()), windows)
    by_bin = lax.all_to_all(
        spectra.reshape(N_TIME, LOCAL_BINS // 2, 2, 2 * PART), "tm", 0, 0, tiled=True
    ).reshape(BINS, 2 * PART)
    mine = pl.pallas_call(
        arrange_kernel,
        out_shape=jax.ShapeDtypeStruct((2 * ROWS, 128), bf16),
        in_specs=[vmem()],
        out_specs=vmem(),
        compiler_params=PARAMS,
        name="arrange",
    )(by_bin)
    stations = lax.all_gather(mine, "pairs", axis=0, tiled=True)
    out = correlate(block_list, station_order, stations)
    out = out.reshape(SLOTS, LOCAL_BINS, GSIZE // 2, 2, 128)
    return jnp.transpose(out, (0, 1, 3, 2, 4)).reshape(SLOTS, LOCAL_BINS, 2, GSIZE * GSIZE)


def solution(mesh):
    placed = (P("pairs", "tm"), P(), P("pairs", None))
    return jax.shard_map(
        local, mesh=mesh, in_specs=placed, out_specs=P("pairs", "tm", None, None), check_vma=False
    )
```

```python
import math

import jax
import jax.numpy as jnp
import ml_dtypes
import numpy as np
from jax import lax
from jax.experimental import pallas as pl
from jax.experimental.pallas import tpu as pltpu
from jax.sharding import PartitionSpec as P

RECEIVER_TOTAL = 2048
GSIZE = 64
GROUPS = 32
SUBWIN = 16
SAMPLES = 4096
TIME = 65536
BINS = 384
FIRST_BIN = 8
BAND = 64
HALF = 64
SLOTS = 10
EPS = 1e-06

N_TIME = 64
N_OWNER = 8
QUAD = 4
SLICE = TIME // N_TIME
ROWS = RECEIVER_TOTAL // N_OWNER
PART = ROWS // QUAD
LOCAL_BINS = BINS // N_TIME
LINES = LOCAL_BINS * 2 * SUBWIN
EDGE = 128

f32 = jnp.float32
bf16 = jnp.bfloat16
NT = (((1,), (1,)), ((), ()))


def quarter_table():
    bins = np.arange(BINS)[:, None] + FIRST_BIN
    phase = (bins * np.arange(SLICE)[None, :] % SAMPLES) * (2.0 * math.pi / SAMPLES)
    return np.concatenate([np.cos(phase), -np.sin(phase)]).astype(ml_dtypes.bfloat16)


def stage_kernel(x_ref, out_ref):
    out_ref[:, :SLICE] = x_ref[...]
    out_ref[:, SLICE:] = jnp.zeros((ROWS, EDGE), bf16)


def join_kernel(edge_ref, _, out_ref, sem):
    copy = pltpu.make_async_copy(edge_ref, out_ref.at[:, SLICE:], sem)
    copy.start()
    copy.wait()


def normalize(me, x, edge):
    quarter = ROWS // QUAD
    first, last = me == 0, me == SUBWIN - 1
    before = edge[:quarter].astype(f32) * jnp.where(first, 0.0, 1.0)
    after = edge[ROWS - quarter :].astype(f32) * jnp.where(last, 0.0, 1.0)
    left = jnp.concatenate([before.astype(bf16), x[: ROWS - quarter, SLICE - EDGE :]], axis=0)
    right = jnp.concatenate([x[quarter:, :EDGE], after.astype(bf16)], axis=0)
    mag = jnp.abs(jnp.concatenate([left, x, right], axis=1))
    step = 256
    span = step + 2 * EDGE
    k = lax.broadcasted_iota(jnp.int32, (span, step), 0)
    n = lax.broadcasted_iota(jnp.int32, (span, step), 1)
    band = jnp.where(jnp.abs(k - EDGE - n) <= HALF, 1.0, 0.0).astype(bf16)
    row = lax.broadcasted_iota(jnp.int32, (ROWS, step), 0)
    lane = lax.broadcasted_iota(jnp.int32, (ROWS, step), 1)
    blocks = []
    for j in range(SLICE // step):
        sums = jnp.dot(mag[:, j * step : j * step + span], band, preferred_element_type=f32)
        position = me * SAMPLES + (row // quarter) * SLICE + j * step + lane
        upper = jnp.minimum(position + HALF, TIME - 1)
        lower = jnp.maximum(position - HALF, 0)
        counts = (upper - lower + 1).astype(f32)
        values = x[:, j * step : (j + 1) * step].astype(f32)
        blocks.append((values / (sums / counts + EPS)).astype(bf16))
    return jnp.concatenate(blocks, axis=1)


def spectra_kernel(me_ref, table_ref, x_ref, out_ref):
    y = normalize(me_ref[0] // QUAD, x_ref[:, :SLICE], x_ref[:, SLICE:])
    p = lax.dot_general(table_ref[...], y, NT, preferred_element_type=f32)
    re, im = p[:BINS], p[BINS:]
    f = lax.broadcasted_iota(jnp.int32, (BINS, 128), 0)
    lane = lax.broadcasted_iota(jnp.int32, (BINS, 128), 1)
    odd = (f & 1) == 1
    low = lane < PART
    u_re = jnp.where(odd, re[:, :128] - re[:, 128:], re[:, :128] + re[:, 128:])
    u_im = jnp.where(odd, im[:, :128] - im[:, 128:], im[:, :128] + im[:, 128:])
    sign = jnp.where((f & 3) < 2, 1.0, -1.0)
    v_re = sign * jnp.where(odd, u_im, u_re)
    v_im = sign * jnp.where(odd, -u_re, u_im)
    raw = jnp.where(low, u_re, v_im) + pltpu.roll(jnp.where(low, u_im, v_re), PART, 1)
    for m in range(BINS // BAND):
        block = raw[m * BAND : (m + 1) * BAND]
        power = jnp.sum(block * block, axis=0, keepdims=True)
        power = jnp.broadcast_to(power, (8, 128))
        power = power + pltpu.roll(power, PART, 1)
        level = jnp.sqrt(power / BAND + EPS)
        out_ref[m * BAND : (m + 1) * BAND] = (block / level[:1]).astype(bf16)


def arrange_kernel(x_ref, out_ref):
    o = lax.broadcasted_iota(jnp.int32, (BINS, BINS), 0)
    i = lax.broadcasted_iota(jnp.int32, (BINS, BINS), 1)
    per = LOCAL_BINS * SUBWIN
    source = (o % SUBWIN) * (QUAD * LOCAL_BINS) + (o // per) * LOCAL_BINS + (o % per) // SUBWIN
    pick = jnp.where(i == source, 1.0, 0.0).astype(bf16)
    z = jnp.dot(pick, x_ref[...], preferred_element_type=f32)
    low = lax.broadcasted_iota(jnp.int32, (per, 128), 1) < PART
    for h in range(QUAD // 2):
        first = z[2 * h * per : (2 * h + 1) * per]
        second = z[(2 * h + 1) * per : (2 * h + 2) * per]
        real = jnp.where(low, first, pltpu.roll(second, PART, 1))
        imag = jnp.where(low, pltpu.roll(first, PART, 1), second)
        lines = []
        for e in range(LOCAL_BINS):
            lines += [part[e * SUBWIN : (e + 1) * SUBWIN] for part in (real, imag)]
        stations = jnp.concatenate(lines, axis=0).T.astype(bf16)
        out_ref[h * 128 : (h + 1) * 128] = stations[:, :128]
        out_ref[ROWS:, h * 64 : (h + 1) * 64] = stations[:, 128:]


def correlate_kernel(
    list_ref, order_ref, s_ref, out_hbm, main_ref, tail_ref, gm_ref, gt_ref, out_ref, sems
):
    for n in range(N_OWNER):
        block = s_ref[n * BINS : (n + 1) * BINS].astype(f32)
        main_ref[n * ROWS : (n + 1) * ROWS] = block[:ROWS]
        tail_ref[n * ROWS : n * ROWS + 128] = block[ROWS:]
        tail_ref[n * ROWS + 128 : (n + 1) * ROWS] = pltpu.roll(block[ROWS:], 64, 1)

    rights = SLOTS * 2 * GSIZE
    for b in range(SLOTS):
        base = jnp.maximum(list_ref[0, b], 0) * GSIZE
        base_right = jnp.maximum(list_ref[1, b], 0) * GSIZE
        for i in range(0, GSIZE, 8):
            ids = [order_ref[base + i + u] for u in range(8)]
            ids_right = [order_ref[base_right + i + u] for u in range(8)]
            for source, g_ref in ((main_ref, gm_ref), (tail_ref, gt_ref)):
                rows = [source[pl.ds(station, 1), :] for station in ids]
                for parity in range(2):
                    at = b * 2 * GSIZE + parity * GSIZE + i
                    twice = [rows[u - u % 2 + parity] for u in range(8)]
                    g_ref[at : at + 8, :] = jnp.concatenate(twice, axis=0)
                at = rights + b * GSIZE + i
                g_ref[at : at + 8, :] = jnp.concatenate(
                    [source[pl.ds(station, 1), :] for station in ids_right], axis=0
                )

    k = lax.broadcasted_iota(jnp.int32, (128, 128), 0)
    n = lax.broadcasted_iota(jnp.int32, (128, 128), 1)
    turn = jnp.where(k == (n ^ SUBWIN), jnp.where((n & SUBWIN) == 0, -1.0, 1.0), 0.0).astype(bf16)
    imag_row = (lax.broadcasted_iota(jnp.int32, (rights, 128), 0) & 1) == 1
    lefts = []
    for g_ref in (gm_ref, gt_ref):
        plain = g_ref[:rights]
        turned = jnp.dot(plain.astype(bf16), turn, preferred_element_type=f32)
        lefts.append(jnp.where(imag_row, turned, plain).astype(bf16))
    bin_of = lax.broadcasted_iota(jnp.int32, (GSIZE, 128), 1) // (2 * SUBWIN)
    zero = jnp.zeros((GSIZE, 128), bf16)
    copies = []
    for b in range(SLOTS):
        scale = jnp.where(list_ref[0, b] >= 0, 1.0 / SUBWIN, 0.0)
        for a, g_ref, bin0, count in ((lefts[0], gm_ref, 0, 4), (lefts[1], gt_ref, 4, 2)):
            at = b * 2 * GSIZE
            lhs = jnp.concatenate(
                [a[at : at + GSIZE], a[at + GSIZE : at + 2 * GSIZE]], axis=1
            )
            r = g_ref[rights + b * GSIZE : rights + (b + 1) * GSIZE]
            blocks = []
            for e in range(count):
                kept = jnp.where(bin_of == e, r, 0.0).astype(bf16)
                blocks.append(jnp.concatenate([kept, zero], axis=1))
                blocks.append(jnp.concatenate([zero, kept], axis=1))
            rhs = jnp.concatenate(blocks, axis=0)
            c = lax.dot_general(lhs, rhs, NT, preferred_element_type=f32) * scale
            for e in range(count):
                out_ref[b, bin0 + e] = c[:, e * 128 : (e + 1) * 128].astype(bf16)
        copies.append(pltpu.make_async_copy(out_ref.at[b], out_hbm.at[b], sems.at[b]))
        copies[-1].start()
    for copy in copies:
        copy.wait()


def vmem():
    return pl.BlockSpec(memory_space=pltpu.VMEM)


def smem():
    return pl.BlockSpec(memory_space=pltpu.SMEM)


PARAMS = pltpu.CompilerParams(vmem_limit_bytes=40 * 1024 * 1024)


def correlate(block_list, station_order, stations):
    return pl.pallas_call(
        correlate_kernel,
        out_shape=jax.ShapeDtypeStruct((SLOTS, LOCAL_BINS, GSIZE, 128), bf16),
        in_specs=[smem(), smem(), vmem()],
        out_specs=pl.BlockSpec(memory_space=pltpu.HBM),
        scratch_shapes=[
            pltpu.VMEM((RECEIVER_TOTAL, 128), f32),
            pltpu.VMEM((RECEIVER_TOTAL, 128), f32),
            pltpu.VMEM((SLOTS * 3 * GSIZE, 128), f32),
            pltpu.VMEM((SLOTS * 3 * GSIZE, 128), f32),
            pltpu.VMEM((SLOTS, LOCAL_BINS, GSIZE, 128), bf16),
            pltpu.SemaphoreType.DMA((SLOTS,)),
        ],
        compiler_params=PARAMS,
        name="correlate",
    )(block_list.T, station_order, stations)


def local(records, station_order, block_list):
    me = lax.axis_index("tm").astype(jnp.int32)
    facing = lax.dynamic_slice(records, (0, (me & 1) * (SLICE - EDGE)), (ROWS, EDGE))
    swap = [(i, i + 1 if i % 2 else i - 1) for i in range(N_TIME)]
    edge = lax.ppermute(facing, "tm", [(i, j % N_TIME) for i, j in swap])
    staged = pl.pallas_call(
        stage_kernel,
        out_shape=jax.ShapeDtypeStruct((ROWS, SLICE + EDGE), bf16),
        in_specs=[vmem()],
        out_specs=vmem(),
        compiler_params=PARAMS,
        cost_estimate=pl.CostEstimate(
            flops=2 * ROWS * SLICE * 512, bytes_accessed=4 * ROWS * SLICE, transcendentals=0
        ),
        name="stage",
    )(records)
    extended = pl.pallas_call(
        join_kernel,
        out_shape=jax.ShapeDtypeStruct((ROWS, SLICE + EDGE), bf16),
        in_specs=[pl.BlockSpec(memory_space=pl.ANY)] * 2,
        out_specs=pl.BlockSpec(memory_space=pl.ANY),
        scratch_shapes=[pltpu.SemaphoreType.DMA(())],
        input_output_aliases={1: 0},
        compiler_params=PARAMS,
        name="join",
    )(edge, staged)
    quads = [[QUAD * g + i for i in range(QUAD)] for g in range(N_TIME // QUAD)]
    windows = lax.all_to_all(
        extended.reshape(QUAD, PART, SLICE + EDGE), "tm", 0, 0, axis_index_groups=quads, tiled=True
    ).reshape(ROWS, SLICE + EDGE)
    spectra = pl.pallas_call(
        spectra_kernel,
        out_shape=jax.ShapeDtypeStruct((BINS, 2 * PART), bf16),
        in_specs=[smem(), vmem(), vmem()],
        out_specs=vmem(),
        compiler_params=PARAMS,
        name="spectra",
    )(me.reshape(1), jnp.asarray(quarter_table()), windows)
    by_bin = lax.all_to_all(
        spectra.reshape(N_TIME, LOCAL_BINS // 2, 2, 2 * PART), "tm", 0, 0, tiled=True
    ).reshape(BINS, 2 * PART)
    mine = pl.pallas_call(
        arrange_kernel,
        out_shape=jax.ShapeDtypeStruct((BINS, 128), bf16),
        in_specs=[vmem()],
        out_specs=vmem(),
        compiler_params=PARAMS,
        name="arrange",
    )(by_bin)
    stations = lax.all_gather(mine, "pairs", axis=0, tiled=True)
    out = correlate(block_list, station_order, stations)
    out = out.reshape(SLOTS, LOCAL_BINS, GSIZE // 2, 2, 128)
    return jnp.transpose(out, (0, 1, 3, 2, 4)).reshape(SLOTS, LOCAL_BINS, 2, GSIZE * GSIZE)


def solution(mesh):
    placed = (P("pairs", "tm"), P(), P("pairs", None))
    return jax.shard_map(
        local, mesh=mesh, in_specs=placed, out_specs=P("pairs", "tm", None, None), check_vma=False
    )
```

```python
import math

import jax
import jax.numpy as jnp
import ml_dtypes
import numpy as np
from jax import lax
from jax.experimental import pallas as pl
from jax.experimental.pallas import tpu as pltpu
from jax.sharding import PartitionSpec as P

RECEIVER_TOTAL = 2048
GSIZE = 64
GROUPS = 32
SUBWIN = 16
SAMPLES = 4096
TIME = 65536
BINS = 384
FIRST_BIN = 8
BAND = 64
HALF = 64
SLOTS = 10
EPS = 1e-06

N_TIME = 64
N_OWNER = 8
QUAD = 4
SLICE = TIME // N_TIME
ROWS = RECEIVER_TOTAL // N_OWNER
PART = ROWS // QUAD
LOCAL_BINS = BINS // N_TIME
LINES = LOCAL_BINS * 2 * SUBWIN
EDGE = 128

f32 = jnp.float32
bf16 = jnp.bfloat16
NT = (((1,), (1,)), ((), ()))


def quarter_table():
    bins = np.arange(BINS)[:, None] + FIRST_BIN
    phase = (bins * np.arange(SLICE)[None, :] % SAMPLES) * (2.0 * math.pi / SAMPLES)
    return np.concatenate([np.cos(phase), -np.sin(phase)]).astype(ml_dtypes.bfloat16)


def stage_kernel(x_ref, out_ref):
    out_ref[:, :SLICE] = x_ref[...]
    out_ref[:, SLICE:] = jnp.zeros((ROWS, EDGE), bf16)


def join_kernel(edge_ref, _, out_ref, sem):
    copy = pltpu.make_async_copy(edge_ref, out_ref.at[:, SLICE:], sem)
    copy.start()
    copy.wait()


def normalize(me, x, edge):
    quarter = ROWS // QUAD
    first, last = me == 0, me == SUBWIN - 1
    before = edge[:quarter].astype(f32) * jnp.where(first, 0.0, 1.0)
    after = edge[ROWS - quarter :].astype(f32) * jnp.where(last, 0.0, 1.0)
    left = jnp.concatenate([before.astype(bf16), x[: ROWS - quarter, SLICE - EDGE :]], axis=0)
    right = jnp.concatenate([x[quarter:, :EDGE], after.astype(bf16)], axis=0)
    mag = jnp.abs(jnp.concatenate([left, x, right], axis=1))
    step = 256
    span = step + 2 * EDGE
    k = lax.broadcasted_iota(jnp.int32, (span, step), 0)
    n = lax.broadcasted_iota(jnp.int32, (span, step), 1)
    band = jnp.where(jnp.abs(k - EDGE - n) <= HALF, 1.0, 0.0).astype(bf16)
    row = lax.broadcasted_iota(jnp.int32, (ROWS, step), 0)
    lane = lax.broadcasted_iota(jnp.int32, (ROWS, step), 1)
    blocks = []
    for j in range(SLICE // step):
        sums = jnp.dot(mag[:, j * step : j * step + span], band, preferred_element_type=f32)
        counts = 2 * HALF + 1.0
        if j == 0 or j == SLICE // step - 1:
            position = me * SAMPLES + (row // quarter) * SLICE + j * step + lane
            upper = jnp.minimum(position + HALF, TIME - 1)
            lower = jnp.maximum(position - HALF, 0)
            counts = (upper - lower + 1).astype(f32)
        values = x[:, j * step : (j + 1) * step].astype(f32)
        blocks.append((values / (sums / counts + EPS)).astype(bf16))
    return jnp.concatenate(blocks, axis=1)


def spectra_kernel(table_ref, x_ref, out_ref):
    y = normalize(lax.axis_index("tm") // QUAD, x_ref[:, :SLICE], x_ref[:, SLICE:])
    p = lax.dot_general(table_ref[...], y, NT, preferred_element_type=f32)
    re, im = p[:BINS], p[BINS:]
    f = lax.broadcasted_iota(jnp.int32, (BINS, 128), 0)
    lane = lax.broadcasted_iota(jnp.int32, (BINS, 128), 1)
    odd = (f & 1) == 1
    low = lane < PART
    u_re = jnp.where(odd, re[:, :128] - re[:, 128:], re[:, :128] + re[:, 128:])
    u_im = jnp.where(odd, im[:, :128] - im[:, 128:], im[:, :128] + im[:, 128:])
    sign = jnp.where((f & 3) < 2, 1.0, -1.0)
    v_re = sign * jnp.where(odd, u_im, u_re)
    v_im = sign * jnp.where(odd, -u_re, u_im)
    raw = jnp.where(low, u_re, v_im) + pltpu.roll(jnp.where(low, u_im, v_re), PART, 1)
    for m in range(BINS // BAND):
        block = raw[m * BAND : (m + 1) * BAND]
        power = jnp.sum(block * block, axis=0, keepdims=True)
        power = jnp.broadcast_to(power, (8, 128))
        power = power + pltpu.roll(power, PART, 1)
        level = jnp.sqrt(power / BAND + EPS)
        out_ref[m * BAND : (m + 1) * BAND] = (block / level[:1]).astype(bf16)


def arrange_kernel(x_ref, out_ref):
    o = lax.broadcasted_iota(jnp.int32, (BINS, BINS), 0)
    i = lax.broadcasted_iota(jnp.int32, (BINS, BINS), 1)
    per = LOCAL_BINS * SUBWIN
    source = (o % SUBWIN) * (QUAD * LOCAL_BINS) + (o // per) * LOCAL_BINS + (o % per) // SUBWIN
    pick = jnp.where(i == source, 1.0, 0.0).astype(bf16)
    z = jnp.dot(pick, x_ref[...], preferred_element_type=f32)
    low = lax.broadcasted_iota(jnp.int32, (per, 128), 1) < PART
    for h in range(QUAD // 2):
        first = z[2 * h * per : (2 * h + 1) * per]
        second = z[(2 * h + 1) * per : (2 * h + 2) * per]
        real = jnp.where(low, first, pltpu.roll(second, PART, 1))
        imag = jnp.where(low, pltpu.roll(first, PART, 1), second)
        lines = []
        for e in range(LOCAL_BINS):
            lines += [part[e * SUBWIN : (e + 1) * SUBWIN] for part in (real, imag)]
        stations = jnp.concatenate(lines, axis=0).T.astype(bf16)
        out_ref[h * 128 : (h + 1) * 128] = stations[:, :128]
        out_ref[ROWS:, h * 64 : (h + 1) * 64] = stations[:, 128:]


def correlate_kernel(
    list_any,
    order_any,
    s_ref,
    out_hbm,
    main_ref,
    tail_ref,
    gm_ref,
    gt_ref,
    out_ref,
    order_ref,
    order_sem,
    list_ref,
    list_sem,
    sems,
):
    order_copy = pltpu.make_async_copy(order_any, order_ref, order_sem)
    order_copy.start()
    list_copy = pltpu.make_async_copy(list_any, list_ref, list_sem)
    list_copy.start()
    for n in range(N_OWNER):
        block = s_ref[n * BINS : (n + 1) * BINS].astype(f32)
        main_ref[n * ROWS : (n + 1) * ROWS] = block[:ROWS]
        tail_ref[n * ROWS : n * ROWS + 128] = block[ROWS:]
        tail_ref[n * ROWS + 128 : (n + 1) * ROWS] = pltpu.roll(block[ROWS:], 64, 1)

    order_copy.wait()
    list_copy.wait()
    rights = SLOTS * 2 * GSIZE
    sub = lax.broadcasted_iota(jnp.int32, (8, 128), 0)
    for b in range(SLOTS):
        base = jnp.maximum(list_ref[0, b], 0) * GSIZE
        base_right = jnp.maximum(list_ref[1, b], 0) * GSIZE
        for i in range(0, GSIZE, 8):
            ids = [order_ref[base + i + u] for u in range(8)]
            ids_right = [order_ref[base_right + i + u] for u in range(8)]
            for source, g_ref in ((main_ref, gm_ref), (tail_ref, gt_ref)):
                rows = [source[pl.ds(station, 8, stride=0), :] for station in ids]
                for parity in range(2):
                    at = b * 2 * GSIZE + parity * GSIZE + i
                    low = jnp.where(sub < 2, rows[parity], rows[2 + parity])
                    high = jnp.where(sub < 6, rows[4 + parity], rows[6 + parity])
                    g_ref[at : at + 8, :] = jnp.where(sub < 4, low, high)
                rows = [source[pl.ds(station, 8, stride=0), :] for station in ids_right]
                pairs = [jnp.where(sub % 2 == 0, rows[u], rows[u + 1]) for u in range(0, 8, 2)]
                low = jnp.where(sub < 2, pairs[0], pairs[1])
                high = jnp.where(sub < 6, pairs[2], pairs[3])
                at = rights + b * GSIZE + i
                g_ref[at : at + 8, :] = jnp.where(sub < 4, low, high)

    k = lax.broadcasted_iota(jnp.int32, (128, 128), 0)
    n = lax.broadcasted_iota(jnp.int32, (128, 128), 1)
    turn = jnp.where(k == (n ^ SUBWIN), jnp.where((n & SUBWIN) == 0, -1.0, 1.0), 0.0).astype(bf16)
    imag_row = (lax.broadcasted_iota(jnp.int32, (rights, 128), 0) & 1) == 1
    lefts = []
    for g_ref in (gm_ref, gt_ref):
        plain = g_ref[:rights]
        turned = jnp.dot(plain.astype(bf16), turn, preferred_element_type=f32)
        lefts.append(jnp.where(imag_row, turned, plain).astype(bf16))
    bin_of = (lax.broadcasted_iota(jnp.int32, (GSIZE, 256), 1) & 127) // (2 * SUBWIN)
    keeps = [jnp.where(bin_of == e, 1.0, 0.0).astype(bf16) for e in range(4)]
    zero = jnp.zeros((GSIZE, 128), bf16)
    copies = []
    for b in range(SLOTS):
        scale = jnp.where(list_ref[0, b] >= 0, 1.0 / SUBWIN, 0.0)
        for a, g_ref, bin0, count in ((lefts[0], gm_ref, 0, 4), (lefts[1], gt_ref, 4, 2)):
            at = b * 2 * GSIZE
            lhs = jnp.concatenate(
                [a[at : at + GSIZE], a[at + GSIZE : at + 2 * GSIZE]], axis=1
            )
            lhs = jnp.concatenate([lhs * keep for keep in keeps[:count]], axis=0)
            r = g_ref[rights + b * GSIZE : rights + (b + 1) * GSIZE].astype(bf16)
            rhs = jnp.concatenate(
                [jnp.concatenate([r, zero], axis=1), jnp.concatenate([zero, r], axis=1)], axis=0
            )
            c = lax.dot_general(lhs, rhs, NT, preferred_element_type=f32) * scale
            for e in range(count):
                out_ref[b, bin0 + e] = c[e * GSIZE : (e + 1) * GSIZE].astype(bf16)
        copies.append(pltpu.make_async_copy(out_ref.at[b], out_hbm.at[b], sems.at[b]))
        copies[-1].start()
    for copy in copies:
        copy.wait()


def vmem():
    return pl.BlockSpec(memory_space=pltpu.VMEM)


PARAMS = pltpu.CompilerParams(vmem_limit_bytes=40 * 1024 * 1024)


def correlate(block_list, station_order, stations):
    return pl.pallas_call(
        correlate_kernel,
        out_shape=jax.ShapeDtypeStruct((SLOTS, LOCAL_BINS, GSIZE, 128), bf16),
        in_specs=[pl.BlockSpec(memory_space=pl.ANY), pl.BlockSpec(memory_space=pl.ANY), vmem()],
        out_specs=pl.BlockSpec(memory_space=pltpu.HBM),
        scratch_shapes=[
            pltpu.VMEM((RECEIVER_TOTAL, 128), f32),
            pltpu.VMEM((RECEIVER_TOTAL, 128), f32),
            pltpu.VMEM((SLOTS * 3 * GSIZE, 128), f32),
            pltpu.VMEM((SLOTS * 3 * GSIZE, 128), f32),
            pltpu.VMEM((SLOTS, LOCAL_BINS, GSIZE, 128), bf16),
            pltpu.SMEM((RECEIVER_TOTAL,), jnp.int32),
            pltpu.SemaphoreType.DMA(()),
            pltpu.SMEM((2, SLOTS), jnp.int32),
            pltpu.SemaphoreType.DMA(()),
            pltpu.SemaphoreType.DMA((SLOTS,)),
        ],
        compiler_params=PARAMS,
        name="correlate",
    )(block_list.T, station_order, stations)


def local(records, station_order, block_list):
    me = lax.axis_index("tm").astype(jnp.int32)
    facing = lax.dynamic_slice(records, (0, (me & 1) * (SLICE - EDGE)), (ROWS, EDGE))
    swap = [(i, i + 1 if i % 2 else i - 1) for i in range(N_TIME)]
    edge = lax.ppermute(facing, "tm", [(i, j % N_TIME) for i, j in swap])
    staged = pl.pallas_call(
        stage_kernel,
        out_shape=jax.ShapeDtypeStruct((ROWS, SLICE + EDGE), bf16),
        in_specs=[vmem()],
        out_specs=vmem(),
        compiler_params=PARAMS,
        cost_estimate=pl.CostEstimate(
            flops=2 * ROWS * SLICE * 512, bytes_accessed=4 * ROWS * SLICE, transcendentals=0
        ),
        name="stage",
    )(records)
    extended = pl.pallas_call(
        join_kernel,
        out_shape=jax.ShapeDtypeStruct((ROWS, SLICE + EDGE), bf16),
        in_specs=[pl.BlockSpec(memory_space=pl.ANY)] * 2,
        out_specs=pl.BlockSpec(memory_space=pl.ANY),
        scratch_shapes=[pltpu.SemaphoreType.DMA(())],
        input_output_aliases={1: 0},
        compiler_params=PARAMS,
        name="join",
    )(edge, staged)
    quads = [[QUAD * g + i for i in range(QUAD)] for g in range(N_TIME // QUAD)]
    windows = lax.all_to_all(
        extended.reshape(QUAD, PART, SLICE + EDGE), "tm", 0, 0, axis_index_groups=quads, tiled=True
    ).reshape(ROWS, SLICE + EDGE)
    spectra = pl.pallas_call(
        spectra_kernel,
        out_shape=jax.ShapeDtypeStruct((BINS, 2 * PART), bf16),
        in_specs=[vmem(), vmem()],
        out_specs=vmem(),
        compiler_params=PARAMS,
        name="spectra",
    )(jnp.asarray(quarter_table()), windows)
    by_bin = lax.all_to_all(
        spectra.reshape(N_TIME, LOCAL_BINS // 2, 2, 2 * PART), "tm", 0, 0, tiled=True
    ).reshape(BINS, 2 * PART)
    mine = pl.pallas_call(
        arrange_kernel,
        out_shape=jax.ShapeDtypeStruct((BINS, 128), bf16),
        in_specs=[vmem()],
        out_specs=vmem(),
        compiler_params=PARAMS,
        name="arrange",
    )(by_bin)
    stations = lax.all_gather(mine, "pairs", axis=0, tiled=True)
    out = correlate(block_list, station_order, stations)
    out = out.reshape(SLOTS, LOCAL_BINS, GSIZE // 2, 2, 128)
    return jnp.transpose(out, (0, 1, 3, 2, 4)).reshape(SLOTS, LOCAL_BINS, 2, GSIZE * GSIZE)


def solution(mesh):
    placed = (P("pairs", "tm"), P(), P("pairs", None))
    return jax.shard_map(
        local, mesh=mesh, in_specs=placed, out_specs=P("pairs", "tm", None, None), check_vma=False
    )
```

```python
import math

import jax
import jax.numpy as jnp
import ml_dtypes
import numpy as np
from jax import lax
from jax.experimental import pallas as pl
from jax.experimental.pallas import tpu as pltpu
from jax.sharding import PartitionSpec as P

RECEIVER_TOTAL = 2048
GSIZE = 64
GROUPS = 32
SUBWIN = 16
SAMPLES = 4096
TIME = 65536
BINS = 384
FIRST_BIN = 8
BAND = 64
HALF = 64
SLOTS = 10
EPS = 1e-06

N_TIME = 64
N_OWNER = 8
QUAD = 4
SLICE = TIME // N_TIME
ROWS = RECEIVER_TOTAL // N_OWNER
PART = ROWS // QUAD
LOCAL_BINS = BINS // N_TIME
LINES = LOCAL_BINS * 2 * SUBWIN
EDGE = 128

f32 = jnp.float32
bf16 = jnp.bfloat16
NT = (((1,), (1,)), ((), ()))


def quarter_table():
    bins = np.arange(BINS)[:, None] + FIRST_BIN
    phase = (bins * np.arange(SLICE)[None, :] % SAMPLES) * (2.0 * math.pi / SAMPLES)
    return np.concatenate([np.cos(phase), -np.sin(phase)]).astype(ml_dtypes.bfloat16)


def stage_kernel(x_ref, facing_ref, out_ref):
    out_ref[:, :SLICE] = x_ref[...]
    out_ref[:, SLICE:] = jnp.zeros((ROWS, EDGE), bf16)
    odd = lax.axis_index("tm") % 2 == 1

    @pl.when(odd)
    def _():
        facing_ref[...] = x_ref[:, SLICE - EDGE :]

    @pl.when(jnp.logical_not(odd))
    def _():
        facing_ref[...] = x_ref[:, :EDGE]


def join_kernel(edges_ref, _, out_ref, sem):
    other = lax.axis_index("tm") % 2
    copy = pltpu.make_async_copy(edges_ref.at[other], out_ref.at[:, SLICE:], sem)
    copy.start()
    copy.wait()


def normalize(me, x, edge):
    quarter = ROWS // QUAD
    first, last = me == 0, me == SUBWIN - 1
    before = edge[:quarter].astype(f32) * jnp.where(first, 0.0, 1.0)
    after = edge[ROWS - quarter :].astype(f32) * jnp.where(last, 0.0, 1.0)
    left = jnp.concatenate([before.astype(bf16), x[: ROWS - quarter, SLICE - EDGE :]], axis=0)
    right = jnp.concatenate([x[quarter:, :EDGE], after.astype(bf16)], axis=0)
    mag = jnp.abs(jnp.concatenate([left, x, right], axis=1))
    step = 256
    span = step + 2 * EDGE
    k = lax.broadcasted_iota(jnp.int32, (span, step), 0)
    n = lax.broadcasted_iota(jnp.int32, (span, step), 1)
    band = jnp.where(jnp.abs(k - EDGE - n) <= HALF, 1.0, 0.0).astype(bf16)
    row = lax.broadcasted_iota(jnp.int32, (ROWS, step), 0)
    lane = lax.broadcasted_iota(jnp.int32, (ROWS, step), 1)
    blocks = []
    for j in range(SLICE // step):
        sums = jnp.dot(mag[:, j * step : j * step + span], band, preferred_element_type=f32)
        counts = 2 * HALF + 1.0
        if j == 0 or j == SLICE // step - 1:
            position = me * SAMPLES + (row // quarter) * SLICE + j * step + lane
            upper = jnp.minimum(position + HALF, TIME - 1)
            lower = jnp.maximum(position - HALF, 0)
            counts = (upper - lower + 1).astype(f32)
        values = x[:, j * step : (j + 1) * step].astype(f32)
        blocks.append((values / (sums / counts + EPS)).astype(bf16))
    return jnp.concatenate(blocks, axis=1)


def spectra_kernel(table_ref, x_ref, out_ref):
    y = normalize(lax.axis_index("tm") // QUAD, x_ref[:, :SLICE], x_ref[:, SLICE:])
    p = lax.dot_general(table_ref[...], y, NT, preferred_element_type=f32)
    re, im = p[:BINS], p[BINS:]
    f = lax.broadcasted_iota(jnp.int32, (BINS, 128), 0)
    lane = lax.broadcasted_iota(jnp.int32, (BINS, 128), 1)
    odd = (f & 1) == 1
    low = lane < PART
    u_re = jnp.where(odd, re[:, :128] - re[:, 128:], re[:, :128] + re[:, 128:])
    u_im = jnp.where(odd, im[:, :128] - im[:, 128:], im[:, :128] + im[:, 128:])
    sign = jnp.where((f & 3) < 2, 1.0, -1.0)
    v_re = sign * jnp.where(odd, u_im, u_re)
    v_im = sign * jnp.where(odd, -u_re, u_im)
    raw = jnp.where(low, u_re, v_im) + pltpu.roll(jnp.where(low, u_im, v_re), PART, 1)
    for m in range(BINS // BAND):
        block = raw[m * BAND : (m + 1) * BAND]
        power = jnp.sum(block * block, axis=0, keepdims=True)
        power = jnp.broadcast_to(power, (8, 128))
        power = power + pltpu.roll(power, PART, 1)
        level = jnp.sqrt(power / BAND + EPS)
        out_ref[m * BAND : (m + 1) * BAND] = (block / level[:1]).astype(bf16)


def arrange_kernel(x_ref, out_ref):
    o = lax.broadcasted_iota(jnp.int32, (BINS, BINS), 0)
    i = lax.broadcasted_iota(jnp.int32, (BINS, BINS), 1)
    per = LOCAL_BINS * SUBWIN
    source = (o % SUBWIN) * (QUAD * LOCAL_BINS) + (o // per) * LOCAL_BINS + (o % per) // SUBWIN
    pick = jnp.where(i == source, 1.0, 0.0).astype(bf16)
    z = jnp.dot(pick, x_ref[...], preferred_element_type=f32)
    low = lax.broadcasted_iota(jnp.int32, (per, 128), 1) < PART
    for h in range(QUAD // 2):
        first = z[2 * h * per : (2 * h + 1) * per]
        second = z[(2 * h + 1) * per : (2 * h + 2) * per]
        real = jnp.where(low, first, pltpu.roll(second, PART, 1))
        imag = jnp.where(low, pltpu.roll(first, PART, 1), second)
        lines = []
        for e in range(LOCAL_BINS):
            lines += [part[e * SUBWIN : (e + 1) * SUBWIN] for part in (real, imag)]
        stations = jnp.concatenate(lines, axis=0).T.astype(bf16)
        out_ref[h * 128 : (h + 1) * 128] = stations[:, :128]
        out_ref[ROWS:, h * 64 : (h + 1) * 64] = stations[:, 128:]


def correlate_kernel(
    list_any,
    order_any,
    s_ref,
    out_hbm,
    main_ref,
    tail_ref,
    gm_ref,
    gt_ref,
    out_ref,
    order_ref,
    order_sem,
    list_ref,
    list_sem,
    sems,
):
    order_copy = pltpu.make_async_copy(order_any, order_ref, order_sem)
    order_copy.start()
    list_copy = pltpu.make_async_copy(list_any, list_ref, list_sem)
    list_copy.start()
    for n in range(N_OWNER):
        block = s_ref[n * BINS : (n + 1) * BINS].astype(f32)
        main_ref[n * ROWS : (n + 1) * ROWS] = block[:ROWS]
        tail_ref[n * ROWS : n * ROWS + 128] = block[ROWS:]
        tail_ref[n * ROWS + 128 : (n + 1) * ROWS] = pltpu.roll(block[ROWS:], 64, 1)

    order_copy.wait()
    list_copy.wait()
    rights = SLOTS * 2 * GSIZE
    sub = lax.broadcasted_iota(jnp.int32, (8, 128), 0)
    for b in range(SLOTS):
        base = jnp.maximum(list_ref[0, b], 0) * GSIZE
        base_right = jnp.maximum(list_ref[1, b], 0) * GSIZE
        for i in range(0, GSIZE, 8):
            ids = [order_ref[base + i + u] for u in range(8)]
            ids_right = [order_ref[base_right + i + u] for u in range(8)]
            for source, g_ref in ((main_ref, gm_ref), (tail_ref, gt_ref)):
                rows = [source[pl.ds(station, 8, stride=0), :] for station in ids]
                for parity in range(2):
                    at = b * 2 * GSIZE + parity * GSIZE + i
                    low = jnp.where(sub < 2, rows[parity], rows[2 + parity])
                    high = jnp.where(sub < 6, rows[4 + parity], rows[6 + parity])
                    g_ref[at : at + 8, :] = jnp.where(sub < 4, low, high)
                rows = [source[pl.ds(station, 8, stride=0), :] for station in ids_right]
                pairs = [jnp.where(sub % 2 == 0, rows[u], rows[u + 1]) for u in range(0, 8, 2)]
                low = jnp.where(sub < 2, pairs[0], pairs[1])
                high = jnp.where(sub < 6, pairs[2], pairs[3])
                at = rights + b * GSIZE + i
                g_ref[at : at + 8, :] = jnp.where(sub < 4, low, high)

    k = lax.broadcasted_iota(jnp.int32, (128, 128), 0)
    n = lax.broadcasted_iota(jnp.int32, (128, 128), 1)
    turn = jnp.where(k == (n ^ SUBWIN), jnp.where((n & SUBWIN) == 0, -1.0, 1.0), 0.0).astype(bf16)
    imag_row = (lax.broadcasted_iota(jnp.int32, (rights, 128), 0) & 1) == 1
    lefts = []
    for g_ref in (gm_ref, gt_ref):
        plain = g_ref[:rights]
        turned = jnp.dot(plain.astype(bf16), turn, preferred_element_type=f32)
        lefts.append(jnp.where(imag_row, turned, plain).astype(bf16))
    bin_of = (lax.broadcasted_iota(jnp.int32, (GSIZE, 256), 1) & 127) // (2 * SUBWIN)
    keeps = [jnp.where(bin_of == e, 1.0, 0.0).astype(bf16) for e in range(4)]
    zero = jnp.zeros((GSIZE, 128), bf16)
    copies = []
    for b in range(SLOTS):
        scale = jnp.where(list_ref[0, b] >= 0, 1.0 / SUBWIN, 0.0)
        for a, g_ref, bin0, count in ((lefts[0], gm_ref, 0, 4), (lefts[1], gt_ref, 4, 2)):
            at = b * 2 * GSIZE
            lhs = jnp.concatenate(
                [a[at : at + GSIZE], a[at + GSIZE : at + 2 * GSIZE]], axis=1
            )
            lhs = jnp.concatenate([lhs * keep for keep in keeps[:count]], axis=0)
            r = g_ref[rights + b * GSIZE : rights + (b + 1) * GSIZE].astype(bf16)
            rhs = jnp.concatenate(
                [jnp.concatenate([r, zero], axis=1), jnp.concatenate([zero, r], axis=1)], axis=0
            )
            c = lax.dot_general(lhs, rhs, NT, preferred_element_type=f32) * scale
            for e in range(count):
                out_ref[b, bin0 + e] = c[e * GSIZE : (e + 1) * GSIZE].astype(bf16)
        copies.append(pltpu.make_async_copy(out_ref.at[b], out_hbm.at[b], sems.at[b]))
        copies[-1].start()
    for copy in copies:
        copy.wait()


def vmem():
    return pl.BlockSpec(memory_space=pltpu.VMEM)


PARAMS = pltpu.CompilerParams(vmem_limit_bytes=40 * 1024 * 1024)


def correlate(block_list, station_order, stations):
    return pl.pallas_call(
        correlate_kernel,
        out_shape=jax.ShapeDtypeStruct((SLOTS, LOCAL_BINS, GSIZE, 128), bf16),
        in_specs=[pl.BlockSpec(memory_space=pl.ANY), pl.BlockSpec(memory_space=pl.ANY), vmem()],
        out_specs=pl.BlockSpec(memory_space=pltpu.HBM),
        scratch_shapes=[
            pltpu.VMEM((RECEIVER_TOTAL, 128), f32),
            pltpu.VMEM((RECEIVER_TOTAL, 128), f32),
            pltpu.VMEM((SLOTS * 3 * GSIZE, 128), f32),
            pltpu.VMEM((SLOTS * 3 * GSIZE, 128), f32),
            pltpu.VMEM((SLOTS, LOCAL_BINS, GSIZE, 128), bf16),
            pltpu.SMEM((RECEIVER_TOTAL,), jnp.int32),
            pltpu.SemaphoreType.DMA(()),
            pltpu.SMEM((2, SLOTS), jnp.int32),
            pltpu.SemaphoreType.DMA(()),
            pltpu.SemaphoreType.DMA((SLOTS,)),
        ],
        compiler_params=PARAMS,
        name="correlate",
    )(block_list.T, station_order, stations)


def local(records, station_order, block_list):
    facing, staged = pl.pallas_call(
        stage_kernel,
        out_shape=[
            jax.ShapeDtypeStruct((ROWS, EDGE), bf16),
            jax.ShapeDtypeStruct((ROWS, SLICE + EDGE), bf16),
        ],
        in_specs=[vmem()],
        out_specs=[vmem()] * 2,
        compiler_params=PARAMS,
        name="stage",
    )(records)
    pairs = [[i, (i + 1) % N_TIME] for i in range(1, N_TIME, 2)]
    edges = lax.all_gather(facing, "tm", axis_index_groups=pairs)
    extended = pl.pallas_call(
        join_kernel,
        out_shape=jax.ShapeDtypeStruct((ROWS, SLICE + EDGE), bf16),
        in_specs=[pl.BlockSpec(memory_space=pl.ANY)] * 2,
        out_specs=pl.BlockSpec(memory_space=pl.ANY),
        scratch_shapes=[pltpu.SemaphoreType.DMA(())],
        input_output_aliases={1: 0},
        compiler_params=PARAMS,
        name="join",
    )(edges, staged)
    quads = [[QUAD * g + i for i in range(QUAD)] for g in range(N_TIME // QUAD)]
    windows = lax.all_to_all(
        extended.reshape(QUAD, PART, SLICE + EDGE), "tm", 0, 0, axis_index_groups=quads, tiled=True
    ).reshape(ROWS, SLICE + EDGE)
    spectra = pl.pallas_call(
        spectra_kernel,
        out_shape=jax.ShapeDtypeStruct((BINS, 2 * PART), bf16),
        in_specs=[vmem(), vmem()],
        out_specs=vmem(),
        compiler_params=PARAMS,
        name="spectra",
    )(jnp.asarray(quarter_table()), windows)
    by_bin = lax.all_to_all(
        spectra.reshape(N_TIME, LOCAL_BINS // 2, 2, 2 * PART), "tm", 0, 0, tiled=True
    ).reshape(BINS, 2 * PART)
    mine = pl.pallas_call(
        arrange_kernel,
        out_shape=jax.ShapeDtypeStruct((BINS, 128), bf16),
        in_specs=[vmem()],
        out_specs=vmem(),
        compiler_params=PARAMS,
        name="arrange",
    )(by_bin)
    stations = lax.all_gather(mine, "pairs", axis=0, tiled=True)
    out = correlate(block_list, station_order, stations)
    out = out.reshape(SLOTS, LOCAL_BINS, GSIZE // 2, 2, 128)
    return jnp.transpose(out, (0, 1, 3, 2, 4)).reshape(SLOTS, LOCAL_BINS, 2, GSIZE * GSIZE)


def solution(mesh):
    placed = (P("pairs", "tm"), P(), P("pairs", None))
    return jax.shard_map(
        local, mesh=mesh, in_specs=placed, out_specs=P("pairs", "tm", None, None), check_vma=False
    )
```

```python
import math

import jax
import jax.numpy as jnp
import ml_dtypes
import numpy as np
from jax import lax
from jax.experimental import pallas as pl
from jax.experimental.pallas import tpu as pltpu
from jax.sharding import PartitionSpec as P

RECEIVER_TOTAL = 2048
GSIZE = 64
GROUPS = 32
SUBWIN = 16
SAMPLES = 4096
TIME = 65536
BINS = 384
FIRST_BIN = 8
BAND = 64
HALF = 64
SLOTS = 10
EPS = 1e-06

N_TIME = 64
N_OWNER = 8
QUAD = 4
SLICE = TIME // N_TIME
ROWS = RECEIVER_TOTAL // N_OWNER
PART = ROWS // QUAD
LOCAL_BINS = BINS // N_TIME
LINES = LOCAL_BINS * 2 * SUBWIN
EDGE = 128

f32 = jnp.float32
bf16 = jnp.bfloat16
NT = (((1,), (1,)), ((), ()))


def quarter_table():
    bins = np.arange(BINS)[:, None] + FIRST_BIN
    phase = (bins * np.arange(SLICE)[None, :] % SAMPLES) * (2.0 * math.pi / SAMPLES)
    return np.concatenate([np.cos(phase), -np.sin(phase)]).astype(ml_dtypes.bfloat16)


TILES = SLICE // 128
BODY = TILES * PART
PACKED = PART // 2


def stage_kernel(x_ref, facing_ref, out_ref):
    low = lax.broadcasted_iota(jnp.int32, (PACKED, 128), 1) < HALF

    def pack(column, first_half):
        edge = x_ref[:, column : column + 128].astype(f32)
        for q in range(QUAD):
            a = edge[q * PART : q * PART + PACKED]
            b = edge[q * PART + PACKED : (q + 1) * PART]
            if first_half:
                b = pltpu.roll(b, HALF, 1)
            else:
                a = pltpu.roll(a, HALF, 1)
            facing_ref[q * PACKED : (q + 1) * PACKED] = jnp.where(low, a, b).astype(bf16)

    odd = lax.axis_index("tm") % 2 == 1

    @pl.when(odd)
    def _():
        pack(SLICE - 128, False)

    @pl.when(jnp.logical_not(odd))
    def _():
        pack(0, True)

    for q in range(QUAD):
        for c in range(TILES):
            out_ref[q, c * PART : (c + 1) * PART] = x_ref[
                q * PART : (q + 1) * PART, c * 128 : (c + 1) * 128
            ]
        out_ref[q, BODY:] = jnp.zeros((PACKED, 128), bf16)


def join_kernel(edges_ref, _, out_ref, sems):
    other = lax.axis_index("tm") % 2
    copies = [
        pltpu.make_async_copy(
            edges_ref.at[other, q * PACKED : (q + 1) * PACKED], out_ref.at[q, BODY:], sems.at[q]
        )
        for q in range(QUAD)
    ]
    for copy in copies:
        copy.start()
    for copy in copies:
        copy.wait()


def normalize(me, x, edge_before, edge_after):
    before = edge_before.astype(f32) * jnp.where(me == 0, 0.0, 1.0)
    after = edge_after.astype(f32) * jnp.where(me == SUBWIN - 1, 0.0, 1.0)
    before = jnp.concatenate([pltpu.roll(before, HALF, 1), before], axis=0).astype(bf16)
    after = jnp.concatenate([after, pltpu.roll(after, HALF, 1)], axis=0).astype(bf16)
    left = jnp.concatenate([before, x[: ROWS - PART, SLICE - EDGE :]], axis=0)
    right = jnp.concatenate([x[PART:, :EDGE], after], axis=0)
    mag = jnp.abs(jnp.concatenate([left, x, right], axis=1))
    step = 256
    span = step + 2 * EDGE
    k = lax.broadcasted_iota(jnp.int32, (span, step), 0)
    n = lax.broadcasted_iota(jnp.int32, (span, step), 1)
    band = jnp.where(jnp.abs(k - EDGE - n) <= HALF, 1.0, 0.0).astype(bf16)
    row = lax.broadcasted_iota(jnp.int32, (ROWS, step), 0)
    lane = lax.broadcasted_iota(jnp.int32, (ROWS, step), 1)
    blocks = []
    for j in range(SLICE // step):
        sums = jnp.dot(mag[:, j * step : j * step + span], band, preferred_element_type=f32)
        counts = 2 * HALF + 1.0
        if j == 0 or j == SLICE // step - 1:
            position = me * SAMPLES + (row // PART) * SLICE + j * step + lane
            upper = jnp.minimum(position + HALF, TIME - 1)
            lower = jnp.maximum(position - HALF, 0)
            counts = (upper - lower + 1).astype(f32)
        values = x[:, j * step : (j + 1) * step].astype(f32)
        blocks.append((values * counts / (sums + EPS * counts)).astype(bf16))
    return jnp.concatenate(blocks, axis=1)


def spectra_kernel(table_ref, x_ref, out_ref):
    columns = [
        jnp.concatenate([x_ref[q, c * PART : (c + 1) * PART] for q in range(QUAD)], axis=0)
        for c in range(TILES)
    ]
    x = jnp.concatenate(columns, axis=1)
    y = normalize(lax.axis_index("tm") // QUAD, x, x_ref[0, BODY:], x_ref[QUAD - 1, BODY:])
    p = lax.dot_general(table_ref[...], y, NT, preferred_element_type=f32)
    re, im = p[:BINS], p[BINS:]
    f = lax.broadcasted_iota(jnp.int32, (BINS, 128), 0)
    lane = lax.broadcasted_iota(jnp.int32, (BINS, 128), 1)
    odd = (f & 1) == 1
    low = lane < PART
    u_re = jnp.where(odd, re[:, :128] - re[:, 128:], re[:, :128] + re[:, 128:])
    u_im = jnp.where(odd, im[:, :128] - im[:, 128:], im[:, :128] + im[:, 128:])
    sign = jnp.where((f & 3) < 2, 1.0, -1.0)
    v_re = sign * jnp.where(odd, u_im, u_re)
    v_im = sign * jnp.where(odd, -u_re, u_im)
    raw = jnp.where(low, u_re, v_im) + pltpu.roll(jnp.where(low, u_im, v_re), PART, 1)
    for m in range(BINS // BAND):
        block = raw[m * BAND : (m + 1) * BAND]
        power = jnp.sum(block * block, axis=0, keepdims=True)
        power = jnp.broadcast_to(power, (8, 128))
        power = power + pltpu.roll(power, PART, 1)
        level = jnp.sqrt(power / BAND + EPS)
        out_ref[m * BAND : (m + 1) * BAND] = (block / level[:1]).astype(bf16)


def bin_rows():
    rows = np.arange(BINS).reshape(SUBWIN, QUAD, LOCAL_BINS).transpose(1, 2, 0).reshape(-1)
    return (np.arange(BINS)[None, :] == rows[:, None]).astype(ml_dtypes.bfloat16)


def arrange_kernel(pick_ref, x_ref, out_ref):
    per = LOCAL_BINS * SUBWIN
    z = jnp.dot(pick_ref[...], x_ref[...], preferred_element_type=f32)
    low = lax.broadcasted_iota(jnp.int32, (per, 128), 1) < PART
    for h in range(QUAD // 2):
        first = z[2 * h * per : (2 * h + 1) * per]
        second = z[(2 * h + 1) * per : (2 * h + 2) * per]
        real = jnp.where(low, first, pltpu.roll(second, PART, 1))
        imag = jnp.where(low, pltpu.roll(first, PART, 1), second)
        lines = []
        for e in range(LOCAL_BINS):
            lines += [part[e * SUBWIN : (e + 1) * SUBWIN] for part in (real, imag)]
        stations = jnp.concatenate(lines, axis=0).T.astype(bf16)
        out_ref[h * 128 : (h + 1) * 128] = stations[:, :128]
        out_ref[ROWS:, h * 64 : (h + 1) * 64] = stations[:, 128:]


def correlate_kernel(
    list_any,
    order_any,
    s_ref,
    out_hbm,
    main_ref,
    tail_ref,
    gm_ref,
    gt_ref,
    out_ref,
    order_ref,
    order_sem,
    list_ref,
    list_sem,
    sems,
):
    order_copy = pltpu.make_async_copy(order_any, order_ref, order_sem)
    order_copy.start()
    list_copy = pltpu.make_async_copy(list_any, list_ref, list_sem)
    list_copy.start()
    for n in range(N_OWNER):
        block = s_ref[n * BINS : (n + 1) * BINS].astype(f32)
        main_ref[n * ROWS : (n + 1) * ROWS] = block[:ROWS]
        tail_ref[n * ROWS : n * ROWS + 128] = block[ROWS:]
        tail_ref[n * ROWS + 128 : (n + 1) * ROWS] = pltpu.roll(block[ROWS:], 64, 1)

    order_copy.wait()
    list_copy.wait()
    rights = SLOTS * 2 * GSIZE
    sub = lax.broadcasted_iota(jnp.int32, (8, 128), 0)
    for b in range(SLOTS):
        base = jnp.maximum(list_ref[0, b], 0) * GSIZE
        base_right = jnp.maximum(list_ref[1, b], 0) * GSIZE
        for i in range(0, GSIZE, 8):
            ids = [order_ref[base + i + u] for u in range(8)]
            ids_right = [order_ref[base_right + i + u] for u in range(8)]
            for source, g_ref in ((main_ref, gm_ref), (tail_ref, gt_ref)):
                rows = [source[pl.ds(station, 8, stride=0), :] for station in ids]
                for parity in range(2):
                    at = b * 2 * GSIZE + parity * GSIZE + i
                    low = jnp.where(sub < 2, rows[parity], rows[2 + parity])
                    high = jnp.where(sub < 6, rows[4 + parity], rows[6 + parity])
                    g_ref[at : at + 8, :] = jnp.where(sub < 4, low, high)
                rows = [source[pl.ds(station, 8, stride=0), :] for station in ids_right]
                pairs = [jnp.where(sub % 2 == 0, rows[u], rows[u + 1]) for u in range(0, 8, 2)]
                low = jnp.where(sub < 2, pairs[0], pairs[1])
                high = jnp.where(sub < 6, pairs[2], pairs[3])
                at = rights + b * GSIZE + i
                g_ref[at : at + 8, :] = jnp.where(sub < 4, low, high)

    k = lax.broadcasted_iota(jnp.int32, (128, 128), 0)
    n = lax.broadcasted_iota(jnp.int32, (128, 128), 1)
    turn = jnp.where(k == (n ^ SUBWIN), jnp.where((n & SUBWIN) == 0, -1.0, 1.0), 0.0).astype(bf16)
    imag_row = (lax.broadcasted_iota(jnp.int32, (rights, 128), 0) & 1) == 1
    lefts = []
    for g_ref in (gm_ref, gt_ref):
        plain = g_ref[:rights]
        turned = jnp.dot(plain.astype(bf16), turn, preferred_element_type=f32)
        lefts.append(jnp.where(imag_row, turned, plain).astype(bf16))
    bin_of = (lax.broadcasted_iota(jnp.int32, (GSIZE, 256), 1) & 127) // (2 * SUBWIN)
    keeps = [jnp.where(bin_of == e, 1.0, 0.0).astype(bf16) for e in range(4)]
    zero = jnp.zeros((GSIZE, 128), bf16)
    copies = []
    for b in range(SLOTS):
        scale = jnp.where(list_ref[0, b] >= 0, 1.0 / SUBWIN, 0.0)
        for a, g_ref, bin0, count in ((lefts[0], gm_ref, 0, 4), (lefts[1], gt_ref, 4, 2)):
            at = b * 2 * GSIZE
            lhs = jnp.concatenate(
                [a[at : at + GSIZE], a[at + GSIZE : at + 2 * GSIZE]], axis=1
            )
            lhs = jnp.concatenate([lhs * keep for keep in keeps[:count]], axis=0)
            r = g_ref[rights + b * GSIZE : rights + (b + 1) * GSIZE].astype(bf16)
            rhs = jnp.concatenate(
                [jnp.concatenate([r, zero], axis=1), jnp.concatenate([zero, r], axis=1)], axis=0
            )
            c = lax.dot_general(lhs, rhs, NT, preferred_element_type=f32) * scale
            for e in range(count):
                out_ref[b, bin0 + e] = c[e * GSIZE : (e + 1) * GSIZE].astype(bf16)
        copies.append(pltpu.make_async_copy(out_ref.at[b], out_hbm.at[b], sems.at[b]))
        copies[-1].start()
    for copy in copies:
        copy.wait()


def vmem():
    return pl.BlockSpec(memory_space=pltpu.VMEM)


PARAMS = pltpu.CompilerParams(vmem_limit_bytes=40 * 1024 * 1024)


def correlate(block_list, station_order, stations):
    return pl.pallas_call(
        correlate_kernel,
        out_shape=jax.ShapeDtypeStruct((SLOTS, LOCAL_BINS, GSIZE, 128), bf16),
        in_specs=[pl.BlockSpec(memory_space=pl.ANY), pl.BlockSpec(memory_space=pl.ANY), vmem()],
        out_specs=pl.BlockSpec(memory_space=pltpu.HBM),
        scratch_shapes=[
            pltpu.VMEM((RECEIVER_TOTAL, 128), f32),
            pltpu.VMEM((RECEIVER_TOTAL, 128), f32),
            pltpu.VMEM((SLOTS * 3 * GSIZE, 128), f32),
            pltpu.VMEM((SLOTS * 3 * GSIZE, 128), f32),
            pltpu.VMEM((SLOTS, LOCAL_BINS, GSIZE, 128), bf16),
            pltpu.SMEM((RECEIVER_TOTAL,), jnp.int32),
            pltpu.SemaphoreType.DMA(()),
            pltpu.SMEM((2, SLOTS), jnp.int32),
            pltpu.SemaphoreType.DMA(()),
            pltpu.SemaphoreType.DMA((SLOTS,)),
        ],
        compiler_params=PARAMS,
        name="correlate",
    )(block_list.T, station_order, stations)


def local(records, station_order, block_list):
    facing, staged = pl.pallas_call(
        stage_kernel,
        out_shape=[
            jax.ShapeDtypeStruct((QUAD * PACKED, 128), bf16),
            jax.ShapeDtypeStruct((QUAD, BODY + PACKED, 128), bf16),
        ],
        in_specs=[vmem()],
        out_specs=[vmem()] * 2,
        compiler_params=PARAMS,
        name="stage",
    )(records)
    pairs = [[i, (i + 1) % N_TIME] for i in range(1, N_TIME, 2)]
    edges = lax.all_gather(facing, "tm", axis_index_groups=pairs)
    extended = pl.pallas_call(
        join_kernel,
        out_shape=jax.ShapeDtypeStruct((QUAD, BODY + PACKED, 128), bf16),
        in_specs=[pl.BlockSpec(memory_space=pl.ANY)] * 2,
        out_specs=pl.BlockSpec(memory_space=pl.ANY),
        scratch_shapes=[pltpu.SemaphoreType.DMA((QUAD,))],
        input_output_aliases={1: 0},
        compiler_params=PARAMS,
        name="join",
    )(edges, staged)
    quads = [[QUAD * g + i for i in range(QUAD)] for g in range(N_TIME // QUAD)]
    windows = lax.all_to_all(extended, "tm", 0, 0, axis_index_groups=quads, tiled=True)
    spectra = pl.pallas_call(
        spectra_kernel,
        out_shape=jax.ShapeDtypeStruct((BINS, 2 * PART), bf16),
        in_specs=[vmem(), vmem()],
        out_specs=vmem(),
        compiler_params=PARAMS,
        name="spectra",
    )(jnp.asarray(quarter_table()), windows)
    by_bin = lax.all_to_all(
        spectra.reshape(N_TIME, LOCAL_BINS // 2, 2, 2 * PART), "tm", 0, 0, tiled=True
    ).reshape(BINS, 2 * PART)
    mine = pl.pallas_call(
        arrange_kernel,
        out_shape=jax.ShapeDtypeStruct((BINS, 128), bf16),
        in_specs=[vmem()] * 2,
        out_specs=vmem(),
        compiler_params=PARAMS,
        name="arrange",
    )(jnp.asarray(bin_rows()), by_bin)
    stations = lax.all_gather(mine, "pairs", axis=0, tiled=True)
    out = correlate(block_list, station_order, stations)
    out = out.reshape(SLOTS, LOCAL_BINS, GSIZE // 2, 2, 128)
    return jnp.transpose(out, (0, 1, 3, 2, 4)).reshape(SLOTS, LOCAL_BINS, 2, GSIZE * GSIZE)


def solution(mesh):
    placed = (P("pairs", "tm"), P(), P("pairs", None))
    return jax.shard_map(
        local, mesh=mesh, in_specs=placed, out_specs=P("pairs", "tm", None, None), check_vma=False
    )
```

```python
import math

import jax
import jax.numpy as jnp
import ml_dtypes
import numpy as np
from jax import lax
from jax.experimental import pallas as pl
from jax.experimental.pallas import tpu as pltpu
from jax.sharding import PartitionSpec as P

RECEIVER_TOTAL = 2048
GSIZE = 64
GROUPS = 32
SUBWIN = 16
SAMPLES = 4096
TIME = 65536
BINS = 384
FIRST_BIN = 8
BAND = 64
HALF = 64
SLOTS = 10
EPS = 1e-06

N_TIME = 64
N_OWNER = 8
QUAD = 4
SLICE = TIME // N_TIME
ROWS = RECEIVER_TOTAL // N_OWNER
PART = ROWS // QUAD
LOCAL_BINS = BINS // N_TIME
LINES = LOCAL_BINS * 2 * SUBWIN
EDGE = 128

f32 = jnp.float32
bf16 = jnp.bfloat16
NT = (((1,), (1,)), ((), ()))


def quarter_table():
    bins = np.arange(BINS)[:, None] + FIRST_BIN
    phase = (bins * np.arange(SLICE)[None, :] % SAMPLES) * (2.0 * math.pi / SAMPLES)
    return np.concatenate([np.cos(phase), -np.sin(phase)]).astype(ml_dtypes.bfloat16)


TILES = SLICE // 128
BODY = TILES * PART
PACKED = PART // 2


def stage_kernel(x_hbm, facing_ref, out_ref, sems):
    low = lax.broadcasted_iota(jnp.int32, (PACKED, 128), 1) < HALF
    copies = [
        pltpu.make_async_copy(
            x_hbm.at[:, :, c * 128 : (c + 1) * 128],
            out_ref.at[:, c * PART : (c + 1) * PART],
            sems.at[c],
        )
        for c in range(TILES)
    ]
    order = [0, TILES - 1] + list(range(1, TILES - 1))
    for c in order:
        copies[c].start()
    for q in range(QUAD):
        out_ref[q, BODY:] = jnp.zeros((PACKED, 128), bf16)
    copies[0].wait()
    copies[TILES - 1].wait()

    def pack(column, first_half):
        for q in range(QUAD):
            edge = out_ref[q, column * PART : (column + 1) * PART].astype(f32)
            a, b = edge[:PACKED], edge[PACKED:]
            if first_half:
                b = pltpu.roll(b, HALF, 1)
            else:
                a = pltpu.roll(a, HALF, 1)
            facing_ref[q * PACKED : (q + 1) * PACKED] = jnp.where(low, a, b).astype(bf16)

    odd = lax.axis_index("tm") % 2 == 1

    @pl.when(odd)
    def _():
        pack(TILES - 1, False)

    @pl.when(jnp.logical_not(odd))
    def _():
        pack(0, True)

    for c in order[2:]:
        copies[c].wait()


def join_kernel(edges_ref, _, out_ref, sems):
    other = lax.axis_index("tm") % 2
    copies = [
        pltpu.make_async_copy(
            edges_ref.at[other, q * PACKED : (q + 1) * PACKED], out_ref.at[q, BODY:], sems.at[q]
        )
        for q in range(QUAD)
    ]
    for copy in copies:
        copy.start()
    for copy in copies:
        copy.wait()


def normalize(me, x, edge_before, edge_after):
    before = edge_before.astype(f32) * jnp.where(me == 0, 0.0, 1.0)
    after = edge_after.astype(f32) * jnp.where(me == SUBWIN - 1, 0.0, 1.0)
    before = jnp.concatenate([pltpu.roll(before, HALF, 1), before], axis=0).astype(bf16)
    after = jnp.concatenate([after, pltpu.roll(after, HALF, 1)], axis=0).astype(bf16)
    left = jnp.concatenate([before, x[: ROWS - PART, SLICE - EDGE :]], axis=0)
    right = jnp.concatenate([x[PART:, :EDGE], after], axis=0)
    mag = jnp.abs(jnp.concatenate([left, x, right], axis=1))
    step = 256
    span = step + 2 * EDGE
    k = lax.broadcasted_iota(jnp.int32, (span, step), 0)
    n = lax.broadcasted_iota(jnp.int32, (span, step), 1)
    band = jnp.where(jnp.abs(k - EDGE - n) <= HALF, 1.0, 0.0).astype(bf16)
    row = lax.broadcasted_iota(jnp.int32, (ROWS, step), 0)
    lane = lax.broadcasted_iota(jnp.int32, (ROWS, step), 1)
    blocks = []
    for j in range(SLICE // step):
        sums = jnp.dot(mag[:, j * step : j * step + span], band, preferred_element_type=f32)
        counts = 2 * HALF + 1.0
        if j == 0 or j == SLICE // step - 1:
            position = me * SAMPLES + (row // PART) * SLICE + j * step + lane
            upper = jnp.minimum(position + HALF, TIME - 1)
            lower = jnp.maximum(position - HALF, 0)
            counts = (upper - lower + 1).astype(f32)
        values = x[:, j * step : (j + 1) * step].astype(f32)
        blocks.append((values * counts / (sums + EPS * counts)).astype(bf16))
    return jnp.concatenate(blocks, axis=1)


def spectra_kernel(table_ref, x_ref, out_ref):
    columns = [
        jnp.concatenate([x_ref[q, c * PART : (c + 1) * PART] for q in range(QUAD)], axis=0)
        for c in range(TILES)
    ]
    x = jnp.concatenate(columns, axis=1)
    y = normalize(lax.axis_index("tm") // QUAD, x, x_ref[0, BODY:], x_ref[QUAD - 1, BODY:])
    p = lax.dot_general(table_ref[...], y, NT, preferred_element_type=f32)
    re, im = p[:BINS], p[BINS:]
    f = lax.broadcasted_iota(jnp.int32, (BINS, 128), 0)
    lane = lax.broadcasted_iota(jnp.int32, (BINS, 128), 1)
    odd = (f & 1) == 1
    low = lane < PART
    u_re = jnp.where(odd, re[:, :128] - re[:, 128:], re[:, :128] + re[:, 128:])
    u_im = jnp.where(odd, im[:, :128] - im[:, 128:], im[:, :128] + im[:, 128:])
    sign = jnp.where((f & 3) < 2, 1.0, -1.0)
    v_re = sign * jnp.where(odd, u_im, u_re)
    v_im = sign * jnp.where(odd, -u_re, u_im)
    raw = jnp.where(low, u_re, v_im) + pltpu.roll(jnp.where(low, u_im, v_re), PART, 1)
    for m in range(BINS // BAND):
        block = raw[m * BAND : (m + 1) * BAND]
        power = jnp.sum(block * block, axis=0, keepdims=True)
        power = jnp.broadcast_to(power, (8, 128))
        power = power + pltpu.roll(power, PART, 1)
        level = jnp.sqrt(power / BAND + EPS)
        out_ref[m * BAND : (m + 1) * BAND] = (block / level[:1]).astype(bf16)


def bin_rows():
    rows = np.arange(BINS).reshape(SUBWIN, QUAD, LOCAL_BINS).transpose(1, 2, 0).reshape(-1)
    return (np.arange(BINS)[None, :] == rows[:, None]).astype(ml_dtypes.bfloat16)


def arrange_kernel(pick_ref, x_ref, out_ref):
    per = LOCAL_BINS * SUBWIN
    z = jnp.dot(pick_ref[...], x_ref[...], preferred_element_type=f32)
    low = lax.broadcasted_iota(jnp.int32, (per, 128), 1) < PART
    for h in range(QUAD // 2):
        first = z[2 * h * per : (2 * h + 1) * per]
        second = z[(2 * h + 1) * per : (2 * h + 2) * per]
        real = jnp.where(low, first, pltpu.roll(second, PART, 1))
        imag = jnp.where(low, pltpu.roll(first, PART, 1), second)
        lines = []
        for e in range(LOCAL_BINS):
            lines += [part[e * SUBWIN : (e + 1) * SUBWIN] for part in (real, imag)]
        stations = jnp.concatenate(lines, axis=0).T.astype(bf16)
        out_ref[h * 128 : (h + 1) * 128] = stations[:, :128]
        out_ref[ROWS:, h * 64 : (h + 1) * 64] = stations[:, 128:]


def correlate_kernel(
    list_any,
    order_any,
    s_ref,
    out_hbm,
    main_ref,
    tail_ref,
    gm_ref,
    gt_ref,
    out_ref,
    order_ref,
    order_sem,
    list_ref,
    list_sem,
    sems,
):
    order_copy = pltpu.make_async_copy(order_any, order_ref, order_sem)
    order_copy.start()
    list_copy = pltpu.make_async_copy(list_any, list_ref, list_sem)
    list_copy.start()
    for n in range(N_OWNER):
        block = s_ref[n * BINS : (n + 1) * BINS].astype(f32)
        main_ref[n * ROWS : (n + 1) * ROWS] = block[:ROWS]
        tail_ref[n * ROWS : n * ROWS + 128] = block[ROWS:]
        tail_ref[n * ROWS + 128 : (n + 1) * ROWS] = pltpu.roll(block[ROWS:], 64, 1)

    order_copy.wait()
    list_copy.wait()
    rights = SLOTS * 2 * GSIZE
    sub = lax.broadcasted_iota(jnp.int32, (8, 128), 0)
    for b in range(SLOTS):
        base = jnp.maximum(list_ref[0, b], 0) * GSIZE
        base_right = jnp.maximum(list_ref[1, b], 0) * GSIZE
        for i in range(0, GSIZE, 8):
            ids = [order_ref[base + i + u] for u in range(8)]
            ids_right = [order_ref[base_right + i + u] for u in range(8)]
            for source, g_ref in ((main_ref, gm_ref), (tail_ref, gt_ref)):
                rows = [source[pl.ds(station, 8, stride=0), :] for station in ids]
                for parity in range(2):
                    at = b * 2 * GSIZE + parity * GSIZE + i
                    low = jnp.where(sub < 2, rows[parity], rows[2 + parity])
                    high = jnp.where(sub < 6, rows[4 + parity], rows[6 + parity])
                    g_ref[at : at + 8, :] = jnp.where(sub < 4, low, high)
                rows = [source[pl.ds(station, 8, stride=0), :] for station in ids_right]
                pairs = [jnp.where(sub % 2 == 0, rows[u], rows[u + 1]) for u in range(0, 8, 2)]
                low = jnp.where(sub < 2, pairs[0], pairs[1])
                high = jnp.where(sub < 6, pairs[2], pairs[3])
                at = rights + b * GSIZE + i
                g_ref[at : at + 8, :] = jnp.where(sub < 4, low, high)

    k = lax.broadcasted_iota(jnp.int32, (128, 128), 0)
    n = lax.broadcasted_iota(jnp.int32, (128, 128), 1)
    turn = jnp.where(k == (n ^ SUBWIN), jnp.where((n & SUBWIN) == 0, -1.0, 1.0), 0.0).astype(bf16)
    imag_row = (lax.broadcasted_iota(jnp.int32, (rights, 128), 0) & 1) == 1
    lefts = []
    for g_ref in (gm_ref, gt_ref):
        plain = g_ref[:rights]
        turned = jnp.dot(plain.astype(bf16), turn, preferred_element_type=f32)
        lefts.append(jnp.where(imag_row, turned, plain).astype(bf16))
    bin_of = (lax.broadcasted_iota(jnp.int32, (GSIZE, 256), 1) & 127) // (2 * SUBWIN)
    keeps = [jnp.where(bin_of == e, 1.0, 0.0).astype(bf16) for e in range(4)]
    zero = jnp.zeros((GSIZE, 128), bf16)
    copies = []
    for b in range(SLOTS):
        scale = jnp.where(list_ref[0, b] >= 0, 1.0 / SUBWIN, 0.0)
        for a, g_ref, bin0, count in ((lefts[0], gm_ref, 0, 4), (lefts[1], gt_ref, 4, 2)):
            at = b * 2 * GSIZE
            lhs = jnp.concatenate(
                [a[at : at + GSIZE], a[at + GSIZE : at + 2 * GSIZE]], axis=1
            )
            lhs = jnp.concatenate([lhs * keep for keep in keeps[:count]], axis=0)
            r = g_ref[rights + b * GSIZE : rights + (b + 1) * GSIZE].astype(bf16)
            rhs = jnp.concatenate(
                [jnp.concatenate([r, zero], axis=1), jnp.concatenate([zero, r], axis=1)], axis=0
            )
            c = lax.dot_general(lhs, rhs, NT, preferred_element_type=f32) * scale
            for e in range(count):
                out_ref[b, bin0 + e] = c[e * GSIZE : (e + 1) * GSIZE].astype(bf16)
        copies.append(pltpu.make_async_copy(out_ref.at[b], out_hbm.at[b], sems.at[b]))
        copies[-1].start()
    for copy in copies:
        copy.wait()


def vmem():
    return pl.BlockSpec(memory_space=pltpu.VMEM)


PARAMS = pltpu.CompilerParams(vmem_limit_bytes=40 * 1024 * 1024)


def correlate(block_list, station_order, stations):
    return pl.pallas_call(
        correlate_kernel,
        out_shape=jax.ShapeDtypeStruct((SLOTS, LOCAL_BINS, GSIZE, 128), bf16),
        in_specs=[pl.BlockSpec(memory_space=pl.ANY), pl.BlockSpec(memory_space=pl.ANY), vmem()],
        out_specs=pl.BlockSpec(memory_space=pltpu.HBM),
        scratch_shapes=[
            pltpu.VMEM((RECEIVER_TOTAL, 128), f32),
            pltpu.VMEM((RECEIVER_TOTAL, 128), f32),
            pltpu.VMEM((SLOTS * 3 * GSIZE, 128), f32),
            pltpu.VMEM((SLOTS * 3 * GSIZE, 128), f32),
            pltpu.VMEM((SLOTS, LOCAL_BINS, GSIZE, 128), bf16),
            pltpu.SMEM((RECEIVER_TOTAL,), jnp.int32),
            pltpu.SemaphoreType.DMA(()),
            pltpu.SMEM((2, SLOTS), jnp.int32),
            pltpu.SemaphoreType.DMA(()),
            pltpu.SemaphoreType.DMA((SLOTS,)),
        ],
        compiler_params=PARAMS,
        name="correlate",
    )(block_list.T, station_order, stations)


def local(records, station_order, block_list):
    facing, staged = pl.pallas_call(
        stage_kernel,
        out_shape=[
            jax.ShapeDtypeStruct((QUAD * PACKED, 128), bf16),
            jax.ShapeDtypeStruct((QUAD, BODY + PACKED, 128), bf16),
        ],
        in_specs=[pl.BlockSpec(memory_space=pltpu.HBM)],
        out_specs=[vmem()] * 2,
        scratch_shapes=[pltpu.SemaphoreType.DMA((TILES,))],
        compiler_params=PARAMS,
        name="stage",
    )(pltpu.with_memory_space_constraint(records.reshape(QUAD, PART, SLICE), pltpu.HBM))
    pairs = [[i, (i + 1) % N_TIME] for i in range(1, N_TIME, 2)]
    edges = lax.all_gather(facing, "tm", axis_index_groups=pairs)
    extended = pl.pallas_call(
        join_kernel,
        out_shape=jax.ShapeDtypeStruct((QUAD, BODY + PACKED, 128), bf16),
        in_specs=[pl.BlockSpec(memory_space=pl.ANY)] * 2,
        out_specs=pl.BlockSpec(memory_space=pl.ANY),
        scratch_shapes=[pltpu.SemaphoreType.DMA((QUAD,))],
        input_output_aliases={1: 0},
        compiler_params=PARAMS,
        name="join",
    )(edges, staged)
    quads = [[QUAD * g + i for i in range(QUAD)] for g in range(N_TIME // QUAD)]
    windows = lax.all_to_all(extended, "tm", 0, 0, axis_index_groups=quads, tiled=True)
    spectra = pl.pallas_call(
        spectra_kernel,
        out_shape=jax.ShapeDtypeStruct((BINS, 2 * PART), bf16),
        in_specs=[vmem(), vmem()],
        out_specs=vmem(),
        compiler_params=PARAMS,
        name="spectra",
    )(jnp.asarray(quarter_table()), windows)
    by_bin = lax.all_to_all(
        spectra.reshape(N_TIME, LOCAL_BINS // 2, 2, 2 * PART), "tm", 0, 0, tiled=True
    ).reshape(BINS, 2 * PART)
    mine = pl.pallas_call(
        arrange_kernel,
        out_shape=jax.ShapeDtypeStruct((BINS, 128), bf16),
        in_specs=[vmem()] * 2,
        out_specs=vmem(),
        compiler_params=PARAMS,
        name="arrange",
    )(jnp.asarray(bin_rows()), by_bin)
    stations = lax.all_gather(mine, "pairs", axis=0, tiled=True)
    out = correlate(block_list, station_order, stations)
    out = out.reshape(SLOTS, LOCAL_BINS, GSIZE // 2, 2, 128)
    return jnp.transpose(out, (0, 1, 3, 2, 4)).reshape(SLOTS, LOCAL_BINS, 2, GSIZE * GSIZE)


def solution(mesh):
    placed = (P("pairs", "tm"), P(), P("pairs", None))
    return jax.shard_map(
        local, mesh=mesh, in_specs=placed, out_specs=P("pairs", "tm", None, None), check_vma=False
    )
```

```python
import math

import jax
import jax.numpy as jnp
import ml_dtypes
import numpy as np
from jax import lax
from jax.experimental import pallas as pl
from jax.experimental.pallas import tpu as pltpu
from jax.sharding import PartitionSpec as P

RECEIVER_TOTAL = 2048
GSIZE = 64
GROUPS = 32
SUBWIN = 16
SAMPLES = 4096
TIME = 65536
BINS = 384
FIRST_BIN = 8
BAND = 64
HALF = 64
SLOTS = 10
EPS = 1e-06

N_TIME = 64
N_OWNER = 8
QUAD = 4
SLICE = TIME // N_TIME
ROWS = RECEIVER_TOTAL // N_OWNER
PART = ROWS // QUAD
LOCAL_BINS = BINS // N_TIME
LINES = LOCAL_BINS * 2 * SUBWIN
EDGE = 128

f32 = jnp.float32
bf16 = jnp.bfloat16
NT = (((1,), (1,)), ((), ()))


def quarter_table():
    bins = np.arange(BINS)[:, None] + FIRST_BIN
    phase = (bins * np.arange(SLICE)[None, :] % SAMPLES) * (2.0 * math.pi / SAMPLES)
    return np.concatenate([np.cos(phase), -np.sin(phase)]).astype(ml_dtypes.bfloat16)


TILES = SLICE // 128
BODY = TILES * PART
PACKED = PART // 2


def stage_kernel(x_ref, facing_ref, out_ref):
    low = lax.broadcasted_iota(jnp.int32, (PACKED, 128), 1) < HALF

    def pack(column, first_half):
        edge = x_ref[:, column : column + 128].astype(f32)
        for q in range(QUAD):
            a = edge[q * PART : q * PART + PACKED]
            b = edge[q * PART + PACKED : (q + 1) * PART]
            if first_half:
                b = pltpu.roll(b, HALF, 1)
            else:
                a = pltpu.roll(a, HALF, 1)
            facing_ref[q * PACKED : (q + 1) * PACKED] = jnp.where(low, a, b).astype(bf16)

    odd = lax.axis_index("tm") % 2 == 1

    @pl.when(odd)
    def _():
        pack(SLICE - 128, False)

    @pl.when(jnp.logical_not(odd))
    def _():
        pack(0, True)

    for q in range(QUAD):
        for c in range(TILES):
            out_ref[q, c * PART : (c + 1) * PART] = x_ref[
                q * PART : (q + 1) * PART, c * 128 : (c + 1) * 128
            ]
        out_ref[q, BODY:] = jnp.zeros((PACKED, 128), bf16)


def join_kernel(edges_ref, _, out_ref, sems):
    other = lax.axis_index("tm") % 2
    copies = [
        pltpu.make_async_copy(
            edges_ref.at[other, q * PACKED : (q + 1) * PACKED], out_ref.at[q, BODY:], sems.at[q]
        )
        for q in range(QUAD)
    ]
    for copy in copies:
        copy.start()
    for copy in copies:
        copy.wait()


def normalize(me, x, edge_before, edge_after):
    before = edge_before.astype(f32) * jnp.where(me == 0, 0.0, 1.0)
    after = edge_after.astype(f32) * jnp.where(me == SUBWIN - 1, 0.0, 1.0)
    before = jnp.concatenate([pltpu.roll(before, HALF, 1), before], axis=0).astype(bf16)
    after = jnp.concatenate([after, pltpu.roll(after, HALF, 1)], axis=0).astype(bf16)
    left = jnp.concatenate([before, x[: ROWS - PART, SLICE - EDGE :]], axis=0)
    right = jnp.concatenate([x[PART:, :EDGE], after], axis=0)
    mag = jnp.abs(jnp.concatenate([left, x, right], axis=1))
    step = 256
    span = step + 2 * EDGE
    k = lax.broadcasted_iota(jnp.int32, (span, step), 0)
    n = lax.broadcasted_iota(jnp.int32, (span, step), 1)
    band = jnp.where(jnp.abs(k - EDGE - n) <= HALF, 1.0, 0.0).astype(bf16)
    row = lax.broadcasted_iota(jnp.int32, (ROWS, step), 0)
    lane = lax.broadcasted_iota(jnp.int32, (ROWS, step), 1)
    blocks = []
    for j in range(SLICE // step):
        sums = jnp.dot(mag[:, j * step : j * step + span], band, preferred_element_type=f32)
        counts = 2 * HALF + 1.0
        if j == 0 or j == SLICE // step - 1:
            position = me * SAMPLES + (row // PART) * SLICE + j * step + lane
            upper = jnp.minimum(position + HALF, TIME - 1)
            lower = jnp.maximum(position - HALF, 0)
            counts = (upper - lower + 1).astype(f32)
        values = x[:, j * step : (j + 1) * step].astype(f32)
        blocks.append((values * counts / (sums + EPS * counts)).astype(bf16))
    return jnp.concatenate(blocks, axis=1)


def spectra_kernel(table_ref, x_ref, out_ref):
    columns = [
        jnp.concatenate([x_ref[q, c * PART : (c + 1) * PART] for q in range(QUAD)], axis=0)
        for c in range(TILES)
    ]
    x = jnp.concatenate(columns, axis=1)
    y = normalize(lax.axis_index("tm") // QUAD, x, x_ref[0, BODY:], x_ref[QUAD - 1, BODY:])
    p = lax.dot_general(table_ref[...], y, NT, preferred_element_type=f32)
    re, im = p[:BINS], p[BINS:]
    f = lax.broadcasted_iota(jnp.int32, (BINS, 128), 0)
    lane = lax.broadcasted_iota(jnp.int32, (BINS, 128), 1)
    odd = (f & 1) == 1
    low = lane < PART
    u_re = jnp.where(odd, re[:, :128] - re[:, 128:], re[:, :128] + re[:, 128:])
    u_im = jnp.where(odd, im[:, :128] - im[:, 128:], im[:, :128] + im[:, 128:])
    sign = jnp.where((f & 3) < 2, 1.0, -1.0)
    v_re = sign * jnp.where(odd, u_im, u_re)
    v_im = sign * jnp.where(odd, -u_re, u_im)
    raw = jnp.where(low, u_re, v_im) + pltpu.roll(jnp.where(low, u_im, v_re), PART, 1)
    for m in range(BINS // BAND):
        block = raw[m * BAND : (m + 1) * BAND]
        power = jnp.sum(block * block, axis=0, keepdims=True)
        power = jnp.broadcast_to(power, (8, 128))
        power = power + pltpu.roll(power, PART, 1)
        level = jnp.sqrt(power / BAND + EPS)
        out_ref[m * BAND : (m + 1) * BAND] = (block / level[:1]).astype(bf16)


def bin_rows():
    rows = np.arange(BINS).reshape(SUBWIN, QUAD, LOCAL_BINS).transpose(1, 2, 0).reshape(-1)
    return (np.arange(BINS)[None, :] == rows[:, None]).astype(ml_dtypes.bfloat16)


def arrange_kernel(pick_ref, x_ref, out_ref):
    per = LOCAL_BINS * SUBWIN
    z = jnp.dot(pick_ref[...], x_ref[...], preferred_element_type=f32)
    low = lax.broadcasted_iota(jnp.int32, (per, 128), 1) < PART
    for h in range(QUAD // 2):
        first = z[2 * h * per : (2 * h + 1) * per]
        second = z[(2 * h + 1) * per : (2 * h + 2) * per]
        real = jnp.where(low, first, pltpu.roll(second, PART, 1))
        imag = jnp.where(low, pltpu.roll(first, PART, 1), second)
        lines = []
        for e in range(LOCAL_BINS):
            lines += [part[e * SUBWIN : (e + 1) * SUBWIN] for part in (real, imag)]
        stations = jnp.concatenate(lines, axis=0).T.astype(bf16)
        out_ref[h * 128 : (h + 1) * 128] = stations[:, :128]
        out_ref[ROWS:, h * 64 : (h + 1) * 64] = stations[:, 128:]


def correlate_kernel(
    list_any,
    order_any,
    s_ref,
    out_hbm,
    main_ref,
    tail_ref,
    gm_ref,
    gt_ref,
    out_ref,
    order_ref,
    order_sem,
    list_ref,
    list_sem,
    sems,
):
    order_copy = pltpu.make_async_copy(order_any, order_ref, order_sem)
    order_copy.start()
    list_copy = pltpu.make_async_copy(list_any, list_ref, list_sem)
    list_copy.start()
    for n in range(N_OWNER):
        block = s_ref[n * BINS : (n + 1) * BINS].astype(f32)
        main_ref[n * ROWS : (n + 1) * ROWS] = block[:ROWS]
        tail_ref[n * ROWS : n * ROWS + 128] = block[ROWS:]
        tail_ref[n * ROWS + 128 : (n + 1) * ROWS] = pltpu.roll(block[ROWS:], 64, 1)

    order_copy.wait()
    list_copy.wait()
    rights = SLOTS * 2 * GSIZE
    sub = lax.broadcasted_iota(jnp.int32, (8, 128), 0)
    for b in range(SLOTS):
        base = jnp.maximum(list_ref[0, b], 0) * GSIZE
        base_right = jnp.maximum(list_ref[1, b], 0) * GSIZE
        for i in range(0, GSIZE, 8):
            ids = [order_ref[base + i + u] for u in range(8)]
            ids_right = [order_ref[base_right + i + u] for u in range(8)]
            for source, g_ref in ((main_ref, gm_ref), (tail_ref, gt_ref)):
                rows = [source[pl.ds(station, 8, stride=0), :] for station in ids]
                for parity in range(2):
                    at = b * 2 * GSIZE + parity * GSIZE + i
                    low = jnp.where(sub < 2, rows[parity], rows[2 + parity])
                    high = jnp.where(sub < 6, rows[4 + parity], rows[6 + parity])
                    g_ref[at : at + 8, :] = jnp.where(sub < 4, low, high)
                rows = [source[pl.ds(station, 8, stride=0), :] for station in ids_right]
                pairs = [jnp.where(sub % 2 == 0, rows[u], rows[u + 1]) for u in range(0, 8, 2)]
                low = jnp.where(sub < 2, pairs[0], pairs[1])
                high = jnp.where(sub < 6, pairs[2], pairs[3])
                at = rights + b * GSIZE + i
                g_ref[at : at + 8, :] = jnp.where(sub < 4, low, high)

    k = lax.broadcasted_iota(jnp.int32, (128, 128), 0)
    n = lax.broadcasted_iota(jnp.int32, (128, 128), 1)
    turn = jnp.where(k == (n ^ SUBWIN), jnp.where((n & SUBWIN) == 0, -1.0, 1.0), 0.0).astype(bf16)
    imag_row = (lax.broadcasted_iota(jnp.int32, (rights, 128), 0) & 1) == 1
    lefts = []
    for g_ref in (gm_ref, gt_ref):
        plain = g_ref[:rights]
        turned = jnp.dot(plain.astype(bf16), turn, preferred_element_type=f32)
        lefts.append(jnp.where(imag_row, turned, plain).astype(bf16))
    bin_of = (lax.broadcasted_iota(jnp.int32, (GSIZE, 256), 1) & 127) // (2 * SUBWIN)
    keeps = [jnp.where(bin_of == e, 1.0, 0.0).astype(bf16) for e in range(4)]
    zero = jnp.zeros((GSIZE, 128), bf16)
    copies = []
    for b in range(SLOTS):
        scale = jnp.where(list_ref[0, b] >= 0, 1.0 / SUBWIN, 0.0)
        for a, g_ref, bin0, count in ((lefts[0], gm_ref, 0, 4), (lefts[1], gt_ref, 4, 2)):
            at = b * 2 * GSIZE
            lhs = jnp.concatenate(
                [a[at : at + GSIZE], a[at + GSIZE : at + 2 * GSIZE]], axis=1
            )
            lhs = jnp.concatenate([lhs * keep for keep in keeps[:count]], axis=0)
            r = g_ref[rights + b * GSIZE : rights + (b + 1) * GSIZE].astype(bf16)
            rhs = jnp.concatenate(
                [jnp.concatenate([r, zero], axis=1), jnp.concatenate([zero, r], axis=1)], axis=0
            )
            c = lax.dot_general(lhs, rhs, NT, preferred_element_type=f32) * scale
            for e in range(count):
                out_ref[b, bin0 + e] = c[e * GSIZE : (e + 1) * GSIZE].astype(bf16)
        copies.append(pltpu.make_async_copy(out_ref.at[b], out_hbm.at[b], sems.at[b]))
        copies[-1].start()
    for copy in copies:
        copy.wait()


def vmem():
    return pl.BlockSpec(memory_space=pltpu.VMEM)


PARAMS = pltpu.CompilerParams(vmem_limit_bytes=40 * 1024 * 1024)


def correlate(block_list, station_order, stations):
    return pl.pallas_call(
        correlate_kernel,
        out_shape=jax.ShapeDtypeStruct((SLOTS, LOCAL_BINS, GSIZE, 128), bf16),
        in_specs=[pl.BlockSpec(memory_space=pl.ANY), pl.BlockSpec(memory_space=pl.ANY), vmem()],
        out_specs=pl.BlockSpec(memory_space=pltpu.HBM),
        scratch_shapes=[
            pltpu.VMEM((RECEIVER_TOTAL, 128), f32),
            pltpu.VMEM((RECEIVER_TOTAL, 128), f32),
            pltpu.VMEM((SLOTS * 3 * GSIZE, 128), f32),
            pltpu.VMEM((SLOTS * 3 * GSIZE, 128), f32),
            pltpu.VMEM((SLOTS, LOCAL_BINS, GSIZE, 128), bf16),
            pltpu.SMEM((RECEIVER_TOTAL,), jnp.int32),
            pltpu.SemaphoreType.DMA(()),
            pltpu.SMEM((2, SLOTS), jnp.int32),
            pltpu.SemaphoreType.DMA(()),
            pltpu.SemaphoreType.DMA((SLOTS,)),
        ],
        compiler_params=PARAMS,
        name="correlate",
    )(block_list.T, station_order, stations)


def local(records, station_order, block_list):
    facing, staged = pl.pallas_call(
        stage_kernel,
        out_shape=[
            jax.ShapeDtypeStruct((QUAD * PACKED, 128), bf16),
            jax.ShapeDtypeStruct((QUAD, BODY + PACKED, 128), bf16),
        ],
        in_specs=[vmem()],
        out_specs=[vmem()] * 2,
        compiler_params=PARAMS,
        name="stage",
    )(records)
    pairs = [[i, (i + 1) % N_TIME] for i in range(1, N_TIME, 2)]
    edges = lax.all_gather(facing, "tm", axis_index_groups=pairs)
    extended = pl.pallas_call(
        join_kernel,
        out_shape=jax.ShapeDtypeStruct((QUAD, BODY + PACKED, 128), bf16),
        in_specs=[pl.BlockSpec(memory_space=pl.ANY)] * 2,
        out_specs=pl.BlockSpec(memory_space=pl.ANY),
        scratch_shapes=[pltpu.SemaphoreType.DMA((QUAD,))],
        input_output_aliases={1: 0},
        compiler_params=PARAMS,
        name="join",
    )(edges, staged)
    quads = [[QUAD * g + i for i in range(QUAD)] for g in range(N_TIME // QUAD)]
    windows = lax.all_to_all(extended, "tm", 0, 0, axis_index_groups=quads, tiled=True)
    spectra = pl.pallas_call(
        spectra_kernel,
        out_shape=jax.ShapeDtypeStruct((BINS, 2 * PART), bf16),
        in_specs=[vmem(), vmem()],
        out_specs=vmem(),
        compiler_params=PARAMS,
        name="spectra",
    )(jnp.asarray(quarter_table()), windows)
    by_bin = lax.all_to_all(
        spectra.reshape(N_TIME, LOCAL_BINS // 2, 2, 2 * PART), "tm", 0, 0, tiled=True
    ).reshape(BINS, 2 * PART)
    mine = pl.pallas_call(
        arrange_kernel,
        out_shape=jax.ShapeDtypeStruct((BINS, 128), bf16),
        in_specs=[vmem()] * 2,
        out_specs=vmem(),
        compiler_params=PARAMS,
        name="arrange",
    )(jnp.asarray(bin_rows()), by_bin)
    twos = [[i, i + 1] for i in range(0, N_OWNER, 2)]
    fours = [list(range(i, N_OWNER, 2)) for i in range(2)]
    two = lax.all_gather(mine, "pairs", axis=0, axis_index_groups=twos, tiled=True)
    stations = lax.all_gather(two, "pairs", axis=0, axis_index_groups=fours, tiled=True)
    out = correlate(block_list, station_order, stations)
    out = out.reshape(SLOTS, LOCAL_BINS, GSIZE // 2, 2, 128)
    return jnp.transpose(out, (0, 1, 3, 2, 4)).reshape(SLOTS, LOCAL_BINS, 2, GSIZE * GSIZE)


def solution(mesh):
    placed = (P("pairs", "tm"), P(), P("pairs", None))
    return jax.shard_map(
        local, mesh=mesh, in_specs=placed, out_specs=P("pairs", "tm", None, None), check_vma=False
    )
```

```python
import math

import jax
import jax.numpy as jnp
import ml_dtypes
import numpy as np
from jax import lax
from jax.experimental import pallas as pl
from jax.experimental.pallas import tpu as pltpu
from jax.sharding import PartitionSpec as P

RECEIVER_TOTAL = 2048
GSIZE = 64
GROUPS = 32
SUBWIN = 16
SAMPLES = 4096
TIME = 65536
BINS = 384
FIRST_BIN = 8
BAND = 64
HALF = 64
SLOTS = 10
EPS = 1e-06

N_TIME = 64
N_OWNER = 8
QUAD = 4
SLICE = TIME // N_TIME
ROWS = RECEIVER_TOTAL // N_OWNER
PART = ROWS // QUAD
LOCAL_BINS = BINS // N_TIME
LINES = LOCAL_BINS * 2 * SUBWIN
EDGE = 128

f32 = jnp.float32
bf16 = jnp.bfloat16
NT = (((1,), (1,)), ((), ()))


def quarter_table():
    bins = np.arange(BINS)[:, None] + FIRST_BIN
    phase = (bins * np.arange(SLICE)[None, :] % SAMPLES) * (2.0 * math.pi / SAMPLES)
    return np.concatenate([np.cos(phase), -np.sin(phase)]).astype(ml_dtypes.bfloat16)


TILES = SLICE // 128
BODY = TILES * PART
PACKED = PART // 2


def stage_kernel(x_ref, facing_ref, out_ref):
    low = lax.broadcasted_iota(jnp.int32, (PACKED, 128), 1) < HALF

    def pack(column, first_half):
        edge = x_ref[:, column : column + 128].astype(f32)
        for q in range(QUAD):
            a = edge[q * PART : q * PART + PACKED]
            b = edge[q * PART + PACKED : (q + 1) * PART]
            if first_half:
                b = pltpu.roll(b, HALF, 1)
            else:
                a = pltpu.roll(a, HALF, 1)
            facing_ref[q * PACKED : (q + 1) * PACKED] = jnp.where(low, a, b).astype(bf16)

    odd = lax.axis_index("tm") % 2 == 1

    @pl.when(odd)
    def _():
        pack(SLICE - 128, False)

    @pl.when(jnp.logical_not(odd))
    def _():
        pack(0, True)

    for q in range(QUAD):
        for c in range(TILES):
            out_ref[q, c * PART : (c + 1) * PART] = x_ref[
                q * PART : (q + 1) * PART, c * 128 : (c + 1) * 128
            ]
        out_ref[q, BODY:] = jnp.zeros((PACKED, 128), bf16)


def join_kernel(edges_ref, _, out_ref, sems):
    other = lax.axis_index("tm") % 2
    copies = [
        pltpu.make_async_copy(
            edges_ref.at[other, q * PACKED : (q + 1) * PACKED], out_ref.at[q, BODY:], sems.at[q]
        )
        for q in range(QUAD)
    ]
    for copy in copies:
        copy.start()
    for copy in copies:
        copy.wait()


def normalize(me, x, edge_before, edge_after):
    before = edge_before.astype(f32) * jnp.where(me == 0, 0.0, 1.0)
    after = edge_after.astype(f32) * jnp.where(me == SUBWIN - 1, 0.0, 1.0)
    before = jnp.concatenate([pltpu.roll(before, HALF, 1), before], axis=0).astype(bf16)
    after = jnp.concatenate([after, pltpu.roll(after, HALF, 1)], axis=0).astype(bf16)
    left = jnp.concatenate([before, x[: ROWS - PART, SLICE - EDGE :]], axis=0)
    right = jnp.concatenate([x[PART:, :EDGE], after], axis=0)
    mag = jnp.abs(jnp.concatenate([left, x, right], axis=1))
    step = 256
    span = step + 2 * EDGE
    k = lax.broadcasted_iota(jnp.int32, (span, step), 0)
    n = lax.broadcasted_iota(jnp.int32, (span, step), 1)
    band = jnp.where(jnp.abs(k - EDGE - n) <= HALF, 1.0, 0.0).astype(bf16)
    row = lax.broadcasted_iota(jnp.int32, (ROWS, step), 0)
    lane = lax.broadcasted_iota(jnp.int32, (ROWS, step), 1)
    blocks = []
    for j in range(SLICE // step):
        sums = jnp.dot(mag[:, j * step : j * step + span], band, preferred_element_type=f32)
        counts = 2 * HALF + 1.0
        if j == 0 or j == SLICE // step - 1:
            position = me * SAMPLES + (row // PART) * SLICE + j * step + lane
            upper = jnp.minimum(position + HALF, TIME - 1)
            lower = jnp.maximum(position - HALF, 0)
            counts = (upper - lower + 1).astype(f32)
        values = x[:, j * step : (j + 1) * step].astype(f32)
        blocks.append((values * counts / (sums + EPS * counts)).astype(bf16))
    return jnp.concatenate(blocks, axis=1)


def spectra_kernel(table_ref, x_ref, out_ref):
    columns = [
        jnp.concatenate([x_ref[q, c * PART : (c + 1) * PART] for q in range(QUAD)], axis=0)
        for c in range(TILES)
    ]
    x = jnp.concatenate(columns, axis=1)
    y = normalize(lax.axis_index("tm") // QUAD, x, x_ref[0, BODY:], x_ref[QUAD - 1, BODY:])
    p = lax.dot_general(table_ref[...], y, NT, preferred_element_type=f32)
    re, im = p[:BINS], p[BINS:]
    f = lax.broadcasted_iota(jnp.int32, (BINS, 128), 0)
    lane = lax.broadcasted_iota(jnp.int32, (BINS, 128), 1)
    odd = (f & 1) == 1
    low = lane < PART
    u_re = jnp.where(odd, re[:, :128] - re[:, 128:], re[:, :128] + re[:, 128:])
    u_im = jnp.where(odd, im[:, :128] - im[:, 128:], im[:, :128] + im[:, 128:])
    sign = jnp.where((f & 3) < 2, 1.0, -1.0)
    v_re = sign * jnp.where(odd, u_im, u_re)
    v_im = sign * jnp.where(odd, -u_re, u_im)
    raw = jnp.where(low, u_re, v_im) + pltpu.roll(jnp.where(low, u_im, v_re), PART, 1)
    for m in range(BINS // BAND):
        block = raw[m * BAND : (m + 1) * BAND]
        power = jnp.sum(block * block, axis=0, keepdims=True)
        power = jnp.broadcast_to(power, (8, 128))
        power = power + pltpu.roll(power, PART, 1)
        level = jnp.sqrt(power / BAND + EPS)
        out_ref[m * BAND : (m + 1) * BAND] = (block / level[:1]).astype(bf16)


def bin_rows():
    rows = np.arange(BINS).reshape(SUBWIN, QUAD, LOCAL_BINS).transpose(1, 2, 0).reshape(-1)
    return (np.arange(BINS)[None, :] == rows[:, None]).astype(ml_dtypes.bfloat16)


def arrange_kernel(pick_ref, x_ref, out_ref):
    per = LOCAL_BINS * SUBWIN
    z = jnp.dot(pick_ref[...], x_ref[...], preferred_element_type=f32)
    low = lax.broadcasted_iota(jnp.int32, (per, 128), 1) < PART
    for h in range(QUAD // 2):
        first = z[2 * h * per : (2 * h + 1) * per]
        second = z[(2 * h + 1) * per : (2 * h + 2) * per]
        real = jnp.where(low, first, pltpu.roll(second, PART, 1))
        imag = jnp.where(low, pltpu.roll(first, PART, 1), second)
        lines = []
        for e in range(LOCAL_BINS):
            lines += [part[e * SUBWIN : (e + 1) * SUBWIN] for part in (real, imag)]
        stations = jnp.concatenate(lines, axis=0).T.astype(bf16)
        out_ref[h * 128 : (h + 1) * 128] = stations[:, :128]
        out_ref[ROWS:, h * 64 : (h + 1) * 64] = stations[:, 128:]


def correlate_kernel(
    list_any,
    order_any,
    s_ref,
    out_hbm,
    main_ref,
    tail_ref,
    gm_ref,
    gt_ref,
    out_ref,
    order_ref,
    order_sem,
    list_ref,
    list_sem,
    sems,
):
    order_copy = pltpu.make_async_copy(order_any, order_ref, order_sem)
    order_copy.start()
    list_copy = pltpu.make_async_copy(list_any, list_ref, list_sem)
    list_copy.start()
    for n in range(N_OWNER):
        block = s_ref[n * BINS : (n + 1) * BINS].astype(f32)
        main_ref[n * ROWS : (n + 1) * ROWS] = block[:ROWS]
        tail_ref[n * ROWS : n * ROWS + 128] = block[ROWS:]
        tail_ref[n * ROWS + 128 : (n + 1) * ROWS] = pltpu.roll(block[ROWS:], 64, 1)

    order_copy.wait()
    list_copy.wait()
    rights = SLOTS * 2 * GSIZE
    sub = lax.broadcasted_iota(jnp.int32, (8, 128), 0)
    for b in range(SLOTS):
        base = jnp.maximum(list_ref[0, b], 0) * GSIZE
        base_right = jnp.maximum(list_ref[1, b], 0) * GSIZE
        for i in range(0, GSIZE, 8):
            ids = [order_ref[base + i + u] for u in range(8)]
            ids_right = [order_ref[base_right + i + u] for u in range(8)]
            for source, g_ref in ((main_ref, gm_ref), (tail_ref, gt_ref)):
                rows = [source[pl.ds(station, 8, stride=0), :] for station in ids]
                for parity in range(2):
                    at = b * 2 * GSIZE + parity * GSIZE + i
                    low = jnp.where(sub < 2, rows[parity], rows[2 + parity])
                    high = jnp.where(sub < 6, rows[4 + parity], rows[6 + parity])
                    g_ref[at : at + 8, :] = jnp.where(sub < 4, low, high)
                rows = [source[pl.ds(station, 8, stride=0), :] for station in ids_right]
                pairs = [jnp.where(sub % 2 == 0, rows[u], rows[u + 1]) for u in range(0, 8, 2)]
                low = jnp.where(sub < 2, pairs[0], pairs[1])
                high = jnp.where(sub < 6, pairs[2], pairs[3])
                at = rights + b * GSIZE + i
                g_ref[at : at + 8, :] = jnp.where(sub < 4, low, high)

    k = lax.broadcasted_iota(jnp.int32, (128, 128), 0)
    n = lax.broadcasted_iota(jnp.int32, (128, 128), 1)
    turn = jnp.where(k == (n ^ SUBWIN), jnp.where((n & SUBWIN) == 0, -1.0, 1.0), 0.0).astype(bf16)
    imag_row = (lax.broadcasted_iota(jnp.int32, (rights, 128), 0) & 1) == 1
    lefts = []
    for g_ref in (gm_ref, gt_ref):
        plain = g_ref[:rights]
        turned = jnp.dot(plain.astype(bf16), turn, preferred_element_type=f32)
        lefts.append(jnp.where(imag_row, turned, plain).astype(bf16))
    bin_of = (lax.broadcasted_iota(jnp.int32, (GSIZE, 256), 1) & 127) // (2 * SUBWIN)
    keeps = [jnp.where(bin_of == e, 1.0, 0.0).astype(bf16) for e in range(4)]
    zero = jnp.zeros((GSIZE, 128), bf16)
    copies = []
    for b in range(SLOTS):
        scale = jnp.where(list_ref[0, b] >= 0, 1.0 / SUBWIN, 0.0)
        for a, g_ref, bin0, count in ((lefts[0], gm_ref, 0, 4), (lefts[1], gt_ref, 4, 2)):
            at = b * 2 * GSIZE
            lhs = jnp.concatenate(
                [a[at : at + GSIZE], a[at + GSIZE : at + 2 * GSIZE]], axis=1
            )
            lhs = jnp.concatenate([lhs * keep for keep in keeps[:count]], axis=0)
            r = g_ref[rights + b * GSIZE : rights + (b + 1) * GSIZE].astype(bf16)
            rhs = jnp.concatenate(
                [jnp.concatenate([r, zero], axis=1), jnp.concatenate([zero, r], axis=1)], axis=0
            )
            c = lax.dot_general(lhs, rhs, NT, preferred_element_type=f32) * scale
            for e in range(count):
                out_ref[b, bin0 + e] = c[e * GSIZE : (e + 1) * GSIZE].astype(bf16)
        copies.append(pltpu.make_async_copy(out_ref.at[b], out_hbm.at[b], sems.at[b]))
        copies[-1].start()
    for copy in copies:
        copy.wait()


def vmem():
    return pl.BlockSpec(memory_space=pltpu.VMEM)


PARAMS = pltpu.CompilerParams(vmem_limit_bytes=40 * 1024 * 1024)


def correlate(block_list, station_order, stations):
    return pl.pallas_call(
        correlate_kernel,
        out_shape=jax.ShapeDtypeStruct((SLOTS, LOCAL_BINS, GSIZE, 128), bf16),
        in_specs=[pl.BlockSpec(memory_space=pl.ANY), pl.BlockSpec(memory_space=pl.ANY), vmem()],
        out_specs=pl.BlockSpec(memory_space=pltpu.HBM),
        scratch_shapes=[
            pltpu.VMEM((RECEIVER_TOTAL + 8, 128), f32),
            pltpu.VMEM((RECEIVER_TOTAL + 8, 128), f32),
            pltpu.VMEM((SLOTS * 3 * GSIZE, 128), f32),
            pltpu.VMEM((SLOTS * 3 * GSIZE, 128), f32),
            pltpu.VMEM((SLOTS, LOCAL_BINS, GSIZE, 128), bf16),
            pltpu.SMEM((RECEIVER_TOTAL,), jnp.int32),
            pltpu.SemaphoreType.DMA(()),
            pltpu.SMEM((2, SLOTS), jnp.int32),
            pltpu.SemaphoreType.DMA(()),
            pltpu.SemaphoreType.DMA((SLOTS,)),
        ],
        compiler_params=PARAMS,
        name="correlate",
    )(block_list.T, station_order, stations)


def local(records, station_order, block_list):
    facing, staged = pl.pallas_call(
        stage_kernel,
        out_shape=[
            jax.ShapeDtypeStruct((QUAD * PACKED, 128), bf16),
            jax.ShapeDtypeStruct((QUAD, BODY + PACKED, 128), bf16),
        ],
        in_specs=[vmem()],
        out_specs=[vmem()] * 2,
        compiler_params=PARAMS,
        name="stage",
    )(records)
    pairs = [[i, (i + 1) % N_TIME] for i in range(1, N_TIME, 2)]
    edges = lax.all_gather(facing, "tm", axis_index_groups=pairs)
    extended = pl.pallas_call(
        join_kernel,
        out_shape=jax.ShapeDtypeStruct((QUAD, BODY + PACKED, 128), bf16),
        in_specs=[pl.BlockSpec(memory_space=pl.ANY)] * 2,
        out_specs=pl.BlockSpec(memory_space=pl.ANY),
        scratch_shapes=[pltpu.SemaphoreType.DMA((QUAD,))],
        input_output_aliases={1: 0},
        compiler_params=PARAMS,
        name="join",
    )(edges, staged)
    quads = [[QUAD * g + i for i in range(QUAD)] for g in range(N_TIME // QUAD)]
    windows = lax.all_to_all(extended, "tm", 0, 0, axis_index_groups=quads, tiled=True)
    spectra = pl.pallas_call(
        spectra_kernel,
        out_shape=jax.ShapeDtypeStruct((BINS, 2 * PART), bf16),
        in_specs=[vmem(), vmem()],
        out_specs=vmem(),
        compiler_params=PARAMS,
        name="spectra",
    )(jnp.asarray(quarter_table()), windows)
    by_bin = lax.all_to_all(
        spectra.reshape(N_TIME, LOCAL_BINS // 2, 2, 2 * PART), "tm", 0, 0, tiled=True
    ).reshape(BINS, 2 * PART)
    mine = pl.pallas_call(
        arrange_kernel,
        out_shape=jax.ShapeDtypeStruct((BINS, 128), bf16),
        in_specs=[vmem()] * 2,
        out_specs=vmem(),
        compiler_params=PARAMS,
        name="arrange",
    )(jnp.asarray(bin_rows()), by_bin)
    twos = [[i, i + 1] for i in range(0, N_OWNER, 2)]
    fours = [list(range(i, N_OWNER, 2)) for i in range(2)]
    two = lax.all_gather(mine, "pairs", axis=0, axis_index_groups=twos, tiled=True)
    stations = lax.all_gather(two, "pairs", axis=0, axis_index_groups=fours, tiled=True)
    out = correlate(block_list, station_order, stations)
    out = out.reshape(SLOTS, LOCAL_BINS, GSIZE // 2, 2, 128)
    return jnp.transpose(out, (0, 1, 3, 2, 4)).reshape(SLOTS, LOCAL_BINS, 2, GSIZE * GSIZE)


def solution(mesh):
    placed = (P("pairs", "tm"), P(), P("pairs", None))
    return jax.shard_map(
        local, mesh=mesh, in_specs=placed, out_specs=P("pairs", "tm", None, None), check_vma=False
    )
```

```python
import math

import jax
import jax.numpy as jnp
import ml_dtypes
import numpy as np
from jax import lax
from jax.experimental import pallas as pl
from jax.experimental.pallas import tpu as pltpu
from jax.sharding import PartitionSpec as P

RECEIVER_TOTAL = 2048
GSIZE = 64
GROUPS = 32
SUBWIN = 16
SAMPLES = 4096
TIME = 65536
BINS = 384
FIRST_BIN = 8
BAND = 64
HALF = 64
SLOTS = 10
EPS = 1e-06

N_TIME = 64
N_OWNER = 8
QUAD = 4
SLICE = TIME // N_TIME
ROWS = RECEIVER_TOTAL // N_OWNER
PART = ROWS // QUAD
LOCAL_BINS = BINS // N_TIME
LINES = LOCAL_BINS * 2 * SUBWIN
EDGE = 128

f32 = jnp.float32
bf16 = jnp.bfloat16
NT = (((1,), (1,)), ((), ()))


def quarter_table():
    bins = np.arange(BINS)[:, None] + FIRST_BIN
    phase = (bins * np.arange(SLICE)[None, :] % SAMPLES) * (2.0 * math.pi / SAMPLES)
    return np.concatenate([np.cos(phase), -np.sin(phase)]).astype(ml_dtypes.bfloat16)


TILES = SLICE // 128
BODY = TILES * PART
PACKED = PART // 2


def stage_kernel(x_hbm, facing_ref, out_ref, sems):
    low = lax.broadcasted_iota(jnp.int32, (PACKED, 128), 1) < HALF
    copies = [
        pltpu.make_async_copy(
            x_hbm.at[:, :, c * 128 : (c + 1) * 128],
            out_ref.at[:, c * PART : (c + 1) * PART],
            sems.at[c],
        )
        for c in range(TILES)
    ]
    order = [0, TILES - 1] + list(range(1, TILES - 1))
    for c in order:
        copies[c].start()
    for q in range(QUAD):
        out_ref[q, BODY:] = jnp.zeros((PACKED, 128), bf16)
    copies[0].wait()
    copies[TILES - 1].wait()

    def pack(column, first_half):
        for q in range(QUAD):
            edge = out_ref[q, column * PART : (column + 1) * PART].astype(f32)
            a, b = edge[:PACKED], edge[PACKED:]
            if first_half:
                b = pltpu.roll(b, HALF, 1)
            else:
                a = pltpu.roll(a, HALF, 1)
            facing_ref[q * PACKED : (q + 1) * PACKED] = jnp.where(low, a, b).astype(bf16)

    odd = lax.axis_index("tm") % 2 == 1

    @pl.when(odd)
    def _():
        pack(TILES - 1, False)

    @pl.when(jnp.logical_not(odd))
    def _():
        pack(0, True)

    for c in order[2:]:
        copies[c].wait()


def join_kernel(edges_ref, _, out_ref, sems):
    other = lax.axis_index("tm") % 2
    copies = [
        pltpu.make_async_copy(
            edges_ref.at[other, q * PACKED : (q + 1) * PACKED], out_ref.at[q, BODY:], sems.at[q]
        )
        for q in range(QUAD)
    ]
    for copy in copies:
        copy.start()
    for copy in copies:
        copy.wait()


def normalize(me, x, edge_before, edge_after):
    before = edge_before.astype(f32) * jnp.where(me == 0, 0.0, 1.0)
    after = edge_after.astype(f32) * jnp.where(me == SUBWIN - 1, 0.0, 1.0)
    before = jnp.concatenate([pltpu.roll(before, HALF, 1), before], axis=0).astype(bf16)
    after = jnp.concatenate([after, pltpu.roll(after, HALF, 1)], axis=0).astype(bf16)
    left = jnp.concatenate([before, x[: ROWS - PART, SLICE - EDGE :]], axis=0)
    right = jnp.concatenate([x[PART:, :EDGE], after], axis=0)
    mag = jnp.abs(jnp.concatenate([left, x, right], axis=1))
    step = 256
    span = step + 2 * EDGE
    k = lax.broadcasted_iota(jnp.int32, (span, step), 0)
    n = lax.broadcasted_iota(jnp.int32, (span, step), 1)
    band = jnp.where(jnp.abs(k - EDGE - n) <= HALF, 1.0, 0.0).astype(bf16)
    row = lax.broadcasted_iota(jnp.int32, (ROWS, step), 0)
    lane = lax.broadcasted_iota(jnp.int32, (ROWS, step), 1)
    blocks = []
    for j in range(SLICE // step):
        sums = jnp.dot(mag[:, j * step : j * step + span], band, preferred_element_type=f32)
        counts = 2 * HALF + 1.0
        if j == 0 or j == SLICE // step - 1:
            position = me * SAMPLES + (row // PART) * SLICE + j * step + lane
            upper = jnp.minimum(position + HALF, TIME - 1)
            lower = jnp.maximum(position - HALF, 0)
            counts = (upper - lower + 1).astype(f32)
        values = x[:, j * step : (j + 1) * step].astype(f32)
        blocks.append((values * counts / (sums + EPS * counts)).astype(bf16))
    return jnp.concatenate(blocks, axis=1)


def spectra_kernel(table_hbm, x_ref, out_ref, table_ref, sems):
    loads = [
        pltpu.make_async_copy(
            table_hbm.at[c * BINS : (c + 1) * BINS],
            table_ref.at[c * BINS : (c + 1) * BINS],
            sems.at[c],
        )
        for c in range(2)
    ]
    for load in loads:
        load.start()
    columns = [
        jnp.concatenate([x_ref[q, c * PART : (c + 1) * PART] for q in range(QUAD)], axis=0)
        for c in range(TILES)
    ]
    x = jnp.concatenate(columns, axis=1)
    y = normalize(lax.axis_index("tm") // QUAD, x, x_ref[0, BODY:], x_ref[QUAD - 1, BODY:])
    loads[0].wait()
    re = lax.dot_general(table_ref[:BINS], y, NT, preferred_element_type=f32)
    loads[1].wait()
    im = lax.dot_general(table_ref[BINS:], y, NT, preferred_element_type=f32)
    f = lax.broadcasted_iota(jnp.int32, (BINS, 128), 0)
    lane = lax.broadcasted_iota(jnp.int32, (BINS, 128), 1)
    odd = (f & 1) == 1
    low = lane < PART
    u_re = jnp.where(odd, re[:, :128] - re[:, 128:], re[:, :128] + re[:, 128:])
    u_im = jnp.where(odd, im[:, :128] - im[:, 128:], im[:, :128] + im[:, 128:])
    sign = jnp.where((f & 3) < 2, 1.0, -1.0)
    v_re = sign * jnp.where(odd, u_im, u_re)
    v_im = sign * jnp.where(odd, -u_re, u_im)
    raw = jnp.where(low, u_re, v_im) + pltpu.roll(jnp.where(low, u_im, v_re), PART, 1)
    for m in range(BINS // BAND):
        block = raw[m * BAND : (m + 1) * BAND]
        power = jnp.sum(block * block, axis=0, keepdims=True)
        power = jnp.broadcast_to(power, (8, 128))
        power = power + pltpu.roll(power, PART, 1)
        level = jnp.sqrt(power / BAND + EPS)
        out_ref[m * BAND : (m + 1) * BAND] = (block / level[:1]).astype(bf16)


def bin_rows():
    rows = np.arange(BINS).reshape(SUBWIN, QUAD, LOCAL_BINS).transpose(1, 2, 0).reshape(-1)
    return (np.arange(BINS)[None, :] == rows[:, None]).astype(ml_dtypes.bfloat16)


def arrange_kernel(pick_ref, x_ref, out_ref):
    per = LOCAL_BINS * SUBWIN
    z = jnp.dot(pick_ref[...], x_ref[...], preferred_element_type=f32)
    low = lax.broadcasted_iota(jnp.int32, (per, 128), 1) < PART
    for h in range(QUAD // 2):
        first = z[2 * h * per : (2 * h + 1) * per]
        second = z[(2 * h + 1) * per : (2 * h + 2) * per]
        real = jnp.where(low, first, pltpu.roll(second, PART, 1))
        imag = jnp.where(low, pltpu.roll(first, PART, 1), second)
        lines = []
        for e in range(LOCAL_BINS):
            lines += [part[e * SUBWIN : (e + 1) * SUBWIN] for part in (real, imag)]
        stations = jnp.concatenate(lines, axis=0).T.astype(bf16)
        out_ref[h * 128 : (h + 1) * 128] = stations[:, :128]
        out_ref[ROWS:, h * 64 : (h + 1) * 64] = stations[:, 128:]


def correlate_kernel(
    list_any,
    order_any,
    s_ref,
    out_hbm,
    main_ref,
    tail_ref,
    gm_ref,
    gt_ref,
    out_ref,
    order_ref,
    order_sem,
    list_ref,
    list_sem,
    sems,
):
    order_copy = pltpu.make_async_copy(order_any, order_ref, order_sem)
    order_copy.start()
    list_copy = pltpu.make_async_copy(list_any, list_ref, list_sem)
    list_copy.start()
    for n in range(N_OWNER):
        block = s_ref[n * BINS : (n + 1) * BINS].astype(f32)
        main_ref[n * ROWS : (n + 1) * ROWS] = block[:ROWS]
        tail_ref[n * ROWS : n * ROWS + 128] = block[ROWS:]
        tail_ref[n * ROWS + 128 : (n + 1) * ROWS] = pltpu.roll(block[ROWS:], 64, 1)

    order_copy.wait()
    list_copy.wait()
    rights = SLOTS * 2 * GSIZE
    sub = lax.broadcasted_iota(jnp.int32, (8, 128), 0)
    for b in range(SLOTS):
        base = jnp.maximum(list_ref[0, b], 0) * GSIZE
        base_right = jnp.maximum(list_ref[1, b], 0) * GSIZE
        for i in range(0, GSIZE, 8):
            ids = [order_ref[base + i + u] for u in range(8)]
            ids_right = [order_ref[base_right + i + u] for u in range(8)]
            for source, g_ref in ((main_ref, gm_ref), (tail_ref, gt_ref)):
                rows = [source[pl.ds(station, 8, stride=0), :] for station in ids]
                for parity in range(2):
                    at = b * 2 * GSIZE + parity * GSIZE + i
                    low = jnp.where(sub < 2, rows[parity], rows[2 + parity])
                    high = jnp.where(sub < 6, rows[4 + parity], rows[6 + parity])
                    g_ref[at : at + 8, :] = jnp.where(sub < 4, low, high)
                rows = [source[pl.ds(station, 8, stride=0), :] for station in ids_right]
                pairs = [jnp.where(sub % 2 == 0, rows[u], rows[u + 1]) for u in range(0, 8, 2)]
                low = jnp.where(sub < 2, pairs[0], pairs[1])
                high = jnp.where(sub < 6, pairs[2], pairs[3])
                at = rights + b * GSIZE + i
                g_ref[at : at + 8, :] = jnp.where(sub < 4, low, high)

    k = lax.broadcasted_iota(jnp.int32, (128, 128), 0)
    n = lax.broadcasted_iota(jnp.int32, (128, 128), 1)
    turn = jnp.where(k == (n ^ SUBWIN), jnp.where((n & SUBWIN) == 0, -1.0, 1.0), 0.0).astype(bf16)
    imag_row = (lax.broadcasted_iota(jnp.int32, (rights, 128), 0) & 1) == 1
    lefts = []
    for g_ref in (gm_ref, gt_ref):
        plain = g_ref[:rights]
        turned = jnp.dot(plain.astype(bf16), turn, preferred_element_type=f32)
        lefts.append(jnp.where(imag_row, turned, plain).astype(bf16))
    bin_of = (lax.broadcasted_iota(jnp.int32, (GSIZE, 256), 1) & 127) // (2 * SUBWIN)
    keeps = [jnp.where(bin_of == e, 1.0, 0.0).astype(bf16) for e in range(4)]
    zero = jnp.zeros((GSIZE, 128), bf16)
    copies = []
    for b in range(SLOTS):
        scale = jnp.where(list_ref[0, b] >= 0, 1.0 / SUBWIN, 0.0)
        for a, g_ref, bin0, count in ((lefts[0], gm_ref, 0, 4), (lefts[1], gt_ref, 4, 2)):
            at = b * 2 * GSIZE
            lhs = jnp.concatenate(
                [a[at : at + GSIZE], a[at + GSIZE : at + 2 * GSIZE]], axis=1
            )
            lhs = jnp.concatenate([lhs * keep for keep in keeps[:count]], axis=0)
            r = g_ref[rights + b * GSIZE : rights + (b + 1) * GSIZE].astype(bf16)
            rhs = jnp.concatenate(
                [jnp.concatenate([r, zero], axis=1), jnp.concatenate([zero, r], axis=1)], axis=0
            )
            c = lax.dot_general(lhs, rhs, NT, preferred_element_type=f32) * scale
            for e in range(count):
                out_ref[b, bin0 + e] = c[e * GSIZE : (e + 1) * GSIZE].astype(bf16)
        copies.append(pltpu.make_async_copy(out_ref.at[b], out_hbm.at[b], sems.at[b]))
        copies[-1].start()
    for copy in copies:
        copy.wait()


def vmem():
    return pl.BlockSpec(memory_space=pltpu.VMEM)


PARAMS = pltpu.CompilerParams(vmem_limit_bytes=40 * 1024 * 1024)


def correlate(block_list, station_order, stations):
    return pl.pallas_call(
        correlate_kernel,
        out_shape=jax.ShapeDtypeStruct((SLOTS, LOCAL_BINS, GSIZE, 128), bf16),
        in_specs=[pl.BlockSpec(memory_space=pl.ANY), pl.BlockSpec(memory_space=pl.ANY), vmem()],
        out_specs=pl.BlockSpec(memory_space=pltpu.HBM),
        scratch_shapes=[
            pltpu.VMEM((RECEIVER_TOTAL + 8, 128), f32),
            pltpu.VMEM((RECEIVER_TOTAL + 8, 128), f32),
            pltpu.VMEM((SLOTS * 3 * GSIZE, 128), f32),
            pltpu.VMEM((SLOTS * 3 * GSIZE, 128), f32),
            pltpu.VMEM((SLOTS, LOCAL_BINS, GSIZE, 128), bf16),
            pltpu.SMEM((RECEIVER_TOTAL,), jnp.int32),
            pltpu.SemaphoreType.DMA(()),
            pltpu.SMEM((2, SLOTS), jnp.int32),
            pltpu.SemaphoreType.DMA(()),
            pltpu.SemaphoreType.DMA((SLOTS,)),
        ],
        compiler_params=PARAMS,
        name="correlate",
    )(block_list.T, station_order, stations)


def local(records, station_order, block_list):
    facing, staged = pl.pallas_call(
        stage_kernel,
        out_shape=[
            jax.ShapeDtypeStruct((QUAD * PACKED, 128), bf16),
            jax.ShapeDtypeStruct((QUAD, BODY + PACKED, 128), bf16),
        ],
        in_specs=[pl.BlockSpec(memory_space=pltpu.HBM)],
        out_specs=[vmem()] * 2,
        scratch_shapes=[pltpu.SemaphoreType.DMA((TILES,))],
        compiler_params=PARAMS,
        name="stage",
    )(pltpu.with_memory_space_constraint(records.reshape(QUAD, PART, SLICE), pltpu.HBM))
    pairs = [[i, (i + 1) % N_TIME] for i in range(1, N_TIME, 2)]
    edges = lax.all_gather(facing, "tm", axis_index_groups=pairs)
    extended = pl.pallas_call(
        join_kernel,
        out_shape=jax.ShapeDtypeStruct((QUAD, BODY + PACKED, 128), bf16),
        in_specs=[pl.BlockSpec(memory_space=pl.ANY)] * 2,
        out_specs=pl.BlockSpec(memory_space=pl.ANY),
        scratch_shapes=[pltpu.SemaphoreType.DMA((QUAD,))],
        input_output_aliases={1: 0},
        compiler_params=PARAMS,
        name="join",
    )(edges, staged)
    quads = [[QUAD * g + i for i in range(QUAD)] for g in range(N_TIME // QUAD)]
    windows = lax.all_to_all(extended, "tm", 0, 0, axis_index_groups=quads, tiled=True)
    spectra = pl.pallas_call(
        spectra_kernel,
        out_shape=jax.ShapeDtypeStruct((BINS, 2 * PART), bf16),
        in_specs=[pl.BlockSpec(memory_space=pltpu.HBM), vmem()],
        out_specs=vmem(),
        scratch_shapes=[
            pltpu.VMEM((2 * BINS, SLICE), bf16),
            pltpu.SemaphoreType.DMA((2,)),
        ],
        compiler_params=PARAMS,
        name="spectra",
    )(pltpu.with_memory_space_constraint(jnp.asarray(quarter_table()), pltpu.HBM), windows)
    by_bin = lax.all_to_all(
        spectra.reshape(N_TIME, LOCAL_BINS // 2, 2, 2 * PART), "tm", 0, 0, tiled=True
    ).reshape(BINS, 2 * PART)
    mine = pl.pallas_call(
        arrange_kernel,
        out_shape=jax.ShapeDtypeStruct((BINS, 128), bf16),
        in_specs=[vmem()] * 2,
        out_specs=vmem(),
        compiler_params=PARAMS,
        name="arrange",
    )(jnp.asarray(bin_rows()), by_bin)
    twos = [[i, i + 1] for i in range(0, N_OWNER, 2)]
    fours = [list(range(i, N_OWNER, 2)) for i in range(2)]
    two = lax.all_gather(mine, "pairs", axis=0, axis_index_groups=twos, tiled=True)
    stations = lax.all_gather(two, "pairs", axis=0, axis_index_groups=fours, tiled=True)
    out = correlate(block_list, station_order, stations)
    out = out.reshape(SLOTS, LOCAL_BINS, GSIZE // 2, 2, 128)
    return jnp.transpose(out, (0, 1, 3, 2, 4)).reshape(SLOTS, LOCAL_BINS, 2, GSIZE * GSIZE)


def solution(mesh):
    placed = (P("pairs", "tm"), P(), P("pairs", None))
    return jax.shard_map(
        local, mesh=mesh, in_specs=placed, out_specs=P("pairs", "tm", None, None), check_vma=False
    )
```

```python
import math

import jax
import jax.numpy as jnp
import ml_dtypes
import numpy as np
from jax import lax
from jax.experimental import pallas as pl
from jax.experimental.pallas import tpu as pltpu
from jax.sharding import PartitionSpec as P

RECEIVER_TOTAL = 2048
GSIZE = 64
GROUPS = 32
SUBWIN = 16
SAMPLES = 4096
TIME = 65536
BINS = 384
FIRST_BIN = 8
BAND = 64
HALF = 64
SLOTS = 10
EPS = 1e-06

N_TIME = 64
N_OWNER = 8
QUAD = 4
SLICE = TIME // N_TIME
ROWS = RECEIVER_TOTAL // N_OWNER
PART = ROWS // QUAD
LOCAL_BINS = BINS // N_TIME
LINES = LOCAL_BINS * 2 * SUBWIN
EDGE = 128

f32 = jnp.float32
bf16 = jnp.bfloat16
NT = (((1,), (1,)), ((), ()))


def quarter_table():
    bins = np.arange(BINS)[:, None] + FIRST_BIN
    phase = (bins * np.arange(SLICE)[None, :] % SAMPLES) * (2.0 * math.pi / SAMPLES)
    return np.concatenate([np.cos(phase), -np.sin(phase)]).astype(ml_dtypes.bfloat16)


TILES = SLICE // 128
BODY = TILES * PART
PACKED = PART // 2


def stage_kernel(x_ref, facing_ref, out_ref):
    low = lax.broadcasted_iota(jnp.int32, (PACKED, 128), 1) < HALF

    def pack(column, first_half):
        edge = x_ref[:, column : column + 128].astype(f32)
        for q in range(QUAD):
            a = edge[q * PART : q * PART + PACKED]
            b = edge[q * PART + PACKED : (q + 1) * PART]
            if first_half:
                b = pltpu.roll(b, HALF, 1)
            else:
                a = pltpu.roll(a, HALF, 1)
            facing_ref[q * PACKED : (q + 1) * PACKED] = jnp.where(low, a, b).astype(bf16)

    odd = lax.axis_index("tm") % 2 == 1

    @pl.when(odd)
    def _():
        pack(SLICE - 128, False)

    @pl.when(jnp.logical_not(odd))
    def _():
        pack(0, True)

    for q in range(QUAD):
        for c in range(TILES):
            out_ref[q, c * PART : (c + 1) * PART] = x_ref[
                q * PART : (q + 1) * PART, c * 128 : (c + 1) * 128
            ]
        out_ref[q, BODY:] = jnp.zeros((PACKED, 128), bf16)


def join_kernel(edges_ref, _, out_ref, sems):
    other = lax.axis_index("tm") % 2
    copies = [
        pltpu.make_async_copy(
            edges_ref.at[other, q * PACKED : (q + 1) * PACKED], out_ref.at[q, BODY:], sems.at[q]
        )
        for q in range(QUAD)
    ]
    for copy in copies:
        copy.start()
    for copy in copies:
        copy.wait()


def normalize(me, x, edge_before, edge_after):
    before = edge_before.astype(f32) * jnp.where(me == 0, 0.0, 1.0)
    after = edge_after.astype(f32) * jnp.where(me == SUBWIN - 1, 0.0, 1.0)
    before = jnp.concatenate([pltpu.roll(before, HALF, 1), before], axis=0).astype(bf16)
    after = jnp.concatenate([after, pltpu.roll(after, HALF, 1)], axis=0).astype(bf16)
    left = jnp.concatenate([before, x[: ROWS - PART, SLICE - EDGE :]], axis=0)
    right = jnp.concatenate([x[PART:, :EDGE], after], axis=0)
    mag = jnp.abs(jnp.concatenate([left, x, right], axis=1))
    step = 256
    span = step + 2 * EDGE
    k = lax.broadcasted_iota(jnp.int32, (span, step), 0)
    n = lax.broadcasted_iota(jnp.int32, (span, step), 1)
    band = jnp.where(jnp.abs(k - EDGE - n) <= HALF, 1.0, 0.0).astype(bf16)
    row = lax.broadcasted_iota(jnp.int32, (ROWS, step), 0)
    lane = lax.broadcasted_iota(jnp.int32, (ROWS, step), 1)
    blocks = []
    for j in range(SLICE // step):
        sums = jnp.dot(mag[:, j * step : j * step + span], band, preferred_element_type=f32)
        counts = 2 * HALF + 1.0
        if j == 0 or j == SLICE // step - 1:
            position = me * SAMPLES + (row // PART) * SLICE + j * step + lane
            upper = jnp.minimum(position + HALF, TIME - 1)
            lower = jnp.maximum(position - HALF, 0)
            counts = (upper - lower + 1).astype(f32)
        values = x[:, j * step : (j + 1) * step].astype(f32)
        blocks.append((values * counts / (sums + EPS * counts)).astype(bf16))
    return jnp.concatenate(blocks, axis=1)


def spectra_kernel(table_ref, x_ref, out_ref):
    columns = [
        jnp.concatenate([x_ref[q, c * PART : (c + 1) * PART] for q in range(QUAD)], axis=0)
        for c in range(TILES)
    ]
    x = jnp.concatenate(columns, axis=1)
    y = normalize(lax.axis_index("tm") // QUAD, x, x_ref[0, BODY:], x_ref[QUAD - 1, BODY:])
    p = lax.dot_general(table_ref[...], y, NT, preferred_element_type=f32)
    re, im = p[:BINS], p[BINS:]
    f = lax.broadcasted_iota(jnp.int32, (BINS, 128), 0)
    lane = lax.broadcasted_iota(jnp.int32, (BINS, 128), 1)
    odd = (f & 1) == 1
    low = lane < PART
    u_re = jnp.where(odd, re[:, :128] - re[:, 128:], re[:, :128] + re[:, 128:])
    u_im = jnp.where(odd, im[:, :128] - im[:, 128:], im[:, :128] + im[:, 128:])
    sign = jnp.where((f & 3) < 2, 1.0, -1.0)
    v_re = sign * jnp.where(odd, u_im, u_re)
    v_im = sign * jnp.where(odd, -u_re, u_im)
    raw = jnp.where(low, u_re, v_im) + pltpu.roll(jnp.where(low, u_im, v_re), PART, 1)
    for m in range(BINS // BAND):
        block = raw[m * BAND : (m + 1) * BAND]
        power = jnp.sum(block * block, axis=0, keepdims=True)
        power = jnp.broadcast_to(power, (8, 128))
        power = power + pltpu.roll(power, PART, 1)
        level = jnp.sqrt(power / BAND + EPS)
        out_ref[m * BAND : (m + 1) * BAND] = (block / level[:1]).astype(bf16)


def bin_rows():
    rows = np.arange(BINS).reshape(SUBWIN, QUAD, LOCAL_BINS).transpose(1, 2, 0).reshape(-1)
    return (np.arange(BINS)[None, :] == rows[:, None]).astype(ml_dtypes.bfloat16)


def arrange_kernel(pick_ref, x_ref, out_ref):
    per = LOCAL_BINS * SUBWIN
    z = jnp.dot(pick_ref[...], x_ref[...], preferred_element_type=f32)
    low = lax.broadcasted_iota(jnp.int32, (per, 128), 1) < PART
    for h in range(QUAD // 2):
        first = z[2 * h * per : (2 * h + 1) * per]
        second = z[(2 * h + 1) * per : (2 * h + 2) * per]
        real = jnp.where(low, first, pltpu.roll(second, PART, 1))
        imag = jnp.where(low, pltpu.roll(first, PART, 1), second)
        lines = []
        for e in range(LOCAL_BINS):
            lines += [part[e * SUBWIN : (e + 1) * SUBWIN] for part in (real, imag)]
        stations = jnp.concatenate(lines, axis=0).T.astype(bf16)
        out_ref[h * 128 : (h + 1) * 128] = stations[:, :128]
        out_ref[ROWS:, h * 64 : (h + 1) * 64] = stations[:, 128:]


def correlate_kernel(
    list_any,
    order_any,
    s_ref,
    out_hbm,
    main_ref,
    tail_ref,
    gm_ref,
    gt_ref,
    out_ref,
    order_ref,
    order_sem,
    list_ref,
    list_sem,
    sems,
):
    order_copy = pltpu.make_async_copy(order_any, order_ref, order_sem)
    order_copy.start()
    list_copy = pltpu.make_async_copy(list_any, list_ref, list_sem)
    list_copy.start()
    for n in range(N_OWNER):
        at = n // 2 + n % 2 * (N_OWNER // 2)
        block = s_ref[at * BINS : (at + 1) * BINS].astype(f32)
        main_ref[n * ROWS : (n + 1) * ROWS] = block[:ROWS]
        tail_ref[n * ROWS : n * ROWS + 128] = block[ROWS:]
        tail_ref[n * ROWS + 128 : (n + 1) * ROWS] = pltpu.roll(block[ROWS:], 64, 1)

    order_copy.wait()
    list_copy.wait()
    rights = SLOTS * 2 * GSIZE
    sub = lax.broadcasted_iota(jnp.int32, (8, 128), 0)
    for b in range(SLOTS):
        base = jnp.maximum(list_ref[0, b], 0) * GSIZE
        base_right = jnp.maximum(list_ref[1, b], 0) * GSIZE
        for i in range(0, GSIZE, 8):
            ids = [order_ref[base + i + u] for u in range(8)]
            ids_right = [order_ref[base_right + i + u] for u in range(8)]
            for source, g_ref in ((main_ref, gm_ref), (tail_ref, gt_ref)):
                rows = [source[pl.ds(station, 8, stride=0), :] for station in ids]
                for parity in range(2):
                    at = b * 2 * GSIZE + parity * GSIZE + i
                    low = jnp.where(sub < 2, rows[parity], rows[2 + parity])
                    high = jnp.where(sub < 6, rows[4 + parity], rows[6 + parity])
                    g_ref[at : at + 8, :] = jnp.where(sub < 4, low, high)
                rows = [source[pl.ds(station, 8, stride=0), :] for station in ids_right]
                pairs = [jnp.where(sub % 2 == 0, rows[u], rows[u + 1]) for u in range(0, 8, 2)]
                low = jnp.where(sub < 2, pairs[0], pairs[1])
                high = jnp.where(sub < 6, pairs[2], pairs[3])
                at = rights + b * GSIZE + i
                g_ref[at : at + 8, :] = jnp.where(sub < 4, low, high)

    k = lax.broadcasted_iota(jnp.int32, (128, 128), 0)
    n = lax.broadcasted_iota(jnp.int32, (128, 128), 1)
    turn = jnp.where(k == (n ^ SUBWIN), jnp.where((n & SUBWIN) == 0, -1.0, 1.0), 0.0).astype(bf16)
    imag_row = (lax.broadcasted_iota(jnp.int32, (rights, 128), 0) & 1) == 1
    lefts = []
    for g_ref in (gm_ref, gt_ref):
        plain = g_ref[:rights]
        turned = jnp.dot(plain.astype(bf16), turn, preferred_element_type=f32)
        lefts.append(jnp.where(imag_row, turned, plain).astype(bf16))
    bin_of = (lax.broadcasted_iota(jnp.int32, (GSIZE, 256), 1) & 127) // (2 * SUBWIN)
    keeps = [jnp.where(bin_of == e, 1.0, 0.0).astype(bf16) for e in range(4)]
    zero = jnp.zeros((GSIZE, 128), bf16)
    copies = []
    for b in range(SLOTS):
        scale = jnp.where(list_ref[0, b] >= 0, 1.0 / SUBWIN, 0.0)
        for a, g_ref, bin0, count in ((lefts[0], gm_ref, 0, 4), (lefts[1], gt_ref, 4, 2)):
            at = b * 2 * GSIZE
            lhs = jnp.concatenate(
                [a[at : at + GSIZE], a[at + GSIZE : at + 2 * GSIZE]], axis=1
            )
            lhs = jnp.concatenate([lhs * keep for keep in keeps[:count]], axis=0)
            r = g_ref[rights + b * GSIZE : rights + (b + 1) * GSIZE].astype(bf16)
            rhs = jnp.concatenate(
                [jnp.concatenate([r, zero], axis=1), jnp.concatenate([zero, r], axis=1)], axis=0
            )
            c = lax.dot_general(lhs, rhs, NT, preferred_element_type=f32) * scale
            for e in range(count):
                out_ref[b, bin0 + e] = c[e * GSIZE : (e + 1) * GSIZE].astype(bf16)
        copies.append(pltpu.make_async_copy(out_ref.at[b], out_hbm.at[b], sems.at[b]))
        copies[-1].start()
    for copy in copies:
        copy.wait()


def vmem():
    return pl.BlockSpec(memory_space=pltpu.VMEM)


PARAMS = pltpu.CompilerParams(vmem_limit_bytes=40 * 1024 * 1024)


def correlate(block_list, station_order, stations):
    return pl.pallas_call(
        correlate_kernel,
        out_shape=jax.ShapeDtypeStruct((SLOTS, LOCAL_BINS, GSIZE, 128), bf16),
        in_specs=[pl.BlockSpec(memory_space=pl.ANY), pl.BlockSpec(memory_space=pl.ANY), vmem()],
        out_specs=pl.BlockSpec(memory_space=pltpu.HBM),
        scratch_shapes=[
            pltpu.VMEM((RECEIVER_TOTAL + 8, 128), f32),
            pltpu.VMEM((RECEIVER_TOTAL + 8, 128), f32),
            pltpu.VMEM((SLOTS * 3 * GSIZE, 128), f32),
            pltpu.VMEM((SLOTS * 3 * GSIZE, 128), f32),
            pltpu.VMEM((SLOTS, LOCAL_BINS, GSIZE, 128), bf16),
            pltpu.SMEM((RECEIVER_TOTAL,), jnp.int32),
            pltpu.SemaphoreType.DMA(()),
            pltpu.SMEM((2, SLOTS), jnp.int32),
            pltpu.SemaphoreType.DMA(()),
            pltpu.SemaphoreType.DMA((SLOTS,)),
        ],
        compiler_params=PARAMS,
        name="correlate",
    )(block_list.T, station_order, stations)


def local(records, station_order, block_list):
    facing, staged = pl.pallas_call(
        stage_kernel,
        out_shape=[
            jax.ShapeDtypeStruct((QUAD * PACKED, 128), bf16),
            jax.ShapeDtypeStruct((QUAD, BODY + PACKED, 128), bf16),
        ],
        in_specs=[vmem()],
        out_specs=[vmem()] * 2,
        compiler_params=PARAMS,
        name="stage",
    )(records)
    pairs = [[i, (i + 1) % N_TIME] for i in range(1, N_TIME, 2)]
    edges = lax.all_gather(facing, "tm", axis_index_groups=pairs)
    extended = pl.pallas_call(
        join_kernel,
        out_shape=jax.ShapeDtypeStruct((QUAD, BODY + PACKED, 128), bf16),
        in_specs=[pl.BlockSpec(memory_space=pl.ANY)] * 2,
        out_specs=pl.BlockSpec(memory_space=pl.ANY),
        scratch_shapes=[pltpu.SemaphoreType.DMA((QUAD,))],
        input_output_aliases={1: 0},
        compiler_params=PARAMS,
        name="join",
    )(edges, staged)
    quads = [[QUAD * g + i for i in range(QUAD)] for g in range(N_TIME // QUAD)]
    windows = lax.all_to_all(extended, "tm", 0, 0, axis_index_groups=quads, tiled=True)
    spectra = pl.pallas_call(
        spectra_kernel,
        out_shape=jax.ShapeDtypeStruct((BINS, 2 * PART), bf16),
        in_specs=[vmem(), vmem()],
        out_specs=vmem(),
        compiler_params=PARAMS,
        name="spectra",
    )(jnp.asarray(quarter_table()), windows)
    by_bin = lax.all_to_all(
        spectra.reshape(N_TIME, LOCAL_BINS // 2, 2, 2 * PART), "tm", 0, 0, tiled=True
    ).reshape(BINS, 2 * PART)
    mine = pl.pallas_call(
        arrange_kernel,
        out_shape=jax.ShapeDtypeStruct((BINS, 128), bf16),
        in_specs=[vmem()] * 2,
        out_specs=vmem(),
        compiler_params=PARAMS,
        name="arrange",
    )(jnp.asarray(bin_rows()), by_bin)
    twos = [[i, i + 1] for i in range(0, N_OWNER, 2)]
    fours = [list(range(i, N_OWNER, 2)) for i in range(2)]
    four = lax.all_gather(mine, "pairs", axis=0, axis_index_groups=fours, tiled=True)
    stations = lax.all_gather(four, "pairs", axis=0, axis_index_groups=twos, tiled=True)
    out = correlate(block_list, station_order, stations)
    out = out.reshape(SLOTS, LOCAL_BINS, GSIZE // 2, 2, 128)
    return jnp.transpose(out, (0, 1, 3, 2, 4)).reshape(SLOTS, LOCAL_BINS, 2, GSIZE * GSIZE)


def solution(mesh):
    placed = (P("pairs", "tm"), P(), P("pairs", None))
    return jax.shard_map(
        local, mesh=mesh, in_specs=placed, out_specs=P("pairs", "tm", None, None), check_vma=False
    )
```
